32 devices in a mesh: dp: 8 (over y, x, core), mp: 4 (over z).
Axes of the slice: x: 2, y: 2, z: 4, core: 2. Of those that a mesh axis runs over, the one named last changes fastest.
Arguments:
- queries: bfloat16 [2048, 2048], P('dp', 'mp'), may hold values from -24 to 24
- context_grad: bfloat16 [2048, 2048], P('dp', 'mp'), may hold values from -6 to 6
- encoder_rows: bfloat16 [7168, 4096], P('dp'), may hold values from -60 to 60
- key_weight: bfloat16 [4096, 2048], P('dp', 'mp'), may hold values from -1 to 1
- value_weight: bfloat16 [4096, 2048], P('dp', 'mp'), may hold values from -0.09375 to 0.09375
- document_lengths: int32 [8, 4], P('dp'), may hold values from 1 to 128, 256 in all within a row
- block_bin: int32 [56], P('dp'), may hold values from 0 to 7, as said below
- block_document: int32 [56], P('dp'), may hold values from 0 to 3
Outputs:
- context: bfloat16 [2048, 2048], P('dp', 'mp')
- query_grad: bfloat16 [2048, 2048], P('dp', 'mp')
- encoder_grad: bfloat16 [7168, 4096], P('dp', 'mp')
- key_weight_grad: bfloat16 [4096, 2048], P('dp', 'mp')
- value_weight_grad: bfloat16 [4096, 2048], P('dp', 'mp')
The draws below stay inside these ranges and needn't reach their ends.
Inputs may be any that keep to these rules, and one draw needn't show every extreme that they name: `block_bin`: each index of dp holds 7 encoder blocks and sends them to 7 different bins; one bin receives a block from every index of dp.
All inputs are finite; a program needn't handle non-finite values.
Results may differ from the reference program's by a relative error of at most 0.03.
The reference program's roundings to bfloat16 on the way count: a program that leaves them out, or rounds other values in their place, can miss the bound.
Values may be sent and summed in bfloat16 or wider, within the bound.
A program may use at most 128 MiB of HBM per device.

```python
import math
import jax
import jax.numpy as jnp
import numpy as np
from jax import lax

D = 4096
HD = 256
H = 8
BLK = 128
NDOC = 4
EBLK = 7
DEC_DEV = 256
ENC_DEV = 896
TOKENS = 2048
ENC_ROWS = 7168
NBLK = 56
N_DP = 8


def draw_queries(key, part):
    values = jnp.clip(jax.random.normal(jax.random.fold_in(key, 11), (TOKENS, H * HD), jnp.float32), -6.0, 6.0)
    return values.astype(jnp.bfloat16)


def draw_encoder_rows(key, part):
    bin_count = ENC_ROWS // ENC_DEV
    slice_width = D // bin_count
    pairing = jax.random.permutation(jax.random.fold_in(key, 21), bin_count)
    owner = jnp.arange(ENC_ROWS, dtype=jnp.int32) // ENC_DEV
    feature_block = jnp.arange(D, dtype=jnp.int32) // slice_width
    boost = jnp.where(pairing[owner][:, None] == feature_block[None, :], 3.0, 1.0)
    values = jax.random.normal(jax.random.fold_in(key, 24), (ENC_ROWS, D), jnp.float32)
    return jnp.clip(values * boost, -60.0, 60.0).astype(jnp.bfloat16)


def draw_key_weight(key, part):
    noise = jax.random.normal(jax.random.fold_in(key, 31), (D, H * HD), jnp.float32) * D ** (-0.5)
    values = noise
    return jnp.clip(values, -1.0, 1.0).astype(jnp.bfloat16)


def draw_block_bin(key, part):
    bin_count = NBLK // EBLK
    heavy = jax.random.randint(jax.random.fold_in(key, 41), (), 0, bin_count)
    leaning = jax.random.randint(jax.random.fold_in(key, 42), (bin_count,), 0, 4)
    jitter = jax.random.randint(jax.random.fold_in(key, 43), (bin_count, bin_count), 0, 1024)
    columns = jnp.arange(bin_count, dtype=jnp.int32)
    ranking = leaning[None, :] * 2 ** 20 + jitter * 64 + columns[None, :]
    ranking = jnp.where(columns[None, :] == heavy, 2 ** 29, ranking).astype(jnp.int32)
    _, chosen = lax.top_k(ranking, EBLK)
    shuffle_keys = jax.random.randint(jax.random.fold_in(key, 44), (bin_count, EBLK), 0, 1024) * 64 + jnp.arange(EBLK, dtype=jnp.int32)[None, :]
    order = jnp.argsort(shuffle_keys, axis=1)
    chosen = jnp.take_along_axis(chosen, order, axis=1)
    return chosen.reshape(-1).astype(jnp.int32)


def with_ends(values, key, least, top_value):
    place = [jax.random.randint(jax.random.fold_in(key, axis), (), 0, length) for axis, length in enumerate(values.shape)]
    widest = values.shape.index(max(values.shape))
    beside = place[:widest] + [(place[widest] + 1) % values.shape[widest]] + place[widest + 1:]
    return values.at[tuple(place)].set(least).at[tuple(beside)].set(top_value)


def block_scale(stream_key, shape, pieces, least, largest):
    level = 1.0
    for position, parts in pieces:
        steps = jax.random.uniform(jax.random.fold_in(jax.random.fold_in(stream_key, 6), position), (parts,), jnp.float32, least / len(pieces), largest / len(pieces))
        level = level * jnp.repeat(jnp.exp(steps), shape[position] // parts).reshape((-1,) + (1,) * (len(shape) - 1 - position))
    return level


def split_up(count, total, most, skew):
    loads = [(1 << 20) // math.isqrt(rank ** skew) + 1 for rank in range(2, count + 1)]
    spare, holding = total - most - (count - 1), [1] * (count - 1)
    while spare > 0:
        candidates = [i for i in range(count - 1) if holding[i] < most]
        pool, remaining = sum([loads[i] for i in candidates]), spare
        for i in candidates:
            extra = min(most - holding[i], max(1, remaining * loads[i] // pool), spare)
            holding[i] = holding[i] + extra
            spare = spare - extra
    return np.array([most] + holding)


def uneven(own_key, number_of, total, limit, skew):
    if number_of == 2:
        one = jax.random.randint(own_key, (), max(1, total - limit), min(limit, total - 1) + 1)
        return jnp.stack([one, total - one])
    lengths = jnp.asarray(split_up(number_of, total, limit, skew), jnp.int32)
    couples = (number_of - 1) // 2
    source_of, taker = lengths[1:1 + 2 * couples:2], lengths[2:2 + 2 * couples:2]
    margin = jnp.minimum(source_of - 1, limit - taker)
    shifted = jax.random.randint(jax.random.fold_in(own_key, 1), (couples,), 0, 1 << 20) % (margin + 1)
    lengths = lengths.at[1:1 + 2 * couples:2].set(source_of - shifted).at[2:2 + 2 * couples:2].set(taker + shifted)
    return lengths[jax.random.permutation(jax.random.fold_in(own_key, 2), number_of)]


def normal_values(key, shape, spread, limit, shards=(), kind=jnp.bfloat16):
    loudness = block_scale(key, shape, shards, -0.22, 0.18) if shards else 1.0
    result = jax.random.normal(key, shape, jnp.float32) * spread * loudness
    return jnp.minimum(jnp.maximum(result, -limit), limit).astype(kind)


def setup_inputs(seed: int = 0) -> dict:
    key_list = jax.random.split(jax.random.key(seed), 9)
    return {
        "queries": draw_queries(jax.random.fold_in(key_list[8], 71), 0),
        "context_grad": normal_values(key_list[1], (TOKENS, H * HD), 1.0, 6.0, ((0, 8), (1, 4))),
        "encoder_rows": draw_encoder_rows(jax.random.fold_in(key_list[8], 71), 0),
        "key_weight": draw_key_weight(jax.random.fold_in(key_list[8], 71), 0),
        "value_weight": normal_values(key_list[4], (D, H * HD), D ** -0.5, 0.09375, ((0, 8), (1, 4))),
        "document_lengths": jax.vmap(lambda own: uneven(own, NDOC, DEC_DEV, DEC_DEV // 2, 2))(jax.random.split(key_list[5], N_DP)).reshape((N_DP, NDOC)).astype(jnp.int32),
        "block_bin": draw_block_bin(jax.random.fold_in(key_list[8], 71), 0),
        "block_document": with_ends(jax.random.randint(key_list[7], (NBLK,), 0, NDOC), jax.random.fold_in(key_list[7], 1), 0, NDOC - 1).astype(jnp.int32),
    }


masked_value = -1e30


def attend_weights(scores, live_mask):
    present = jnp.any(live_mask, axis=1)[None, :, None]
    blocked = jnp.where(live_mask[None], scores, masked_value)
    highest = jnp.max(blocked, axis=2, keepdims=True)
    highest = jnp.where(present, highest, 0.0)
    raised = jnp.exp(jnp.where(live_mask[None], scores - highest, masked_value))
    totals = jnp.maximum(jnp.sum(raised, axis=2, keepdims=True), 1.0)
    return raised / totals


def reference(queries, context_grad, encoder_rows, key_weight, value_weight, document_lengths, block_bin, block_document):
    width = H * HD
    scaling = HD ** -0.5
    both_weights = jnp.concatenate([key_weight, value_weight], axis=1).astype(jnp.float32)
    key_values = jnp.dot(encoder_rows.astype(jnp.float32), both_weights).astype(jnp.bfloat16)
    kv_blocks = key_values.reshape(N_DP, EBLK, BLK, 2 * width)
    bins_of = block_bin.reshape(N_DP, EBLK)
    docs_of = block_document.reshape(N_DP, EBLK)
    sources = jnp.arange(N_DP, dtype=jnp.int32)
    local_slots = jnp.arange(EBLK, dtype=jnp.int32)
    positions = jnp.arange(DEC_DEV, dtype=jnp.int32)

    def bin_step(grad_blocks, bin_index):
        arrives = bins_of == bin_index
        present = jnp.any(arrives, axis=1)
        local_index = jnp.sum(jnp.where(arrives, local_slots[None, :], 0), axis=1).astype(jnp.int32)
        slot_kv = kv_blocks[sources, local_index]
        slot_doc = jnp.where(present, docs_of[sources, local_index], -1)
        doc_ends = jnp.cumsum(document_lengths[bin_index])
        token_doc = jnp.sum((doc_ends[None, :] <= positions[:, None]).astype(jnp.int32), axis=1)
        live_mask = token_doc[:, None] == jnp.repeat(slot_doc, BLK)[None, :]
        key_rows = slot_kv[:, :, :width].reshape(N_DP * BLK, H, HD).astype(jnp.float32)
        value_rows = slot_kv[:, :, width:].reshape(N_DP * BLK, H, HD).astype(jnp.float32)
        row_start = (bin_index * DEC_DEV).astype(jnp.int32)
        query_rows = lax.dynamic_slice_in_dim(queries, row_start, DEC_DEV, 0).reshape(DEC_DEV, H, HD).astype(jnp.float32)
        grad_rows = lax.dynamic_slice_in_dim(context_grad, row_start, DEC_DEV, 0).reshape(DEC_DEV, H, HD).astype(jnp.float32)
        scores = jnp.einsum("thd,shd->hts", query_rows, key_rows) * scaling
        attention = attend_weights(scores, live_mask)
        rounded = lax.optimization_barrier(attention.astype(jnp.bfloat16)).astype(jnp.float32)
        context = jnp.einsum("hts,shd->thd", rounded, value_rows).astype(jnp.bfloat16)
        grad_raw = jnp.einsum("thd,shd->hts", grad_rows, value_rows)
        deltas = jnp.sum(attention * grad_raw, axis=2, keepdims=True)
        score_grad = lax.optimization_barrier((attention * (grad_raw - deltas) * scaling).astype(jnp.bfloat16)).astype(jnp.float32)
        query_grad = jnp.einsum("hts,shd->thd", score_grad, key_rows).astype(jnp.bfloat16)
        key_grad = jnp.einsum("hts,thd->shd", score_grad, query_rows).astype(jnp.bfloat16)
        value_grad = jnp.einsum("hts,thd->shd", rounded, grad_rows).astype(jnp.bfloat16)
        slot_grads = jnp.concatenate([key_grad.reshape(N_DP, BLK, width), value_grad.reshape(N_DP, BLK, width)], axis=2)
        grad_blocks = jnp.where(arrives[:, :, None, None], slot_grads[:, None], grad_blocks)
        return grad_blocks, (context.reshape(DEC_DEV, width), query_grad.reshape(DEC_DEV, width))

    start_blocks = jnp.zeros((N_DP, EBLK, BLK, 2 * width), jnp.bfloat16)
    grad_blocks, (context_all, query_all) = lax.scan(bin_step, start_blocks, jnp.arange(N_DP, dtype=jnp.int32))
    context = context_all.reshape(TOKENS, width)
    query_grad = query_all.reshape(TOKENS, width)
    kv_grad = grad_blocks.reshape(N_DP, ENC_DEV, 2 * width)
    encoder_split = encoder_rows.reshape(N_DP, ENC_DEV, D)

    def add_source(weight_sum, source):
        partial_value = jnp.dot(encoder_split[source].astype(jnp.float32).T, kv_grad[source].astype(jnp.float32))
        partial_value = lax.optimization_barrier(partial_value.astype(jnp.bfloat16)).astype(jnp.float32)
        return weight_sum + partial_value, None

    weight_sum, _ = lax.scan(add_source, jnp.zeros((D, 2 * width), jnp.float32), jnp.arange(N_DP, dtype=jnp.int32))
    key_weight_grad = weight_sum[:, :width].astype(jnp.bfloat16)
    value_weight_grad = weight_sum[:, width:].astype(jnp.bfloat16)
    encoder_grad = jnp.dot(kv_grad.reshape(ENC_ROWS, 2 * width).astype(jnp.float32), both_weights.T).astype(jnp.bfloat16)
    return (context, query_grad, encoder_grad, key_weight_grad, value_weight_grad)
```

```python
import functools

import jax
import jax.numpy as jnp
from jax import lax
from jax.experimental import pallas as pl
from jax.experimental.pallas import tpu as pltpu
from jax.sharding import PartitionSpec as P

HD = 256
BLK = 128


masked_value = -1e30


def attend_weights(scores, live_mask):
    present = jnp.any(live_mask, axis=1)[None, :, None]
    blocked = jnp.where(live_mask[None], scores, masked_value)
    highest = jnp.max(blocked, axis=2, keepdims=True)
    highest = jnp.where(present, highest, 0.0)
    raised = jnp.exp(jnp.where(live_mask[None], scores - highest, masked_value))
    totals = jnp.maximum(jnp.sum(raised, axis=2, keepdims=True), 1.0)
    return raised / totals


def token_documents(lengths, token_count):
    doc_ends = jnp.cumsum(lengths)
    positions = jnp.arange(token_count, dtype=jnp.int32)
    return jnp.sum((doc_ends[None, :] <= positions[:, None]).astype(jnp.int32), axis=1)


def per_device(
    queries,
    context_grad,
    encoder_rows,
    key_weight,
    value_weight,
    document_lengths,
    block_bin,
    block_document,
):
    bin_count = lax.axis_size("dp")
    full_key, full_value = (
        lax.all_gather(key_weight, "dp", axis=0, tiled=True),
        lax.all_gather(value_weight, "dp", axis=0, tiled=True),
    )
    head_width = full_key.shape[1]
    head_count = head_width // HD
    block_rows = BLK
    blocks_here = block_bin.shape[0]
    both_weights = jnp.concatenate([full_key, full_value], axis=1)
    projected = jnp.dot(encoder_rows, both_weights, preferred_element_type=jnp.float32).astype(
        jnp.bfloat16
    )
    route_table = (block_bin[:, None] == jnp.arange(bin_count, dtype=jnp.int32)[None, :]).astype(
        jnp.bfloat16
    )
    flat_blocks = projected.reshape(blocks_here, block_rows * 2 * head_width)
    outbound = lax.dot_general(
        route_table, flat_blocks, (((0,), (0,)), ((), ())), preferred_element_type=jnp.float32
    )
    outbound = outbound.astype(jnp.bfloat16).reshape(bin_count, block_rows, 2 * head_width)
    slot_docs = (
        lax.dot_general(
            route_table.astype(jnp.float32),
            (block_document + 1).astype(jnp.float32),
            (((0,), (0,)), ((), ())),
        )
        - 1.0
    )
    tag_rows = jnp.broadcast_to(slot_docs[:, None], (bin_count, block_rows)).astype(jnp.bfloat16)
    arrived, arrived_tags = (
        lax.all_to_all(outbound, "dp", split_axis=0, concat_axis=0, tiled=True),
        lax.all_to_all(tag_rows, "dp", split_axis=0, concat_axis=0, tiled=True),
    )
    key_slots = arrived[:, :, :head_width].reshape(bin_count * block_rows, head_count, HD)
    value_slots = arrived[:, :, head_width:].reshape(bin_count * block_rows, head_count, HD)
    token_count = queries.shape[0]
    token_docs = token_documents(document_lengths[0], token_count).astype(jnp.float32)
    live_mask = arrived_tags.reshape(-1).astype(jnp.float32)[None, :] == token_docs[:, None]
    query_heads = queries.reshape(token_count, head_count, HD)
    grad_heads = context_grad.reshape(token_count, head_count, HD)
    scaling = HD ** (-0.5)
    scores = (
        jnp.einsum("thd,shd->hts", query_heads, key_slots, preferred_element_type=jnp.float32)
        * scaling
    )
    attention = attend_weights(scores, live_mask)
    rounded = attention.astype(jnp.bfloat16)
    context = jnp.einsum(
        "hts,shd->thd", rounded, value_slots, preferred_element_type=jnp.float32
    ).astype(jnp.bfloat16)
    grad_raw = jnp.einsum(
        "thd,shd->hts", grad_heads, value_slots, preferred_element_type=jnp.float32
    )
    deltas = jnp.sum(attention * grad_raw, axis=2, keepdims=True)
    score_grad = (attention * (grad_raw - deltas) * scaling).astype(jnp.bfloat16)
    query_grad = jnp.einsum(
        "hts,shd->thd", score_grad, key_slots, preferred_element_type=jnp.float32
    ).astype(jnp.bfloat16)
    key_grad = jnp.einsum(
        "hts,thd->shd", score_grad, query_heads, preferred_element_type=jnp.float32
    ).astype(jnp.bfloat16)
    value_grad = jnp.einsum(
        "hts,thd->shd", rounded, grad_heads, preferred_element_type=jnp.float32
    ).astype(jnp.bfloat16)
    slot_grads = jnp.concatenate(
        [
            key_grad.reshape(bin_count, block_rows, head_width),
            value_grad.reshape(bin_count, block_rows, head_width),
        ],
        axis=2,
    )
    returned = lax.all_to_all(slot_grads, "dp", split_axis=0, concat_axis=0, tiled=True)
    own_grads = jnp.dot(
        route_table,
        returned.reshape(bin_count, block_rows * 2 * head_width),
        preferred_element_type=jnp.float32,
    )
    own_grads = own_grads.astype(jnp.bfloat16).reshape(encoder_rows.shape[0], 2 * head_width)
    weight_terms = lax.dot_general(
        encoder_rows, own_grads, (((0,), (0,)), ((), ())), preferred_element_type=jnp.float32
    )
    weight_sums = lax.psum_scatter(
        weight_terms.astype(jnp.bfloat16), "dp", scatter_dimension=0, tiled=True
    ).astype(jnp.float32)
    key_weight_grad = weight_sums[:, :head_width].astype(jnp.bfloat16)
    value_weight_grad = weight_sums[:, head_width:].astype(jnp.bfloat16)
    row_terms = lax.dot_general(
        own_grads, both_weights, (((1,), (1,)), ((), ())), preferred_element_type=jnp.float32
    )
    encoder_grad = lax.psum_scatter(
        row_terms.astype(jnp.bfloat16), "mp", scatter_dimension=1, tiled=True
    )
    return (
        context.reshape(token_count, head_width),
        query_grad.reshape(token_count, head_width),
        encoder_grad,
        key_weight_grad,
        value_weight_grad,
    )


MESH = pl.DeviceIdType.MESH


def contract(a, b, dim_a, dim_b):
    return lax.dot_general(
        a, b, (((dim_a,), (dim_b,)), ((), ())), preferred_element_type=jnp.float32
    )


def step_kernel(
    n,
    count,
    q_ref,
    g_ref,
    enc_hbm,
    kw_ref,
    vw_ref,
    lengths_ref,
    bins_ref,
    docs_ref,
    held_ref,
    ctx_ref,
    qg_ref,
    eg_ref,
    kwg_ref,
    vwg_ref,
    enc,
    wts,
    wend,
    acc,
    arrived,
    tags,
    arrived_tags,
    grads,
    ret,
    own,
    gend,
    msend,
    mrecv,
    tsend,
    trecv,
    hops,
    passed,
    local_sem,
    gather_send,
    gather_recv,
    lift_send,
    lift_recv,
    core_send,
    core_recv,
    tag_send,
    tag_recv,
    out_send,
    out_recv,
    back_send,
    back_recv,
    g_send,
    g_recv,
    mid_send,
    mid_recv,
    end_send,
    end_recv,
    pair_send,
    pair_recv,
    hop_send,
    hop_recv,
):
    bf16 = jnp.bfloat16
    me, z = lax.axis_index("dp"), lax.axis_index("mp")
    core = me % 2
    x = (me // 2) % 2
    y = me // 4

    def place(py, px, pc):
        return (py * 2 + px) * 2 + pc

    at_x, at_y = place(y, 1 - x, core), place(1 - y, x, core)
    at_c, at_d = place(y, x, 1 - core), place(1 - y, 1 - x, core)
    c_x, c_y = place(y, 1 - x, 1 - core), place(1 - y, x, 1 - core)
    c_d = place(1 - y, 1 - x, 1 - core)
    depth, width = kw_ref.shape
    rows = enc.shape[0]
    blocks = rows // BLK
    blk = BLK
    heads = width // HD
    last = count - 1
    end = (z // 2) * last
    far_end = last - end
    is_end = z == end
    is_inner = z != end
    mate = z + 1 - 2 * (z % 2)
    across = last - z

    def remote(src, dst, send, recv, **device):
        return pltpu.make_async_remote_copy(
            src_ref=src,
            dst_ref=dst,
            send_sem=send,
            recv_sem=recv,
            device_id=device,
            device_id_type=MESH,
        )

    load_enc = pltpu.make_async_copy(enc_hbm, enc, local_sem.at[0])
    load_enc.start()
    barrier = pltpu.get_barrier_semaphore()
    for d in range(1, n):
        pl.semaphore_signal(
            barrier, inc=1, device_id={"dp": (me + d) % n}, device_id_type=MESH
        )
    for d in range(1, count):
        pl.semaphore_signal(
            barrier, inc=1, device_id={"mp": (z + d) % count}, device_id_type=MESH
        )

    for d in range(n):
        to = (me + d) % n
        doc = jnp.int32(-1)
        for b in range(blocks):
            doc = jnp.where(bins_ref[b] == to, docs_ref[b], doc)
        tags[to] = jnp.full(tags.shape[1:], doc.astype(jnp.float32), jnp.float32)
    pl.semaphore_wait(barrier, n - 1 + count - 1)

    def part_cols(part):
        return pl.ds(part * width, width)

    def land(src, part):
        return wts.at[src, :, part_cols(part)]

    started = []

    def ship(ident, ref, src, part, to):
        copy = remote(
            ref, land(src, part), gather_send.at[ident], gather_recv.at[ident], dp=to
        )
        copy.start()
        started.append(copy)

    def landed(ident, src, part):
        remote(
            land(src, part), land(src, part), gather_send.at[ident], gather_recv.at[ident], dp=at_c
        ).wait_recv()

    def lifted(src, part):
        slot = (src // 2 - 1 + end // last) * 2 + src % 2
        return wend.at[slot, :, part_cols(part)]

    ours, theirs = (me, at_x, at_y, at_d), (at_c, c_x, c_y, c_d)
    pieces = [(0, 0), (0, 1), (1, 0), (2, 1), (1, 1), (2, 0), (3, 0), (3, 1)]

    def lift(i, part, ref=None):
        src = ours[i]
        ident = 2 * i + part

        @pl.when(jnp.logical_and(is_end, src // 2 != end))
        def _():
            remote(
                land(src, part) if ref is None else ref,
                lifted(src, part),
                lift_send.at[ident],
                lift_recv.at[ident],
                mp=mate,
            ).start()

    def each_piece(todo, listed, of_end):
        for i, part in listed:
            for src, mirror in ((ours[i], theirs[i]),):

                @pl.when(jnp.logical_and(is_end if of_end else is_inner, src // 2 != end))
                def _():
                    todo(i, part, src, mirror)

    def lift_copy(i, part, src):
        ident = 2 * i + part
        return remote(
            lifted(src, part), lifted(src, part), lift_send.at[ident], lift_recv.at[ident], mp=mate
        )

    def core_copy(i, part, src):
        ident = 2 * i + part
        return remote(
            lifted(src, part), lifted(src, part), core_send.at[ident], core_recv.at[ident], dp=at_c
        )

    def hand_over(i, part, src, mirror):
        lift_copy(i, part, src).wait_recv()
        core_copy(i, part, src).start()

    ship(0, kw_ref, me, 0, at_x)
    ship(3, vw_ref, me, 1, at_y)
    ship(1, vw_ref, me, 1, at_x)
    ship(2, kw_ref, me, 0, at_y)
    ship(6, kw_ref, me, 0, at_c)
    ship(7, vw_ref, me, 1, at_c)
    lift(0, 0, kw_ref)
    lift(0, 1, vw_ref)
    own_k = pltpu.make_async_copy(kw_ref, land(me, 0), local_sem.at[1])
    own_v = pltpu.make_async_copy(vw_ref, land(me, 1), local_sem.at[2])
    own_k.start()
    own_v.start()
    tag_copies = []
    for d in range(1, n):
        to = (me + d) % n
        copy = remote(
            tags.at[to], arrived_tags.at[me], tag_send.at[d], tag_recv.at[d], dp=to
        )
        copy.start()
        tag_copies.append(copy)
    arrived_tags[me] = tags[me]
    own_k.wait()
    own_v.wait()
    load_enc.wait()

    def multiply(src, part, first=False):
        columns = pl.ds(pl.multiple_of(src * depth, depth), depth)

        @pl.loop(0, width // HD)
        def _(t):
            cols = pl.ds(pl.multiple_of(part * width + t * HD, HD), HD)
            product = jnp.dot(
                enc[:, columns], wts[src, :, cols], preferred_element_type=jnp.float32
            ).reshape(blocks, blk, HD)
            if first:
                acc[:, :, cols] = product
            else:
                acc[:, :, cols] += product

    multiply(me, 0, True)
    multiply(me, 1, True)
    landed(6, at_c, 0)
    multiply(at_c, 0)
    landed(7, at_c, 1)
    multiply(at_c, 1)
    landed(0, at_x, 0)
    ship(4, land(at_x, 0), at_x, 0, at_y)
    ship(8, land(at_x, 0), at_x, 0, at_c)
    lift(1, 0)
    landed(3, at_y, 1)
    ship(5, land(at_y, 1), at_y, 1, at_x)
    ship(11, land(at_y, 1), at_y, 1, at_c)
    lift(2, 1)
    multiply(at_x, 0)
    multiply(at_y, 1)
    landed(8, c_x, 0)
    multiply(c_x, 0)
    landed(11, c_y, 1)
    multiply(c_y, 1)
    landed(1, at_x, 1)
    ship(9, land(at_x, 1), at_x, 1, at_c)
    lift(1, 1)
    landed(2, at_y, 0)
    ship(10, land(at_y, 0), at_y, 0, at_c)
    lift(2, 0)
    multiply(at_x, 1)
    multiply(at_y, 0)
    landed(9, c_x, 1)
    multiply(c_x, 1)
    landed(10, c_y, 0)
    multiply(c_y, 0)
    landed(4, at_d, 0)
    ship(12, land(at_d, 0), at_d, 0, at_c)
    lift(3, 0)
    landed(5, at_d, 1)
    ship(13, land(at_d, 1), at_d, 1, at_c)
    lift(3, 1)
    multiply(at_d, 0)
    multiply(at_d, 1)
    landed(12, c_d, 0)
    multiply(c_d, 0)
    landed(13, c_d, 1)
    multiply(c_d, 1)

    out_copies = []
    mine = pl.ds(pl.multiple_of(me * blk, blk), blk)
    for d in [*range(1, n), 0]:
        to = (me + d) % n
        msend[d // blocks, d % blocks] = acc[held_ref[to]].astype(bf16)

        if d == 0:
            arrived[mine, :] = msend[0, 0]
            continue
        copy = remote(
            msend.at[d // blocks, d % blocks], arrived.at[mine, :], out_send.at[d], out_recv.at[d], dp=to
        )
        copy.start()
        out_copies.append(copy)

    each_piece(hand_over, pieces[:4], False)
    position = lax.broadcasted_iota(jnp.int32, (q_ref.shape[0], 1), 0)
    token_doc = jnp.zeros(position.shape, jnp.float32)
    doc_end = jnp.int32(0)
    for k in range(lengths_ref.shape[1]):
        doc_end = doc_end + lengths_ref[0, k]
        token_doc = token_doc + jnp.where(position >= doc_end, 1.0, 0.0)
    for copy in tag_copies:
        copy.wait()
    for copy in out_copies:
        copy.wait()
    tag_row = jnp.concatenate([arrived_tags[s, 0:1, :] for s in range(n)], axis=1)
    live = tag_row == token_doc
    present = jnp.max(jnp.where(live, 1.0, 0.0), axis=1, keepdims=True) > 0.0
    scaling = HD ** (-0.5)
    back_copies = []
    for h in range(heads):
        hk, hv = pl.ds(h * HD, HD), pl.ds(width + h * HD, HD)
        q, g = q_ref[:, hk], g_ref[:, hk]
        scores = contract(q, arrived[:, hk], 1, 1) * scaling
        highest = jnp.max(jnp.where(live, scores, masked_value), axis=1, keepdims=True)
        highest = jnp.where(present, highest, 0.0)
        raised = jnp.exp(jnp.where(live, scores - highest, masked_value))
        totals = jnp.maximum(jnp.sum(raised, axis=1, keepdims=True), 1.0)
        attention = raised / totals
        rounded = attention.astype(bf16)
        grad_raw = contract(g, arrived[:, hv], 1, 1)
        deltas = jnp.sum(attention * grad_raw, axis=1, keepdims=True)
        score_grad = (attention * (grad_raw - deltas) * scaling).astype(bf16)
        grads[:, h, 0] = contract(score_grad, q, 0, 0).astype(bf16).reshape(n, blk, HD)
        grads[:, h, 1] = contract(rounded, g, 0, 0).astype(bf16).reshape(n, blk, HD)
        for d in range(1, n):
            to = (me + d) % n
            copy = remote(
                grads.at[to, h],
                ret.at[me, h],
                back_send.at[h, d],
                back_recv.at[h, d],
                dp=to,
            )
            copy.start()
            back_copies.append(copy)
        ret[me, h] = grads[me, h]
        ctx_ref[:, hk] = jnp.dot(
            rounded, arrived[:, hv], preferred_element_type=jnp.float32
        ).astype(bf16)
        qg_ref[:, hk] = jnp.dot(
            score_grad, arrived[:, hk], preferred_element_type=jnp.float32
        ).astype(bf16)
    each_piece(hand_over, pieces[4:], False)
    for copy in back_copies:
        copy.wait()

    def block(r):
        return pl.ds(r * blk if isinstance(r, int) else pl.multiple_of(r * blk, blk), blk)

    def g_copy(r):
        return remote(own.at[block(r), :], gend.at[r], g_send.at[r], g_recv.at[r], mp=mate)

    def mid_copy(way, r):
        return remote(
            msend.at[way, r], mrecv.at[way, r], mid_send.at[way, r], mid_recv.at[way, r], mp=across
        )

    def end_copy(r):
        return remote(arrived.at[block(r), :], gend.at[r], end_send.at[r], end_recv.at[r], mp=mate)

    def pair_copy(i):
        return remote(tsend.at[i], trecv.at[i], pair_send.at[i], pair_recv.at[i], dp=at_c)

    def hop_copy(way, i, src):
        to = at_x if (way == 0) == (i < 2) else at_y
        return remote(src, hops.at[way, i], hop_send.at[way, i], hop_recv.at[way, i], dp=to)

    for r in range(blocks):
        for h in range(heads):
            own[block(r), pl.ds(h * HD, HD)] = ret[bins_ref[r], h, 0]
            own[block(r), pl.ds(width + h * HD, HD)] = ret[bins_ref[r], h, 1]

        @pl.when(is_end)
        def _():
            g_copy(r).start()

    for i, part in pieces:
        mirror = theirs[i]

        @pl.when(jnp.logical_and(is_inner, mirror // 2 != end))
        def _():
            core_copy(i, part, mirror).wait_recv()

    def own_weights(d, j):
        return wts[2 * d + j]

    def end_weights(d, j):
        return wend[(d - 1 + end // last) * 2 + j]

    def shard_of(i, parity):
        flip_x, flip_y = 1 - i // 2, 1 - i % 2
        px = x + flip_x - 2 * x * flip_x
        py = y + flip_y - 2 * y * flip_y
        return place(py, px, parity)

    def term(shard, cols):
        columns = pl.ds(pl.multiple_of(shard * depth, depth), depth)
        return contract(enc[:, columns], own[:, cols], 0, 0).astype(bf16)

    def half_cols(j):
        return pl.ds(pl.multiple_of(j * width, width), width)

    @pl.loop(0, blocks)
    def _(r):
        @pl.when(r < 2)
        def _():
            @pl.loop(0, 2)
            def _(k):
                i = 2 * r + k
                shard = shard_of(i, 1 - core)

                @pl.loop(0, 2)
                def _(j):
                    tsend[i, :, half_cols(j)] = term(shard, half_cols(j))

                pair_copy(i).start()

        @pl.when(is_inner)
        def _():
            g_copy(r).wait_recv()
            for way, dest in ((0, far_end), (1, across)):

                @pl.loop(0, 2)
                def _(j):
                    summed = contract(own[block(r), :], own_weights(dest, j), 1, 1)
                    summed += contract(gend[r], end_weights(dest, j), 1, 1)
                    msend[way, r, :, half_cols(j)] = summed.astype(bf16)

                mid_copy(way, r).start()

        @pl.when(jnp.logical_and(r >= 2, r < 4))
        def _():
            @pl.loop(0, 2)
            def _(k):
                i = 2 * (r - 2) + k
                shard = shard_of(i, core)
                pair_copy(i).wait_recv()

                @pl.loop(0, 2)
                def _(j):
                    cols = half_cols(j)
                    summed = term(shard, cols).astype(jnp.float32)
                    summed += trecv[i, :, cols].astype(jnp.float32)
                    trecv[i, :, cols] = summed.astype(bf16)

        @pl.when(r == 2)
        def _():
            hop_copy(0, 1, trecv.at[0, :, part_cols(0)]).start()
            hop_copy(0, 0, trecv.at[1, :, part_cols(0)]).start()
            hop_copy(1, 1, trecv.at[0, :, part_cols(1)]).start()

        @pl.when(r == 3)
        def _():
            hop_copy(1, 0, trecv.at[2, :, part_cols(1)]).start()

    for way in range(2):
        hop_copy(way, 1, hops.at[way, 1]).wait_recv()
        summed = trecv[2 - way, :, part_cols(way)].astype(jnp.float32)
        summed += hops[way, 1].astype(jnp.float32)
        passed[way] = summed.astype(bf16)
        hop_copy(way, 2, passed.at[way]).start()

    total = acc.at[0]

    @pl.loop(0, blocks)
    def _(r):
        @pl.when(is_inner)
        def _():
            @pl.loop(0, 2)
            def _(j):
                total[:, half_cols(j)] = contract(own[block(r), :], own_weights(end, j), 1, 1)

            mid_copy(0, r).wait_recv()
            arrived[block(r), :] = (total[...] + mrecv[0, r].astype(jnp.float32)).astype(bf16)
            end_copy(r).start()

            @pl.loop(0, 2)
            def _(j):
                summed = contract(own[block(r), :], own_weights(z, j), 1, 1)
                summed += contract(gend[r], end_weights(z, j), 1, 1)
                total[:, half_cols(j)] = summed

            mid_copy(1, r).wait_recv()
            eg_ref[block(r), :] = (total[...] + mrecv[1, r].astype(jnp.float32)).astype(bf16)

        @pl.when(is_end)
        def _():
            @pl.loop(0, 2)
            def _(j):
                total[:, half_cols(j)] = contract(own[block(r), :], own_weights(z, j), 1, 1)

            end_copy(r).wait_recv()
            eg_ref[block(r), :] = (total[...] + gend[r].astype(jnp.float32)).astype(bf16)

        @pl.when(r == blocks - 2)
        def _():
            for way, out in ((0, kwg_ref), (1, vwg_ref)):
                hop_copy(way, 0, hops.at[way, 0]).wait_recv()
                hop_copy(way, 2, hops.at[way, 2]).wait_recv()
                summed = trecv[3, :, part_cols(way)].astype(jnp.float32)
                summed += hops[way, 0].astype(jnp.float32) + hops[way, 2].astype(jnp.float32)
                out[...] = summed.astype(bf16)

    for copy in started:
        copy.wait_send()
    each_piece(lambda i, part, src, mirror: lift_copy(i, part, src).wait_send(), pieces, True)
    each_piece(lambda i, part, src, mirror: core_copy(i, part, src).wait_send(), pieces, False)

    @pl.loop(0, blocks)
    def _(r):
        @pl.when(is_end)
        def _():
            g_copy(r).wait_send()

        @pl.when(is_inner)
        def _():
            mid_copy(0, r).wait_send()
            mid_copy(1, r).wait_send()
            end_copy(r).wait_send()

    for i in range(4):
        pair_copy(i).wait_send()
    for way in range(2):
        for i in range(3):
            hop_copy(way, i, hops.at[way, i]).wait_send()


def per_device_cube(
    queries,
    context_grad,
    encoder_rows,
    key_weight,
    value_weight,
    document_lengths,
    block_bin,
    block_document,
):
    n, count = lax.axis_size("dp"), lax.axis_size("mp")
    rows, model = encoder_rows.shape
    depth, width = key_weight.shape
    heads = width // HD
    tokens = queries.shape[0]
    blocks = rows // BLK
    chips = n // 2
    hits = block_bin[:, None] == jnp.arange(n, dtype=jnp.int32)[None, :]
    held = jnp.sum(jnp.where(hits, jnp.arange(blocks, dtype=jnp.int32)[:, None], 0), axis=0)
    vmem = pl.BlockSpec(memory_space=pltpu.VMEM)
    smem = pl.BlockSpec(memory_space=pltpu.SMEM)
    hbm = pl.BlockSpec(memory_space=pl.ANY)
    bf16 = jnp.bfloat16
    dma = pltpu.SemaphoreType.DMA
    shape = jax.ShapeDtypeStruct
    pairs = []
    for extent in [(14,), (8,), (8,), (n,), (n,), (heads, n), (blocks,), (2, blocks), (blocks,), (chips,), (2, 3)]:
        pairs += [dma(extent), dma(extent)]
    return pl.pallas_call(
        functools.partial(step_kernel, n, count),
        out_shape=(
            shape((tokens, width), bf16),
            shape((tokens, width), bf16),
            shape((rows, model // count), bf16),
            shape((depth, width), bf16),
            shape((depth, width), bf16),
        ),
        in_specs=[vmem, vmem, hbm, vmem, vmem, smem, smem, smem, smem],
        out_specs=(vmem,) * 5,
        scratch_shapes=[
            pltpu.VMEM((rows, model), bf16),
            pltpu.VMEM((n, depth, 2 * width), bf16),
            pltpu.VMEM((n - 2, depth, 2 * width), bf16),
            pltpu.VMEM((blocks, BLK, 2 * width), jnp.float32),
            pltpu.VMEM((n * BLK, 2 * width), bf16),
            pltpu.VMEM((n, 8, BLK), jnp.float32),
            pltpu.VMEM((n, 8, BLK), jnp.float32),
            pltpu.VMEM((n, heads, 2, BLK, HD), bf16),
            pltpu.VMEM((n, heads, 2, BLK, HD), bf16),
            pltpu.VMEM((rows, 2 * width), bf16),
            pltpu.VMEM((blocks, BLK, 2 * width), bf16),
            pltpu.VMEM((2, blocks, BLK, 2 * width), bf16),
            pltpu.VMEM((2, blocks, BLK, 2 * width), bf16),
            pltpu.VMEM((chips, depth, 2 * width), bf16),
            pltpu.VMEM((chips, depth, 2 * width), bf16),
            pltpu.VMEM((2, 3, depth, width), bf16),
            pltpu.VMEM((2, depth, width), bf16),
            dma((3,)),
            *pairs,
        ],
        compiler_params=pltpu.CompilerParams(
            collective_id=0, has_side_effects=True, vmem_limit_bytes=67043328
        ),
    )(
        queries,
        context_grad,
        encoder_rows,
        key_weight,
        value_weight,
        document_lengths,
        block_bin,
        block_document,
        held,
    )


def solution(mesh):
    in_specs = (
        P("dp", "mp"),
        P("dp", "mp"),
        P("dp", None),
        P("dp", "mp"),
        P("dp", "mp"),
        P("dp", None),
        P("dp"),
        P("dp"),
    )
    out_specs = (P("dp", "mp"), P("dp", "mp"), P("dp", "mp"), P("dp", "mp"), P("dp", "mp"))
    cube = mesh.shape["dp"] == 2 * 2 * 2 and mesh.shape["mp"] == 2 * 2
    return jax.shard_map(
        per_device_cube if cube else per_device, mesh=mesh, in_specs=in_specs, out_specs=out_specs, check_vma=False
    )
```

```python
import functools

import jax
import jax.numpy as jnp
from jax import lax
from jax.experimental import pallas as pl
from jax.experimental.pallas import tpu as pltpu
from jax.sharding import PartitionSpec as P

HD = 256
BLK = 128


masked_value = -1e30


def attend_weights(scores, live_mask):
    present = jnp.any(live_mask, axis=1)[None, :, None]
    blocked = jnp.where(live_mask[None], scores, masked_value)
    highest = jnp.max(blocked, axis=2, keepdims=True)
    highest = jnp.where(present, highest, 0.0)
    raised = jnp.exp(jnp.where(live_mask[None], scores - highest, masked_value))
    totals = jnp.maximum(jnp.sum(raised, axis=2, keepdims=True), 1.0)
    return raised / totals


def token_documents(lengths, token_count):
    doc_ends = jnp.cumsum(lengths)
    positions = jnp.arange(token_count, dtype=jnp.int32)
    return jnp.sum((doc_ends[None, :] <= positions[:, None]).astype(jnp.int32), axis=1)


def per_device(
    queries,
    context_grad,
    encoder_rows,
    key_weight,
    value_weight,
    document_lengths,
    block_bin,
    block_document,
):
    bin_count = lax.axis_size("dp")
    full_key, full_value = (
        lax.all_gather(key_weight, "dp", axis=0, tiled=True),
        lax.all_gather(value_weight, "dp", axis=0, tiled=True),
    )
    head_width = full_key.shape[1]
    head_count = head_width // HD
    block_rows = BLK
    blocks_here = block_bin.shape[0]
    both_weights = jnp.concatenate([full_key, full_value], axis=1)
    projected = jnp.dot(encoder_rows, both_weights, preferred_element_type=jnp.float32).astype(
        jnp.bfloat16
    )
    route_table = (block_bin[:, None] == jnp.arange(bin_count, dtype=jnp.int32)[None, :]).astype(
        jnp.bfloat16
    )
    flat_blocks = projected.reshape(blocks_here, block_rows * 2 * head_width)
    outbound = lax.dot_general(
        route_table, flat_blocks, (((0,), (0,)), ((), ())), preferred_element_type=jnp.float32
    )
    outbound = outbound.astype(jnp.bfloat16).reshape(bin_count, block_rows, 2 * head_width)
    slot_docs = (
        lax.dot_general(
            route_table.astype(jnp.float32),
            (block_document + 1).astype(jnp.float32),
            (((0,), (0,)), ((), ())),
        )
        - 1.0
    )
    tag_rows = jnp.broadcast_to(slot_docs[:, None], (bin_count, block_rows)).astype(jnp.bfloat16)
    arrived, arrived_tags = (
        lax.all_to_all(outbound, "dp", split_axis=0, concat_axis=0, tiled=True),
        lax.all_to_all(tag_rows, "dp", split_axis=0, concat_axis=0, tiled=True),
    )
    key_slots = arrived[:, :, :head_width].reshape(bin_count * block_rows, head_count, HD)
    value_slots = arrived[:, :, head_width:].reshape(bin_count * block_rows, head_count, HD)
    token_count = queries.shape[0]
    token_docs = token_documents(document_lengths[0], token_count).astype(jnp.float32)
    live_mask = arrived_tags.reshape(-1).astype(jnp.float32)[None, :] == token_docs[:, None]
    query_heads = queries.reshape(token_count, head_count, HD)
    grad_heads = context_grad.reshape(token_count, head_count, HD)
    scaling = HD ** (-0.5)
    scores = (
        jnp.einsum("thd,shd->hts", query_heads, key_slots, preferred_element_type=jnp.float32)
        * scaling
    )
    attention = attend_weights(scores, live_mask)
    rounded = attention.astype(jnp.bfloat16)
    context = jnp.einsum(
        "hts,shd->thd", rounded, value_slots, preferred_element_type=jnp.float32
    ).astype(jnp.bfloat16)
    grad_raw = jnp.einsum(
        "thd,shd->hts", grad_heads, value_slots, preferred_element_type=jnp.float32
    )
    deltas = jnp.sum(attention * grad_raw, axis=2, keepdims=True)
    score_grad = (attention * (grad_raw - deltas) * scaling).astype(jnp.bfloat16)
    query_grad = jnp.einsum(
        "hts,shd->thd", score_grad, key_slots, preferred_element_type=jnp.float32
    ).astype(jnp.bfloat16)
    key_grad = jnp.einsum(
        "hts,thd->shd", score_grad, query_heads, preferred_element_type=jnp.float32
    ).astype(jnp.bfloat16)
    value_grad = jnp.einsum(
        "hts,thd->shd", rounded, grad_heads, preferred_element_type=jnp.float32
    ).astype(jnp.bfloat16)
    slot_grads = jnp.concatenate(
        [
            key_grad.reshape(bin_count, block_rows, head_width),
            value_grad.reshape(bin_count, block_rows, head_width),
        ],
        axis=2,
    )
    returned = lax.all_to_all(slot_grads, "dp", split_axis=0, concat_axis=0, tiled=True)
    own_grads = jnp.dot(
        route_table,
        returned.reshape(bin_count, block_rows * 2 * head_width),
        preferred_element_type=jnp.float32,
    )
    own_grads = own_grads.astype(jnp.bfloat16).reshape(encoder_rows.shape[0], 2 * head_width)
    weight_terms = lax.dot_general(
        encoder_rows, own_grads, (((0,), (0,)), ((), ())), preferred_element_type=jnp.float32
    )
    weight_sums = lax.psum_scatter(
        weight_terms.astype(jnp.bfloat16), "dp", scatter_dimension=0, tiled=True
    ).astype(jnp.float32)
    key_weight_grad = weight_sums[:, :head_width].astype(jnp.bfloat16)
    value_weight_grad = weight_sums[:, head_width:].astype(jnp.bfloat16)
    row_terms = lax.dot_general(
        own_grads, both_weights, (((1,), (1,)), ((), ())), preferred_element_type=jnp.float32
    )
    encoder_grad = lax.psum_scatter(
        row_terms.astype(jnp.bfloat16), "mp", scatter_dimension=1, tiled=True
    )
    return (
        context.reshape(token_count, head_width),
        query_grad.reshape(token_count, head_width),
        encoder_grad,
        key_weight_grad,
        value_weight_grad,
    )


MESH = pl.DeviceIdType.MESH


def contract(a, b, dim_a, dim_b):
    return lax.dot_general(
        a, b, (((dim_a,), (dim_b,)), ((), ())), preferred_element_type=jnp.float32
    )


def step_kernel(
    n,
    count,
    q_ref,
    g_ref,
    enc_hbm,
    kw_ref,
    vw_ref,
    lengths_ref,
    bins_ref,
    docs_ref,
    table_ref,
    ctx_ref,
    qg_ref,
    eg_ref,
    kwg_ref,
    vwg_ref,
    enc,
    wts,
    wend,
    acc,
    arrived,
    tags,
    arrived_tags,
    grads,
    ret,
    own,
    gend,
    pend,
    msend,
    mrecv,
    tsend,
    trecv,
    hops,
    passed,
    local_sem,
    gather_send,
    gather_recv,
    lift_send,
    lift_recv,
    core_send,
    core_recv,
    tag_send,
    tag_recv,
    out_send,
    out_recv,
    back_send,
    back_recv,
    g_send,
    g_recv,
    mid_send,
    mid_recv,
    end_send,
    end_recv,
    prod_send,
    prod_recv,
    pair_send,
    pair_recv,
    hop_send,
    hop_recv,
):
    bf16 = jnp.bfloat16
    me, z = lax.axis_index("dp"), lax.axis_index("mp")
    core = me % 2
    x = (me // 2) % 2
    y = me // 4

    def place(py, px, pc):
        return (py * 2 + px) * 2 + pc

    at_x, at_y = place(y, 1 - x, core), place(1 - y, x, core)
    at_c, at_d = place(y, x, 1 - core), place(1 - y, 1 - x, core)
    c_x, c_y = place(y, 1 - x, 1 - core), place(1 - y, x, 1 - core)
    c_d = place(1 - y, 1 - x, 1 - core)
    depth, width = kw_ref.shape
    rows = enc.shape[0]
    blocks = rows // BLK
    blk = BLK
    heads = width // HD
    tokens = q_ref.shape[0]
    last = count - 1
    end = (z // 2) * last
    far_end = last - end
    side = z // 2
    is_end = z == end
    is_inner = z != end
    mate = z + 1 - 2 * (z % 2)
    across = last - z

    def remote(src, dst, send, recv, **device):
        return pltpu.make_async_remote_copy(
            src_ref=src,
            dst_ref=dst,
            send_sem=send,
            recv_sem=recv,
            device_id=device,
            device_id_type=MESH,
        )

    load_enc = pltpu.make_async_copy(enc_hbm, enc, local_sem.at[0])
    load_enc.start()
    barrier = pltpu.get_barrier_semaphore()
    for d in range(1, n):
        pl.semaphore_signal(
            barrier, inc=1, device_id={"dp": (me + d) % n}, device_id_type=MESH
        )
    for d in range(1, count):
        pl.semaphore_signal(
            barrier, inc=1, device_id={"mp": (z + d) % count}, device_id_type=MESH
        )

    for d in range(n):
        to = (me + d) % n
        doc = jnp.int32(-1)
        for b in range(blocks):
            doc = jnp.where(bins_ref[b] == to, docs_ref[b], doc)
        tags[to] = jnp.full(tags.shape[1:], doc.astype(jnp.float32), jnp.float32)
    pl.semaphore_wait(barrier, n - 1 + count - 1)

    def part_cols(part):
        return pl.ds(part * width, width)

    def land(src, part):
        return wts.at[src, :, part_cols(part)]

    started = []

    def ship(ident, ref, src, part, to):
        copy = remote(
            ref, land(src, part), gather_send.at[ident], gather_recv.at[ident], dp=to
        )
        copy.start()
        started.append(copy)

    def landed(ident, src, part):
        remote(
            land(src, part), land(src, part), gather_send.at[ident], gather_recv.at[ident], dp=at_c
        ).wait_recv()

    def lifted(src, part):
        return wend.at[src % 4, :, part_cols(part)]

    ours, theirs = (me, at_x, at_y, at_d), (at_c, c_x, c_y, c_d)
    pieces = [(0, 0), (0, 1), (1, 0), (2, 1), (1, 1), (2, 0), (3, 0), (3, 1)]

    def lift(i, part, ref=None):
        src = ours[i]
        ident = 2 * i + part

        @pl.when(jnp.logical_and(is_end, src // 4 != side))
        def _():
            remote(
                land(src, part) if ref is None else ref,
                lifted(src, part),
                lift_send.at[ident],
                lift_recv.at[ident],
                mp=mate,
            ).start()

    def each_piece(todo, listed, of_end):
        for i, part in listed:

            @pl.when(jnp.logical_and(is_end if of_end else is_inner, ours[i] // 4 != side))
            def _():
                todo(i, part, ours[i], theirs[i])

    def lift_copy(i, part, src):
        ident = 2 * i + part
        return remote(
            lifted(src, part), lifted(src, part), lift_send.at[ident], lift_recv.at[ident], mp=mate
        )

    def core_copy(i, part, src):
        ident = 2 * i + part
        return remote(
            lifted(src, part), lifted(src, part), core_send.at[ident], core_recv.at[ident], dp=at_c
        )

    def hand_over(i, part, src, mirror):
        lift_copy(i, part, src).wait_recv()
        core_copy(i, part, src).start()

    ship(0, kw_ref, me, 0, at_x)
    ship(3, vw_ref, me, 1, at_y)
    ship(1, vw_ref, me, 1, at_x)
    ship(2, kw_ref, me, 0, at_y)
    ship(6, kw_ref, me, 0, at_c)
    ship(7, vw_ref, me, 1, at_c)
    lift(0, 0, kw_ref)
    lift(0, 1, vw_ref)
    own_k = pltpu.make_async_copy(kw_ref, land(me, 0), local_sem.at[1])
    own_v = pltpu.make_async_copy(vw_ref, land(me, 1), local_sem.at[2])
    own_k.start()
    own_v.start()
    tag_copies = []
    for d in range(1, n):
        to = (me + d) % n
        copy = remote(
            tags.at[to], arrived_tags.at[me], tag_send.at[d], tag_recv.at[d], dp=to
        )
        copy.start()
        tag_copies.append(copy)
    arrived_tags[me] = tags[me]
    own_k.wait()
    own_v.wait()
    load_enc.wait()

    def multiply(src, part, first=False):
        columns = pl.ds(pl.multiple_of(src * depth, depth), depth)

        @pl.loop(0, width // HD)
        def _(t):
            cols = pl.ds(pl.multiple_of(part * width + t * HD, HD), HD)
            product = jnp.dot(
                enc[:, columns], wts[src, :, cols], preferred_element_type=jnp.float32
            ).reshape(blocks, blk, HD)
            if first:
                acc[:, :, cols] = product
            else:
                acc[:, :, cols] += product

    multiply(me, 0, True)
    multiply(me, 1, True)
    landed(6, at_c, 0)
    multiply(at_c, 0)
    landed(7, at_c, 1)
    multiply(at_c, 1)
    landed(0, at_x, 0)
    ship(4, land(at_x, 0), at_x, 0, at_y)
    ship(8, land(at_x, 0), at_x, 0, at_c)
    lift(1, 0)
    landed(3, at_y, 1)
    ship(5, land(at_y, 1), at_y, 1, at_x)
    ship(11, land(at_y, 1), at_y, 1, at_c)
    lift(2, 1)
    multiply(at_x, 0)
    multiply(at_y, 1)
    landed(8, c_x, 0)
    multiply(c_x, 0)
    landed(11, c_y, 1)
    multiply(c_y, 1)
    landed(1, at_x, 1)
    ship(9, land(at_x, 1), at_x, 1, at_c)
    lift(1, 1)
    landed(2, at_y, 0)
    ship(10, land(at_y, 0), at_y, 0, at_c)
    lift(2, 0)
    multiply(at_x, 1)
    multiply(at_y, 0)
    landed(9, c_x, 1)
    multiply(c_x, 1)
    landed(10, c_y, 0)
    multiply(c_y, 0)
    landed(4, at_d, 0)
    ship(12, land(at_d, 0), at_d, 0, at_c)
    lift(3, 0)
    landed(5, at_d, 1)
    ship(13, land(at_d, 1), at_d, 1, at_c)
    lift(3, 1)
    multiply(at_d, 0)
    multiply(at_d, 1)
    landed(12, c_d, 0)
    multiply(c_d, 0)
    landed(13, c_d, 1)
    multiply(c_d, 1)

    def rows_of(slot):
        return pl.ds(pl.multiple_of(slot * blk, blk), blk)

    def slot_at(i):
        flip_c, flip_x, flip_y = i % 2, (i // 2) % 2, i // 4
        return place(
            y + flip_y - 2 * y * flip_y,
            x + flip_x - 2 * x * flip_x,
            core + flip_c - 2 * core * flip_c,
        )

    def out_copy(h, i):
        to = slot_at(i)
        return remote(
            grads.at[h, :, rows_of(to), :],
            arrived.at[h, :, rows_of(me), :],
            out_send.at[h, i],
            out_recv.at[h, i],
            dp=to,
        )

    for h in range(heads):
        for i in [*range(1, n), 0]:
            to = slot_at(i)
            for part in range(2):
                cols = pl.ds(part * width + h * HD, HD)
                picked = acc[table_ref[0, to], :, cols].astype(bf16)
                if i == 0:
                    arrived[h, part, rows_of(me), :] = picked
                else:
                    grads[h, part, rows_of(to), :] = picked
            if i > 0:
                out_copy(h, i).start()

    each_piece(hand_over, pieces[:6], False)
    position = lax.broadcasted_iota(jnp.int32, (tokens, 1), 0)
    token_doc = jnp.zeros(position.shape, jnp.float32)
    doc_end = jnp.int32(0)
    for k in range(lengths_ref.shape[1]):
        doc_end = doc_end + lengths_ref[0, k]
        token_doc = token_doc + jnp.where(position >= doc_end, 1.0, 0.0)
    for copy in tag_copies:
        copy.wait()
    tag_row = jnp.concatenate([arrived_tags[s, 0:1, :] for s in range(n)], axis=1)
    live = tag_row == token_doc
    present = jnp.max(jnp.where(live, 1.0, 0.0), axis=1, keepdims=True) > 0.0
    scaling = HD ** (-0.5)
    for h in range(heads):
        for i in range(1, n):
            out_copy(h, i).wait()
        hk = pl.ds(h * HD, HD)
        q, g = q_ref[:, hk], g_ref[:, hk]
        scores = contract(q, arrived[h, 0], 1, 1) * scaling
        highest = jnp.max(jnp.where(live, scores, masked_value), axis=1, keepdims=True)
        highest = jnp.where(present, highest, 0.0)
        raised = jnp.exp(jnp.where(live, scores - highest, masked_value))
        totals = jnp.maximum(jnp.sum(raised, axis=1, keepdims=True), 1.0)
        attention = raised / totals
        rounded = attention.astype(bf16)
        grad_raw = contract(g, arrived[h, 1], 1, 1)
        deltas = jnp.sum(attention * grad_raw, axis=1, keepdims=True)
        score_grad = (attention * (grad_raw - deltas) * scaling).astype(bf16)
        grads[h, 0] = contract(score_grad, q, 0, 0).astype(bf16)
        grads[h, 1] = contract(rounded, g, 0, 0).astype(bf16)
        tsend[h, pl.ds(0, tokens), :] = rounded
        tsend[h, pl.ds(tokens, tokens), :] = score_grad
        if h == 0:
            each_piece(hand_over, pieces[6:], False)

    def back_copy(i):
        to = slot_at(i)
        return remote(
            grads.at[:, :, rows_of(to), :],
            ret.at[:, :, rows_of(me), :],
            back_send.at[i],
            back_recv.at[i],
            dp=to,
        )

    for i in range(1, n):
        back_copy(i).start()
    ret[:, :, rows_of(me), :] = grads[:, :, rows_of(me), :]
    for h in range(heads):
        hk = pl.ds(h * HD, HD)
        ctx_ref[:, hk] = jnp.dot(
            tsend[h, pl.ds(0, tokens), :], arrived[h, 1], preferred_element_type=jnp.float32
        ).astype(bf16)
        qg_ref[:, hk] = jnp.dot(
            tsend[h, pl.ds(tokens, tokens), :], arrived[h, 0], preferred_element_type=jnp.float32
        ).astype(bf16)

    def g_copy(r):
        return remote(own.at[r], gend.at[r], g_send.at[r], g_recv.at[r], mp=mate)

    def mid_copy(way, r):
        return remote(
            msend.at[way, r], mrecv.at[way, r], mid_send.at[way, r], mid_recv.at[way, r], mp=across
        )

    def end_copy(r):
        return remote(mrecv.at[0, r], mrecv.at[0, r], end_send.at[r], end_recv.at[r], mp=mate)

    def prod_copy(r):
        return remote(msend.at[0, r], pend.at[r], prod_send.at[r], prod_recv.at[r], mp=mate)

    def pair_copy(i):
        return remote(tsend.at[i], trecv.at[i], pair_send.at[i], pair_recv.at[i], dp=at_c)

    def hop_copy(way, i, src):
        to = at_x if (way == 0) == (i < 2) else at_y
        return remote(src, hops.at[way, i], hop_send.at[way, i], hop_recv.at[way, i], dp=to)

    for i, part in pieces:

        @pl.when(jnp.logical_and(is_inner, theirs[i] // 4 != side))
        def _():
            core_copy(i, part, theirs[i]).wait_recv()

    def collect(r):
        back_copy_at = slot_at(r + 1)
        remote(
            ret.at[:, :, rows_of(back_copy_at), :],
            ret.at[:, :, rows_of(back_copy_at), :],
            back_send.at[r + 1],
            back_recv.at[r + 1],
            dp=at_c,
        ).wait_recv()
        later = table_ref[2, r] > 0
        for h in range(heads):
            for part in range(2):
                own[r, :, pl.ds(part * width + h * HD, HD)] = jnp.where(
                    later,
                    ret[h, part, rows_of(back_copy_at), :],
                    ret[h, part, rows_of(slot_at(r)), :],
                )

        @pl.when(is_end)
        def _():
            g_copy(r).start()

    def own_weights(d, j):
        return wts[2 * d + j]

    def end_weights(d, j):
        return wend[(d % 2) * 2 + j]

    def shard_of(i, parity):
        flip_x, flip_y = 1 - i // 2, 1 - i % 2
        px = x + flip_x - 2 * x * flip_x
        py = y + flip_y - 2 * y * flip_y
        return place(py, px, parity)

    def term(shard, part, h):
        columns = pl.ds(pl.multiple_of(shard * depth, depth), depth)
        return contract(enc[:, columns], ret[h, part, pl.ds(0, rows), :], 0, 0).astype(bf16)

    def each_slab(todo):
        for part in range(2):
            for h in range(heads):
                todo(part, h, pl.ds(part * width + h * HD, HD))

    def half_cols(j):
        return pl.ds(pl.multiple_of(j * width, width), width)

    @pl.loop(0, blocks)
    def _(r):
        @pl.when(r < 3)
        def _():
            collect(r)

        @pl.when(is_inner)
        def _():
            g_copy(r).wait_recv()
            for way, dest in ((0, far_end), (1, across)):

                @pl.loop(0, 2)
                def _(j):
                    summed = contract(own[r], own_weights(dest, j), 1, 1)
                    summed += contract(gend[r], end_weights(dest, j), 1, 1)
                    msend[way, r, :, half_cols(j)] = summed.astype(bf16)

                mid_copy(way, r).start()

        @pl.when(r == 2)
        def _():
            @pl.loop(3, blocks)
            def _(later):
                collect(later)

            for b in range(blocks):
                block = own[table_ref[1, b]]
                for h in range(heads):
                    for part in range(2):
                        first = part * width + h * HD
                        ret[h, part, pl.ds(b * blk, blk), :] = block[:, first : first + HD]

            @pl.loop(0, 4)
            def _(i):
                shard = shard_of(i, 1 - core)

                def fill(part, h, cols):
                    tsend[i, :, cols] = term(shard, part, h)

                each_slab(fill)
                pair_copy(i).start()

        @pl.when(r == 3)
        def _():
            @pl.loop(0, 4)
            def _(i):
                shard = shard_of(i, core)
                pair_copy(i).wait_recv()

                def fill(part, h, cols):
                    summed = term(shard, part, h).astype(jnp.float32)
                    summed += trecv[i, :, cols].astype(jnp.float32)
                    trecv[i, :, cols] = summed.astype(bf16)

                each_slab(fill)

                @pl.when(i == 1)
                def _():
                    hop_copy(0, 1, trecv.at[0, :, part_cols(0)]).start()
                    hop_copy(0, 0, trecv.at[1, :, part_cols(0)]).start()
                    hop_copy(1, 1, trecv.at[0, :, part_cols(1)]).start()

                @pl.when(i == 2)
                def _():
                    hop_copy(1, 0, trecv.at[2, :, part_cols(1)]).start()

    @pl.when(is_end)
    def _():
        @pl.loop(0, blocks)
        def _(r):
            @pl.loop(0, 2)
            def _(j):
                msend[0, r, :, half_cols(j)] = contract(own[r], own_weights(mate, j), 1, 1).astype(bf16)

            prod_copy(r).start()

    for way in range(2):
        hop_copy(way, 1, hops.at[way, 1]).wait_recv()
        summed = trecv[2 - way, :, part_cols(way)].astype(jnp.float32)
        summed += hops[way, 1].astype(jnp.float32)
        passed[way] = summed.astype(bf16)
        hop_copy(way, 2, passed.at[way]).start()

    total = acc.at[0]

    def own_product(r, dest):
        @pl.loop(0, 2)
        def _(j):
            total[:, half_cols(j)] = contract(own[r], own_weights(dest, j), 1, 1)

    @pl.loop(0, blocks)
    def _(r):
        @pl.when(is_inner)
        def _():
            own_product(r, end)
            mid_copy(0, r).wait_recv()
            mrecv[0, r] = (total[...] + mrecv[0, r].astype(jnp.float32)).astype(bf16)
            end_copy(r).start()
            own_product(r, z)
            prod_copy(r).wait_recv()
            total[...] += pend[r].astype(jnp.float32)
            mid_copy(1, r).wait_recv()
            eg_ref[r] = (total[...] + mrecv[1, r].astype(jnp.float32)).astype(bf16)

        @pl.when(is_end)
        def _():
            own_product(r, z)
            end_copy(r).wait_recv()
            eg_ref[r] = (total[...] + mrecv[0, r].astype(jnp.float32)).astype(bf16)

        @pl.when(r == blocks - 2)
        def _():
            for way, out in ((0, kwg_ref), (1, vwg_ref)):
                hop_copy(way, 0, hops.at[way, 0]).wait_recv()
                hop_copy(way, 2, hops.at[way, 2]).wait_recv()
                summed = trecv[3, :, part_cols(way)].astype(jnp.float32)
                summed += hops[way, 0].astype(jnp.float32) + hops[way, 2].astype(jnp.float32)
                out[...] = summed.astype(bf16)

    for copy in started:
        copy.wait_send()
    each_piece(lambda i, part, src, mirror: lift_copy(i, part, src).wait_send(), pieces, True)
    each_piece(lambda i, part, src, mirror: core_copy(i, part, src).wait_send(), pieces, False)

    @pl.loop(0, blocks)
    def _(r):
        @pl.when(is_end)
        def _():
            g_copy(r).wait_send()
            prod_copy(r).wait_send()

        @pl.when(is_inner)
        def _():
            mid_copy(0, r).wait_send()
            mid_copy(1, r).wait_send()
            end_copy(r).wait_send()

    for i in range(1, n):
        back_copy(i).wait_send()
    for i in range(4):
        pair_copy(i).wait_send()
    for way in range(2):
        for i in range(3):
            hop_copy(way, i, hops.at[way, i]).wait_send()


def deliver_kernel(table_ref, *refs):
    count = (len(refs) - 2) // 3
    ins, outs = refs[:count], refs[count : 2 * count]
    held, (load_sem, store_sem) = refs[2 * count : 3 * count], refs[3 * count :]
    loads, stores = [], []
    for k in range(count):
        pieces = [(ins[k], held[k], outs[k])]
        if len(ins[k].shape) == 3:
            blocks, size, _ = ins[k].shape
            pieces = [
                (ins[k].at[table_ref[1, b]], held[k].at[b], outs[k].at[pl.ds(b * size, size), :])
                for b in range(blocks)
            ]
        for source, room, target in pieces:
            ident = len(loads)
            load = pltpu.make_async_copy(source, room, load_sem.at[ident])
            load.start()
            loads.append(load)
            stores.append(pltpu.make_async_copy(room, target, store_sem.at[ident]))
    for load, store in zip(loads, stores):
        load.wait()
        store.start()
    for store in stores:
        store.wait()


def deliver(table, arrays):
    hbm = pl.BlockSpec(memory_space=pl.ANY)
    copies = sum(a.shape[0] if a.ndim == 3 else 1 for a in arrays)
    dma = pltpu.SemaphoreType.DMA((copies,))
    return pl.pallas_call(
        deliver_kernel,
        out_shape=tuple(
            jax.ShapeDtypeStruct((a.size // a.shape[-1], a.shape[-1]), a.dtype) for a in arrays
        ),
        in_specs=[pl.BlockSpec(memory_space=pltpu.SMEM)] + [hbm] * len(arrays),
        out_specs=(hbm,) * len(arrays),
        scratch_shapes=[pltpu.VMEM(a.shape, a.dtype) for a in arrays] + [dma, dma],
    )(table, *arrays)


def per_device_cube(
    queries,
    context_grad,
    encoder_rows,
    key_weight,
    value_weight,
    document_lengths,
    block_bin,
    block_document,
):
    n, count = lax.axis_size("dp"), lax.axis_size("mp")
    rows, model = encoder_rows.shape
    depth, width = key_weight.shape
    heads = width // HD
    tokens = queries.shape[0]
    blocks = rows // BLK
    chips = n // 2
    me = lax.axis_index("dp")
    order = jnp.arange(n, dtype=jnp.int32)
    hits = block_bin[None, :] == order[:, None]
    held = jnp.sum(jnp.where(hits, jnp.arange(blocks, dtype=jnp.int32)[None, :], 0), axis=1)
    hole = (n * (n - 1) // 2 - jnp.sum(block_bin)) ^ me
    turn = jnp.pad(block_bin, (0, n - blocks)) ^ me
    turn = jnp.clip(turn - (turn > hole).astype(jnp.int32), 0, blocks - 1)
    table = jnp.stack([held, turn, (order >= hole).astype(jnp.int32)])
    vmem = pl.BlockSpec(memory_space=pltpu.VMEM)
    smem = pl.BlockSpec(memory_space=pltpu.SMEM)
    hbm = pl.BlockSpec(memory_space=pl.ANY)
    bf16 = jnp.bfloat16
    dma = pltpu.SemaphoreType.DMA
    shape = jax.ShapeDtypeStruct
    pairs = []
    for extent in [(14,), (8,), (8,), (n,), (heads, n), (n,), (blocks,), (2, blocks), (blocks,), (blocks,), (chips,), (2, 3)]:
        pairs += [dma(extent), dma(extent)]
    outs = pl.pallas_call(
        functools.partial(step_kernel, n, count),
        out_shape=(
            shape((tokens, width), bf16),
            shape((tokens, width), bf16),
            shape((blocks, BLK, model // count), bf16),
            shape((depth, width), bf16),
            shape((depth, width), bf16),
        ),
        in_specs=[vmem, vmem, hbm, vmem, vmem, smem, smem, smem, smem],
        out_specs=(vmem,) * 5,
        scratch_shapes=[
            pltpu.VMEM((rows, model), bf16),
            pltpu.VMEM((n, depth, 2 * width), bf16),
            pltpu.VMEM((n // 2, depth, 2 * width), bf16),
            pltpu.VMEM((blocks, BLK, 2 * width), jnp.float32),
            pltpu.VMEM((heads, 2, n * BLK, HD), bf16),
            pltpu.VMEM((n, 8, BLK), jnp.float32),
            pltpu.VMEM((n, 8, BLK), jnp.float32),
            pltpu.VMEM((heads, 2, n * BLK, HD), bf16),
            pltpu.VMEM((heads, 2, n * BLK, HD), bf16),
            pltpu.VMEM((blocks, BLK, 2 * width), bf16),
            pltpu.VMEM((blocks, BLK, 2 * width), bf16),
            pltpu.VMEM((blocks, BLK, 2 * width), bf16),
            pltpu.VMEM((2, blocks, BLK, 2 * width), bf16),
            pltpu.VMEM((2, blocks, BLK, 2 * width), bf16),
            pltpu.VMEM((chips, depth, 2 * width), bf16),
            pltpu.VMEM((chips, depth, 2 * width), bf16),
            pltpu.VMEM((2, 3, depth, width), bf16),
            pltpu.VMEM((2, depth, width), bf16),
            dma((3,)),
            *pairs,
        ],
        compiler_params=pltpu.CompilerParams(
            collective_id=0, has_side_effects=True, vmem_limit_bytes=67043328
        ),
    )(
        queries,
        context_grad,
        encoder_rows,
        key_weight,
        value_weight,
        document_lengths,
        block_bin,
        block_document,
        table,
    )
    return deliver(table, outs)


def solution(mesh):
    in_specs = (
        P("dp", "mp"),
        P("dp", "mp"),
        P("dp", None),
        P("dp", "mp"),
        P("dp", "mp"),
        P("dp", None),
        P("dp"),
        P("dp"),
    )
    out_specs = (P("dp", "mp"), P("dp", "mp"), P("dp", "mp"), P("dp", "mp"), P("dp", "mp"))
    cube = mesh.shape["dp"] == 2 * 2 * 2 and mesh.shape["mp"] == 2 * 2
    return jax.shard_map(
        per_device_cube if cube else per_device, mesh=mesh, in_specs=in_specs, out_specs=out_specs, check_vma=False
    )
```

```python
import functools

import jax
import jax.numpy as jnp
from jax import lax
from jax.experimental import pallas as pl
from jax.experimental.pallas import tpu as pltpu
from jax.sharding import PartitionSpec as P

HD = 256
BLK = 128


masked_value = -1e30


def attend_weights(scores, live_mask):
    present = jnp.any(live_mask, axis=1)[None, :, None]
    blocked = jnp.where(live_mask[None], scores, masked_value)
    highest = jnp.max(blocked, axis=2, keepdims=True)
    highest = jnp.where(present, highest, 0.0)
    raised = jnp.exp(jnp.where(live_mask[None], scores - highest, masked_value))
    totals = jnp.maximum(jnp.sum(raised, axis=2, keepdims=True), 1.0)
    return raised / totals


def token_documents(lengths, token_count):
    doc_ends = jnp.cumsum(lengths)
    positions = jnp.arange(token_count, dtype=jnp.int32)
    return jnp.sum((doc_ends[None, :] <= positions[:, None]).astype(jnp.int32), axis=1)


def per_device(
    queries,
    context_grad,
    encoder_rows,
    key_weight,
    value_weight,
    document_lengths,
    block_bin,
    block_document,
):
    bin_count = lax.axis_size("dp")
    full_key, full_value = (
        lax.all_gather(key_weight, "dp", axis=0, tiled=True),
        lax.all_gather(value_weight, "dp", axis=0, tiled=True),
    )
    head_width = full_key.shape[1]
    head_count = head_width // HD
    block_rows = BLK
    blocks_here = block_bin.shape[0]
    both_weights = jnp.concatenate([full_key, full_value], axis=1)
    projected = jnp.dot(encoder_rows, both_weights, preferred_element_type=jnp.float32).astype(
        jnp.bfloat16
    )
    route_table = (block_bin[:, None] == jnp.arange(bin_count, dtype=jnp.int32)[None, :]).astype(
        jnp.bfloat16
    )
    flat_blocks = projected.reshape(blocks_here, block_rows * 2 * head_width)
    outbound = lax.dot_general(
        route_table, flat_blocks, (((0,), (0,)), ((), ())), preferred_element_type=jnp.float32
    )
    outbound = outbound.astype(jnp.bfloat16).reshape(bin_count, block_rows, 2 * head_width)
    slot_docs = (
        lax.dot_general(
            route_table.astype(jnp.float32),
            (block_document + 1).astype(jnp.float32),
            (((0,), (0,)), ((), ())),
        )
        - 1.0
    )
    tag_rows = jnp.broadcast_to(slot_docs[:, None], (bin_count, block_rows)).astype(jnp.bfloat16)
    arrived, arrived_tags = (
        lax.all_to_all(outbound, "dp", split_axis=0, concat_axis=0, tiled=True),
        lax.all_to_all(tag_rows, "dp", split_axis=0, concat_axis=0, tiled=True),
    )
    key_slots = arrived[:, :, :head_width].reshape(bin_count * block_rows, head_count, HD)
    value_slots = arrived[:, :, head_width:].reshape(bin_count * block_rows, head_count, HD)
    token_count = queries.shape[0]
    token_docs = token_documents(document_lengths[0], token_count).astype(jnp.float32)
    live_mask = arrived_tags.reshape(-1).astype(jnp.float32)[None, :] == token_docs[:, None]
    query_heads = queries.reshape(token_count, head_count, HD)
    grad_heads = context_grad.reshape(token_count, head_count, HD)
    scaling = HD ** (-0.5)
    scores = (
        jnp.einsum("thd,shd->hts", query_heads, key_slots, preferred_element_type=jnp.float32)
        * scaling
    )
    attention = attend_weights(scores, live_mask)
    rounded = attention.astype(jnp.bfloat16)
    context = jnp.einsum(
        "hts,shd->thd", rounded, value_slots, preferred_element_type=jnp.float32
    ).astype(jnp.bfloat16)
    grad_raw = jnp.einsum(
        "thd,shd->hts", grad_heads, value_slots, preferred_element_type=jnp.float32
    )
    deltas = jnp.sum(attention * grad_raw, axis=2, keepdims=True)
    score_grad = (attention * (grad_raw - deltas) * scaling).astype(jnp.bfloat16)
    query_grad = jnp.einsum(
        "hts,shd->thd", score_grad, key_slots, preferred_element_type=jnp.float32
    ).astype(jnp.bfloat16)
    key_grad = jnp.einsum(
        "hts,thd->shd", score_grad, query_heads, preferred_element_type=jnp.float32
    ).astype(jnp.bfloat16)
    value_grad = jnp.einsum(
        "hts,thd->shd", rounded, grad_heads, preferred_element_type=jnp.float32
    ).astype(jnp.bfloat16)
    slot_grads = jnp.concatenate(
        [
            key_grad.reshape(bin_count, block_rows, head_width),
            value_grad.reshape(bin_count, block_rows, head_width),
        ],
        axis=2,
    )
    returned = lax.all_to_all(slot_grads, "dp", split_axis=0, concat_axis=0, tiled=True)
    own_grads = jnp.dot(
        route_table,
        returned.reshape(bin_count, block_rows * 2 * head_width),
        preferred_element_type=jnp.float32,
    )
    own_grads = own_grads.astype(jnp.bfloat16).reshape(encoder_rows.shape[0], 2 * head_width)
    weight_terms = lax.dot_general(
        encoder_rows, own_grads, (((0,), (0,)), ((), ())), preferred_element_type=jnp.float32
    )
    weight_sums = lax.psum_scatter(
        weight_terms.astype(jnp.bfloat16), "dp", scatter_dimension=0, tiled=True
    ).astype(jnp.float32)
    key_weight_grad = weight_sums[:, :head_width].astype(jnp.bfloat16)
    value_weight_grad = weight_sums[:, head_width:].astype(jnp.bfloat16)
    row_terms = lax.dot_general(
        own_grads, both_weights, (((1,), (1,)), ((), ())), preferred_element_type=jnp.float32
    )
    encoder_grad = lax.psum_scatter(
        row_terms.astype(jnp.bfloat16), "mp", scatter_dimension=1, tiled=True
    )
    return (
        context.reshape(token_count, head_width),
        query_grad.reshape(token_count, head_width),
        encoder_grad,
        key_weight_grad,
        value_weight_grad,
    )


MESH = pl.DeviceIdType.MESH


def contract(a, b, dim_a, dim_b):
    return lax.dot_general(
        a, b, (((dim_a,), (dim_b,)), ((), ())), preferred_element_type=jnp.float32
    )


def bin_at(me, i):
    def flip(bit, turned):
        return bit + turned - 2 * bit * turned

    core, x, y = me % 2, (me // 2) % 2, me // 4
    return (flip(y, i // 4) * 2 + flip(x, (i // 2) % 2)) * 2 + flip(core, i % 2)


def find(value, options):
    index = jnp.int32(0)
    for k, option in enumerate(options):
        index = jnp.where(option == value, k, index)
    return index


def block_turns(me, n, bins_ref):
    bins = [bins_ref[b] for b in range(bins_ref.shape[0])]
    order = [bin_at(me, i) for i in range(n)]
    hole = find(n * (n - 1) // 2 - sum(bins), order)
    places = [find(b, order) for b in bins]
    return hole, [jnp.where(p > hole, p - 1, p) for p in places]


def step_kernel(
    n,
    count,
    q_ref,
    g_ref,
    enc_hbm,
    kw_ref,
    vw_ref,
    lengths_ref,
    bins_ref,
    docs_ref,
    ctx_ref,
    qg_ref,
    eg_ref,
    kwg_ref,
    vwg_ref,
    enc,
    wts,
    wend,
    acc,
    arrived,
    tags,
    arrived_tags,
    grads,
    ret,
    own,
    gend,
    pend,
    msend,
    mrecv,
    tsend,
    trecv,
    hops,
    passed,
    local_sem,
    gather_send,
    gather_recv,
    lift_send,
    lift_recv,
    core_send,
    core_recv,
    tag_send,
    tag_recv,
    out_send,
    out_recv,
    back_send,
    back_recv,
    g_send,
    g_recv,
    mid_send,
    mid_recv,
    end_send,
    end_recv,
    prod_send,
    prod_recv,
    pair_send,
    pair_recv,
    hop_send,
    hop_recv,
):
    bf16 = jnp.bfloat16
    me, z = lax.axis_index("dp"), lax.axis_index("mp")
    core = me % 2
    x = (me // 2) % 2
    y = me // 4

    def place(py, px, pc):
        return (py * 2 + px) * 2 + pc

    at_x, at_y = place(y, 1 - x, core), place(1 - y, x, core)
    at_c, at_d = place(y, x, 1 - core), place(1 - y, 1 - x, core)
    c_x, c_y = place(y, 1 - x, 1 - core), place(1 - y, x, 1 - core)
    c_d = place(1 - y, 1 - x, 1 - core)
    depth, width = kw_ref.shape
    rows = enc.shape[0]
    blocks = rows // BLK
    blk = BLK
    heads = width // HD
    tokens = q_ref.shape[0]
    last = count - 1
    end = (z // 2) * last
    far_end = last - end
    side = z // 2
    is_end = z == end
    is_inner = z != end
    mate = z + 1 - 2 * (z % 2)
    across = last - z

    def remote(src, dst, send, recv, **device):
        return pltpu.make_async_remote_copy(
            src_ref=src,
            dst_ref=dst,
            send_sem=send,
            recv_sem=recv,
            device_id=device,
            device_id_type=MESH,
        )

    load_enc = pltpu.make_async_copy(enc_hbm, enc, local_sem.at[0])
    load_enc.start()
    barrier = pltpu.get_barrier_semaphore()
    for d in range(1, n):
        pl.semaphore_signal(
            barrier, inc=1, device_id={"dp": (me + d) % n}, device_id_type=MESH
        )
    for d in range(1, count):
        pl.semaphore_signal(
            barrier, inc=1, device_id={"mp": (z + d) % count}, device_id_type=MESH
        )

    for d in range(n):
        to = (me + d) % n
        doc = jnp.int32(-1)
        for b in range(blocks):
            doc = jnp.where(bins_ref[b] == to, docs_ref[b], doc)
        tags[to] = jnp.full(tags.shape[1:], doc.astype(jnp.float32), jnp.float32)
    pl.semaphore_wait(barrier, n - 1 + count - 1)

    def part_cols(part):
        return pl.ds(part * width, width)

    def land(src, part):
        return wts.at[src, :, part_cols(part)]

    started = []

    def ship(ident, ref, src, part, to):
        copy = remote(
            ref, land(src, part), gather_send.at[ident], gather_recv.at[ident], dp=to
        )
        copy.start()
        started.append(copy)

    def landed(ident, src, part):
        remote(
            land(src, part), land(src, part), gather_send.at[ident], gather_recv.at[ident], dp=at_c
        ).wait_recv()

    def lifted(src, part):
        return wend.at[src % 4, :, part_cols(part)]

    ours, theirs = (me, at_x, at_y, at_d), (at_c, c_x, c_y, c_d)
    pieces = [(0, 0), (0, 1), (1, 0), (2, 1), (1, 1), (2, 0), (3, 0), (3, 1)]

    def lift(i, part, ref=None):
        src = ours[i]
        ident = 2 * i + part

        @pl.when(jnp.logical_and(is_end, src // 4 != side))
        def _():
            remote(
                land(src, part) if ref is None else ref,
                lifted(src, part),
                lift_send.at[ident],
                lift_recv.at[ident],
                mp=mate,
            ).start()

    def each_piece(todo, listed, of_end):
        for i, part in listed:

            @pl.when(jnp.logical_and(is_end if of_end else is_inner, ours[i] // 4 != side))
            def _():
                todo(i, part, ours[i], theirs[i])

    def lift_copy(i, part, src):
        ident = 2 * i + part
        return remote(
            lifted(src, part), lifted(src, part), lift_send.at[ident], lift_recv.at[ident], mp=mate
        )

    def core_copy(i, part, src):
        ident = 2 * i + part
        return remote(
            lifted(src, part), lifted(src, part), core_send.at[ident], core_recv.at[ident], dp=at_c
        )

    def hand_over(i, part, src, mirror):
        lift_copy(i, part, src).wait_recv()
        core_copy(i, part, src).start()

    ship(0, kw_ref, me, 0, at_x)
    ship(3, vw_ref, me, 1, at_y)
    ship(1, vw_ref, me, 1, at_x)
    ship(2, kw_ref, me, 0, at_y)
    ship(6, kw_ref, me, 0, at_c)
    ship(7, vw_ref, me, 1, at_c)
    lift(0, 0, kw_ref)
    lift(0, 1, vw_ref)
    own_k = pltpu.make_async_copy(kw_ref, land(me, 0), local_sem.at[1])
    own_v = pltpu.make_async_copy(vw_ref, land(me, 1), local_sem.at[2])
    own_k.start()
    own_v.start()
    tag_copies = []
    for d in range(1, n):
        to = (me + d) % n
        copy = remote(
            tags.at[to], arrived_tags.at[me], tag_send.at[d], tag_recv.at[d], dp=to
        )
        copy.start()
        tag_copies.append(copy)
    arrived_tags[me] = tags[me]
    own_k.wait()
    own_v.wait()
    load_enc.wait()

    def multiply(src, part, first=False):
        columns = pl.ds(pl.multiple_of(src * depth, depth), depth)

        @pl.loop(0, width // HD)
        def _(t):
            cols = pl.ds(pl.multiple_of(part * width + t * HD, HD), HD)
            product = jnp.dot(
                enc[:, columns], wts[src, :, cols], preferred_element_type=jnp.float32
            ).reshape(blocks, blk, HD)
            if first:
                acc[:, :, cols] = product
            else:
                acc[:, :, cols] += product

    multiply(me, 0, True)
    multiply(me, 1, True)
    landed(6, at_c, 0)
    multiply(at_c, 0)
    landed(7, at_c, 1)
    multiply(at_c, 1)
    landed(0, at_x, 0)
    ship(4, land(at_x, 0), at_x, 0, at_y)
    ship(8, land(at_x, 0), at_x, 0, at_c)
    lift(1, 0)
    landed(3, at_y, 1)
    ship(5, land(at_y, 1), at_y, 1, at_x)
    ship(11, land(at_y, 1), at_y, 1, at_c)
    lift(2, 1)
    multiply(at_x, 0)
    multiply(at_y, 1)
    landed(8, c_x, 0)
    multiply(c_x, 0)
    landed(11, c_y, 1)
    multiply(c_y, 1)
    landed(1, at_x, 1)
    ship(9, land(at_x, 1), at_x, 1, at_c)
    lift(1, 1)
    landed(2, at_y, 0)
    ship(10, land(at_y, 0), at_y, 0, at_c)
    lift(2, 0)
    multiply(at_x, 1)
    multiply(at_y, 0)
    landed(9, c_x, 1)
    multiply(c_x, 1)
    landed(10, c_y, 0)
    multiply(c_y, 0)
    landed(4, at_d, 0)
    ship(12, land(at_d, 0), at_d, 0, at_c)
    lift(3, 0)
    landed(5, at_d, 1)
    ship(13, land(at_d, 1), at_d, 1, at_c)
    lift(3, 1)
    multiply(at_d, 0)
    multiply(at_d, 1)
    landed(12, c_d, 0)
    multiply(c_d, 0)
    landed(13, c_d, 1)
    multiply(c_d, 1)

    def rows_of(slot):
        return pl.ds(pl.multiple_of(slot * blk, blk), blk)

    def slot_at(i):
        return bin_at(me, i)

    bins = [bins_ref[b] for b in range(blocks)]
    hole, turns = block_turns(me, n, bins_ref)

    def out_copy(h, i):
        to = slot_at(i)
        return remote(
            grads.at[h, :, rows_of(to), :],
            arrived.at[h, :, rows_of(me), :],
            out_send.at[h, i],
            out_recv.at[h, i],
            dp=to,
        )

    for h in range(heads):
        for i in [*range(1, n), 0]:
            to = slot_at(i)
            index = find(to, bins)
            for part in range(2):
                cols = pl.ds(part * width + h * HD, HD)
                picked = acc[index, :, cols].astype(bf16)
                if i == 0:
                    arrived[h, part, rows_of(me), :] = picked
                else:
                    grads[h, part, rows_of(to), :] = picked
            if i > 0:
                out_copy(h, i).start()

    each_piece(hand_over, pieces[:6], False)
    position = lax.broadcasted_iota(jnp.int32, (tokens, 1), 0)
    token_doc = jnp.zeros(position.shape, jnp.float32)
    doc_end = jnp.int32(0)
    for k in range(lengths_ref.shape[1]):
        doc_end = doc_end + lengths_ref[0, k]
        token_doc = token_doc + jnp.where(position >= doc_end, 1.0, 0.0)
    for copy in tag_copies:
        copy.wait()
    tag_row = jnp.concatenate([arrived_tags[s, 0:1, :] for s in range(n)], axis=1)
    live = tag_row == token_doc
    present = jnp.max(jnp.where(live, 1.0, 0.0), axis=1, keepdims=True) > 0.0
    scaling = HD ** (-0.5)
    for h in range(heads):
        for i in range(1, n):
            out_copy(h, i).wait()
        hk = pl.ds(h * HD, HD)
        q, g = q_ref[:, hk], g_ref[:, hk]
        scores = contract(q, arrived[h, 0], 1, 1) * scaling
        highest = jnp.max(jnp.where(live, scores, masked_value), axis=1, keepdims=True)
        highest = jnp.where(present, highest, 0.0)
        raised = jnp.exp(jnp.where(live, scores - highest, masked_value))
        totals = jnp.maximum(jnp.sum(raised, axis=1, keepdims=True), 1.0)
        attention = raised / totals
        rounded = attention.astype(bf16)
        grad_raw = contract(g, arrived[h, 1], 1, 1)
        deltas = jnp.sum(attention * grad_raw, axis=1, keepdims=True)
        score_grad = (attention * (grad_raw - deltas) * scaling).astype(bf16)
        grads[h, 0] = contract(score_grad, q, 0, 0).astype(bf16)
        grads[h, 1] = contract(rounded, g, 0, 0).astype(bf16)
        tsend[h, pl.ds(0, tokens), :] = rounded
        tsend[h, pl.ds(tokens, tokens), :] = score_grad
        if h == 0:
            each_piece(hand_over, pieces[6:], False)

    def back_copy(i):
        to = slot_at(i)
        return remote(
            grads.at[:, :, rows_of(to), :],
            ret.at[:, :, rows_of(me), :],
            back_send.at[i],
            back_recv.at[i],
            dp=to,
        )

    for i in range(1, n):
        back_copy(i).start()
    ret[:, :, rows_of(me), :] = grads[:, :, rows_of(me), :]
    for h in range(heads):
        hk = pl.ds(h * HD, HD)
        ctx_ref[:, hk] = jnp.dot(
            tsend[h, pl.ds(0, tokens), :], arrived[h, 1], preferred_element_type=jnp.float32
        ).astype(bf16)
        qg_ref[:, hk] = jnp.dot(
            tsend[h, pl.ds(tokens, tokens), :], arrived[h, 0], preferred_element_type=jnp.float32
        ).astype(bf16)

    def g_copy(r):
        return remote(own.at[r], gend.at[r], g_send.at[r], g_recv.at[r], mp=mate)

    half = blk // 2

    def half_rows(k):
        return pl.ds(pl.multiple_of(k * half, half), half)

    def first_g_copy(k):
        sem = k * blocks
        return remote(
            own.at[0, half_rows(k)], gend.at[0, half_rows(k)], g_send.at[sem], g_recv.at[sem], mp=mate
        )


    def first_mid_copy(way, k):
        sem = k * blocks
        return remote(
            msend.at[way, 0, half_rows(k)],
            mrecv.at[way, 0, half_rows(k)],
            mid_send.at[way, sem],
            mid_recv.at[way, sem],
            mp=across,
        )

    def mid_copy(way, r):
        return remote(
            msend.at[way, r], mrecv.at[way, r], mid_send.at[way, r], mid_recv.at[way, r], mp=across
        )

    def end_copy(r):
        return remote(mrecv.at[0, r], mrecv.at[0, r], end_send.at[r], end_recv.at[r], mp=mate)

    def prod_copy(r):
        return remote(msend.at[0, r], pend.at[r], prod_send.at[r], prod_recv.at[r], mp=mate)

    def pair_copy(i):
        return remote(tsend.at[i], trecv.at[i], pair_send.at[i], pair_recv.at[i], dp=at_c)

    def hop_copy(way, i, src):
        to = at_x if (way == 0) == (i < 2) else at_y
        return remote(src, hops.at[way, i], hop_send.at[way, i], hop_recv.at[way, i], dp=to)

    for i, part in pieces:

        @pl.when(jnp.logical_and(is_inner, theirs[i] // 4 != side))
        def _():
            core_copy(i, part, theirs[i]).wait_recv()

    def collect(r):
        back_copy_at = slot_at(r + 1)
        remote(
            ret.at[:, :, rows_of(back_copy_at), :],
            ret.at[:, :, rows_of(back_copy_at), :],
            back_send.at[r + 1],
            back_recv.at[r + 1],
            dp=at_c,
        ).wait_recv()
        later = hole <= r
        for h in range(heads):
            for part in range(2):
                own[r, :, pl.ds(part * width + h * HD, HD)] = jnp.where(
                    later,
                    ret[h, part, rows_of(back_copy_at), :],
                    ret[h, part, rows_of(slot_at(r)), :],
                )

        @pl.when(jnp.logical_and(is_end, r > 0))
        def _():
            g_copy(r).start()

    def own_weights(d, j):
        return wts[2 * d + j]

    def end_weights(d, j):
        return wend[(d % 2) * 2 + j]

    def shard_of(i, parity):
        flip_x, flip_y = 1 - i // 2, 1 - i % 2
        px = x + flip_x - 2 * x * flip_x
        py = y + flip_y - 2 * y * flip_y
        return place(py, px, parity)

    def term(shard, part, h):
        columns = pl.ds(pl.multiple_of(shard * depth, depth), depth)
        return contract(enc[:, columns], ret[h, part, pl.ds(0, rows), :], 0, 0).astype(bf16)

    def each_slab(todo):
        for part in range(2):
            for h in range(heads):
                todo(part, h, pl.ds(part * width + h * HD, HD))

    def half_cols(j):
        return pl.ds(pl.multiple_of(j * width, width), width)

    collect(0)

    @pl.when(is_end)
    def _():
        first_g_copy(0).start()
        first_g_copy(1).start()

    @pl.when(is_inner)
    def _():
        @pl.loop(0, 2)
        def _(k):
            first_g_copy(k).wait_recv()
            for way, dest in ((0, far_end), (1, across)):

                @pl.loop(0, 2)
                def _(j):
                    summed = contract(own[0, half_rows(k)], own_weights(dest, j), 1, 1)
                    summed += contract(gend[0, half_rows(k)], end_weights(dest, j), 1, 1)
                    msend[way, 0, half_rows(k), half_cols(j)] = summed.astype(bf16)

                first_mid_copy(way, k).start()

    @pl.loop(1, blocks)
    def _(r):
        @pl.when(r < 3)
        def _():
            collect(r)

        @pl.when(is_inner)
        def _():
            g_copy(r).wait_recv()
            for way, dest in ((0, far_end), (1, across)):

                @pl.loop(0, 2)
                def _(j):
                    summed = contract(own[r], own_weights(dest, j), 1, 1)
                    summed += contract(gend[r], end_weights(dest, j), 1, 1)
                    msend[way, r, :, half_cols(j)] = summed.astype(bf16)

                mid_copy(way, r).start()

        @pl.when(r == 2)
        def _():
            @pl.loop(3, blocks)
            def _(later):
                collect(later)

            for b in range(blocks):
                block = own[turns[b]]
                for h in range(heads):
                    for part in range(2):
                        first = part * width + h * HD
                        ret[h, part, pl.ds(b * blk, blk), :] = block[:, first : first + HD]

            @pl.loop(0, 4)
            def _(i):
                shard = shard_of(i, 1 - core)

                def fill(part, h, cols):
                    tsend[i, :, cols] = term(shard, part, h)

                each_slab(fill)
                pair_copy(i).start()

        @pl.when(r == 3)
        def _():
            @pl.loop(0, 4)
            def _(i):
                shard = shard_of(i, core)
                pair_copy(i).wait_recv()

                def fill(part, h, cols):
                    summed = term(shard, part, h).astype(jnp.float32)
                    summed += trecv[i, :, cols].astype(jnp.float32)
                    trecv[i, :, cols] = summed.astype(bf16)

                each_slab(fill)

                @pl.when(i == 1)
                def _():
                    hop_copy(0, 1, trecv.at[0, :, part_cols(0)]).start()
                    hop_copy(0, 0, trecv.at[1, :, part_cols(0)]).start()
                    hop_copy(1, 1, trecv.at[0, :, part_cols(1)]).start()

                @pl.when(i == 2)
                def _():
                    hop_copy(1, 0, trecv.at[2, :, part_cols(1)]).start()

    @pl.when(is_end)
    def _():
        @pl.loop(0, blocks)
        def _(r):
            @pl.loop(0, 2)
            def _(j):
                msend[0, r, :, half_cols(j)] = contract(own[r], own_weights(mate, j), 1, 1).astype(bf16)

            prod_copy(r).start()

    for way in range(2):
        hop_copy(way, 1, hops.at[way, 1]).wait_recv()
        summed = trecv[2 - way, :, part_cols(way)].astype(jnp.float32)
        summed += hops[way, 1].astype(jnp.float32)
        passed[way] = summed.astype(bf16)
        hop_copy(way, 2, passed.at[way]).start()

    total = acc.at[0]

    def wait_mid(way, r):
        @pl.when(r == 0)
        def _():
            first_mid_copy(way, 0).wait_recv()
            first_mid_copy(way, 1).wait_recv()

        @pl.when(r > 0)
        def _():
            mid_copy(way, r).wait_recv()

    def own_product(r, dest):
        @pl.loop(0, 2)
        def _(j):
            total[:, half_cols(j)] = contract(own[r], own_weights(dest, j), 1, 1)

    @pl.loop(0, blocks)
    def _(r):
        @pl.when(is_inner)
        def _():
            own_product(r, end)
            wait_mid(0, r)
            mrecv[0, r] = (total[...] + mrecv[0, r].astype(jnp.float32)).astype(bf16)
            end_copy(r).start()
            own_product(r, z)
            prod_copy(r).wait_recv()
            total[...] += pend[r].astype(jnp.float32)
            wait_mid(1, r)
            eg_ref[r] = (total[...] + mrecv[1, r].astype(jnp.float32)).astype(bf16)

        @pl.when(is_end)
        def _():
            own_product(r, z)
            end_copy(r).wait_recv()
            eg_ref[r] = (total[...] + mrecv[0, r].astype(jnp.float32)).astype(bf16)

        @pl.when(r == blocks - 2)
        def _():
            for way, out in ((0, kwg_ref), (1, vwg_ref)):
                hop_copy(way, 0, hops.at[way, 0]).wait_recv()
                hop_copy(way, 2, hops.at[way, 2]).wait_recv()
                summed = trecv[3, :, part_cols(way)].astype(jnp.float32)
                summed += hops[way, 0].astype(jnp.float32) + hops[way, 2].astype(jnp.float32)
                out[...] = summed.astype(bf16)

    for copy in started:
        copy.wait_send()
    each_piece(lambda i, part, src, mirror: lift_copy(i, part, src).wait_send(), pieces, True)
    each_piece(lambda i, part, src, mirror: core_copy(i, part, src).wait_send(), pieces, False)

    @pl.loop(0, blocks)
    def _(r):
        @pl.when(is_end)
        def _():
            prod_copy(r).wait_send()

            @pl.when(r > 0)
            def _():
                g_copy(r).wait_send()

        @pl.when(is_inner)
        def _():
            end_copy(r).wait_send()

            @pl.when(r > 0)
            def _():
                mid_copy(0, r).wait_send()
                mid_copy(1, r).wait_send()

    @pl.loop(0, 2)
    def _(k):
        @pl.when(is_end)
        def _():
            first_g_copy(k).wait_send()

        @pl.when(is_inner)
        def _():
            first_mid_copy(0, k).wait_send()
            first_mid_copy(1, k).wait_send()

    for i in range(1, n):
        back_copy(i).wait_send()
    for i in range(4):
        pair_copy(i).wait_send()
    for way in range(2):
        for i in range(3):
            hop_copy(way, i, hops.at[way, i]).wait_send()


def deliver_kernel(n, bins_ref, *refs):
    turns = block_turns(lax.axis_index("dp"), n, bins_ref)[1]
    count = (len(refs) - 2) // 3
    ins, outs = refs[:count], refs[count : 2 * count]
    held, (load_sem, store_sem) = refs[2 * count : 3 * count], refs[3 * count :]
    loads, stores = [], []
    for k in range(count):
        pieces = [(ins[k], held[k], outs[k])]
        if len(ins[k].shape) == 3:
            blocks, size, _ = ins[k].shape
            pieces = [
                (ins[k].at[turns[b]], held[k].at[b], outs[k].at[pl.ds(b * size, size), :])
                for b in range(blocks)
            ]
        for source, room, target in pieces:
            ident = len(loads)
            load = pltpu.make_async_copy(source, room, load_sem.at[ident])
            load.start()
            loads.append(load)
            stores.append(pltpu.make_async_copy(room, target, store_sem.at[ident]))
    for load, store in zip(loads, stores):
        load.wait()
        store.start()
    for store in stores:
        store.wait()


def deliver(n, bins, arrays):
    hbm = pl.BlockSpec(memory_space=pl.ANY)
    copies = sum(a.shape[0] if a.ndim == 3 else 1 for a in arrays)
    dma = pltpu.SemaphoreType.DMA((copies,))
    return pl.pallas_call(
        functools.partial(deliver_kernel, n),
        out_shape=tuple(
            jax.ShapeDtypeStruct((a.size // a.shape[-1], a.shape[-1]), a.dtype) for a in arrays
        ),
        in_specs=[pl.BlockSpec(memory_space=pltpu.SMEM)] + [hbm] * len(arrays),
        out_specs=(hbm,) * len(arrays),
        scratch_shapes=[pltpu.VMEM(a.shape, a.dtype) for a in arrays] + [dma, dma],
    )(bins, *arrays)


def per_device_cube(
    queries,
    context_grad,
    encoder_rows,
    key_weight,
    value_weight,
    document_lengths,
    block_bin,
    block_document,
):
    n, count = lax.axis_size("dp"), lax.axis_size("mp")
    rows, model = encoder_rows.shape
    depth, width = key_weight.shape
    heads = width // HD
    tokens = queries.shape[0]
    blocks = rows // BLK
    chips = n // 2
    vmem = pl.BlockSpec(memory_space=pltpu.VMEM)
    smem = pl.BlockSpec(memory_space=pltpu.SMEM)
    hbm = pl.BlockSpec(memory_space=pl.ANY)
    bf16 = jnp.bfloat16
    dma = pltpu.SemaphoreType.DMA
    shape = jax.ShapeDtypeStruct
    pairs = []
    for extent in [(14,), (8,), (8,), (n,), (heads, n), (n,), (n,), (2, n), (blocks,), (blocks,), (chips,), (2, 3)]:
        pairs += [dma(extent), dma(extent)]
    outs = pl.pallas_call(
        functools.partial(step_kernel, n, count),
        out_shape=(
            shape((tokens, width), bf16),
            shape((tokens, width), bf16),
            shape((blocks, BLK, model // count), bf16),
            shape((depth, width), bf16),
            shape((depth, width), bf16),
        ),
        in_specs=[vmem, vmem, hbm, vmem, vmem, smem, smem, smem],
        out_specs=(vmem,) * 5,
        scratch_shapes=[
            pltpu.VMEM((rows, model), bf16),
            pltpu.VMEM((n, depth, 2 * width), bf16),
            pltpu.VMEM((n // 2, depth, 2 * width), bf16),
            pltpu.VMEM((blocks, BLK, 2 * width), jnp.float32),
            pltpu.VMEM((heads, 2, n * BLK, HD), bf16),
            pltpu.VMEM((n, 8, BLK), jnp.float32),
            pltpu.VMEM((n, 8, BLK), jnp.float32),
            pltpu.VMEM((heads, 2, n * BLK, HD), bf16),
            pltpu.VMEM((heads, 2, n * BLK, HD), bf16),
            pltpu.VMEM((blocks, BLK, 2 * width), bf16),
            pltpu.VMEM((blocks, BLK, 2 * width), bf16),
            pltpu.VMEM((blocks, BLK, 2 * width), bf16),
            pltpu.VMEM((2, blocks, BLK, 2 * width), bf16),
            pltpu.VMEM((2, blocks, BLK, 2 * width), bf16),
            pltpu.VMEM((chips, depth, 2 * width), bf16),
            pltpu.VMEM((chips, depth, 2 * width), bf16),
            pltpu.VMEM((2, 3, depth, width), bf16),
            pltpu.VMEM((2, depth, width), bf16),
            dma((3,)),
            *pairs,
        ],
        compiler_params=pltpu.CompilerParams(
            collective_id=0, has_side_effects=True, vmem_limit_bytes=67043328
        ),
    )(
        queries,
        context_grad,
        encoder_rows,
        key_weight,
        value_weight,
        document_lengths,
        block_bin,
        block_document,
    )
    return deliver(n, block_bin, outs)


def solution(mesh):
    in_specs = (
        P("dp", "mp"),
        P("dp", "mp"),
        P("dp", None),
        P("dp", "mp"),
        P("dp", "mp"),
        P("dp", None),
        P("dp"),
        P("dp"),
    )
    out_specs = (P("dp", "mp"), P("dp", "mp"), P("dp", "mp"), P("dp", "mp"), P("dp", "mp"))
    cube = mesh.shape["dp"] == 2 * 2 * 2 and mesh.shape["mp"] == 2 * 2
    return jax.shard_map(
        per_device_cube if cube else per_device, mesh=mesh, in_specs=in_specs, out_specs=out_specs, check_vma=False
    )
```

```python
import functools

import jax
import jax.numpy as jnp
from jax import lax
from jax.experimental import pallas as pl
from jax.experimental.pallas import tpu as pltpu
from jax.sharding import PartitionSpec as P

HD = 256
BLK = 128


masked_value = -1e30


def attend_weights(scores, live_mask):
    present = jnp.any(live_mask, axis=1)[None, :, None]
    blocked = jnp.where(live_mask[None], scores, masked_value)
    highest = jnp.max(blocked, axis=2, keepdims=True)
    highest = jnp.where(present, highest, 0.0)
    raised = jnp.exp(jnp.where(live_mask[None], scores - highest, masked_value))
    totals = jnp.maximum(jnp.sum(raised, axis=2, keepdims=True), 1.0)
    return raised / totals


def token_documents(lengths, token_count):
    doc_ends = jnp.cumsum(lengths)
    positions = jnp.arange(token_count, dtype=jnp.int32)
    return jnp.sum((doc_ends[None, :] <= positions[:, None]).astype(jnp.int32), axis=1)


def per_device(
    queries,
    context_grad,
    encoder_rows,
    key_weight,
    value_weight,
    document_lengths,
    block_bin,
    block_document,
):
    bin_count = lax.axis_size("dp")
    full_key, full_value = (
        lax.all_gather(key_weight, "dp", axis=0, tiled=True),
        lax.all_gather(value_weight, "dp", axis=0, tiled=True),
    )
    head_width = full_key.shape[1]
    head_count = head_width // HD
    block_rows = BLK
    blocks_here = block_bin.shape[0]
    both_weights = jnp.concatenate([full_key, full_value], axis=1)
    projected = jnp.dot(encoder_rows, both_weights, preferred_element_type=jnp.float32).astype(
        jnp.bfloat16
    )
    route_table = (block_bin[:, None] == jnp.arange(bin_count, dtype=jnp.int32)[None, :]).astype(
        jnp.bfloat16
    )
    flat_blocks = projected.reshape(blocks_here, block_rows * 2 * head_width)
    outbound = lax.dot_general(
        route_table, flat_blocks, (((0,), (0,)), ((), ())), preferred_element_type=jnp.float32
    )
    outbound = outbound.astype(jnp.bfloat16).reshape(bin_count, block_rows, 2 * head_width)
    slot_docs = (
        lax.dot_general(
            route_table.astype(jnp.float32),
            (block_document + 1).astype(jnp.float32),
            (((0,), (0,)), ((), ())),
        )
        - 1.0
    )
    tag_rows = jnp.broadcast_to(slot_docs[:, None], (bin_count, block_rows)).astype(jnp.bfloat16)
    arrived, arrived_tags = (
        lax.all_to_all(outbound, "dp", split_axis=0, concat_axis=0, tiled=True),
        lax.all_to_all(tag_rows, "dp", split_axis=0, concat_axis=0, tiled=True),
    )
    key_slots = arrived[:, :, :head_width].reshape(bin_count * block_rows, head_count, HD)
    value_slots = arrived[:, :, head_width:].reshape(bin_count * block_rows, head_count, HD)
    token_count = queries.shape[0]
    token_docs = token_documents(document_lengths[0], token_count).astype(jnp.float32)
    live_mask = arrived_tags.reshape(-1).astype(jnp.float32)[None, :] == token_docs[:, None]
    query_heads = queries.reshape(token_count, head_count, HD)
    grad_heads = context_grad.reshape(token_count, head_count, HD)
    scaling = HD ** (-0.5)
    scores = (
        jnp.einsum("thd,shd->hts", query_heads, key_slots, preferred_element_type=jnp.float32)
        * scaling
    )
    attention = attend_weights(scores, live_mask)
    rounded = attention.astype(jnp.bfloat16)
    context = jnp.einsum(
        "hts,shd->thd", rounded, value_slots, preferred_element_type=jnp.float32
    ).astype(jnp.bfloat16)
    grad_raw = jnp.einsum(
        "thd,shd->hts", grad_heads, value_slots, preferred_element_type=jnp.float32
    )
    deltas = jnp.sum(attention * grad_raw, axis=2, keepdims=True)
    score_grad = (attention * (grad_raw - deltas) * scaling).astype(jnp.bfloat16)
    query_grad = jnp.einsum(
        "hts,shd->thd", score_grad, key_slots, preferred_element_type=jnp.float32
    ).astype(jnp.bfloat16)
    key_grad = jnp.einsum(
        "hts,thd->shd", score_grad, query_heads, preferred_element_type=jnp.float32
    ).astype(jnp.bfloat16)
    value_grad = jnp.einsum(
        "hts,thd->shd", rounded, grad_heads, preferred_element_type=jnp.float32
    ).astype(jnp.bfloat16)
    slot_grads = jnp.concatenate(
        [
            key_grad.reshape(bin_count, block_rows, head_width),
            value_grad.reshape(bin_count, block_rows, head_width),
        ],
        axis=2,
    )
    returned = lax.all_to_all(slot_grads, "dp", split_axis=0, concat_axis=0, tiled=True)
    own_grads = jnp.dot(
        route_table,
        returned.reshape(bin_count, block_rows * 2 * head_width),
        preferred_element_type=jnp.float32,
    )
    own_grads = own_grads.astype(jnp.bfloat16).reshape(encoder_rows.shape[0], 2 * head_width)
    weight_terms = lax.dot_general(
        encoder_rows, own_grads, (((0,), (0,)), ((), ())), preferred_element_type=jnp.float32
    )
    weight_sums = lax.psum_scatter(
        weight_terms.astype(jnp.bfloat16), "dp", scatter_dimension=0, tiled=True
    ).astype(jnp.float32)
    key_weight_grad = weight_sums[:, :head_width].astype(jnp.bfloat16)
    value_weight_grad = weight_sums[:, head_width:].astype(jnp.bfloat16)
    row_terms = lax.dot_general(
        own_grads, both_weights, (((1,), (1,)), ((), ())), preferred_element_type=jnp.float32
    )
    encoder_grad = lax.psum_scatter(
        row_terms.astype(jnp.bfloat16), "mp", scatter_dimension=1, tiled=True
    )
    return (
        context.reshape(token_count, head_width),
        query_grad.reshape(token_count, head_width),
        encoder_grad,
        key_weight_grad,
        value_weight_grad,
    )


MESH = pl.DeviceIdType.MESH


def contract(a, b, dim_a, dim_b):
    return lax.dot_general(
        a, b, (((dim_a,), (dim_b,)), ((), ())), preferred_element_type=jnp.float32
    )


def bin_at(me, i):
    def flip(bit, turned):
        return bit + turned - 2 * bit * turned

    core, x, y = me % 2, (me // 2) % 2, me // 4
    return (flip(y, i // 4) * 2 + flip(x, (i // 2) % 2)) * 2 + flip(core, i % 2)


def find(value, options):
    index = jnp.int32(0)
    for k, option in enumerate(options):
        index = jnp.where(option == value, k, index)
    return index


def block_turns(me, n, bins_ref):
    bins = [bins_ref[b] for b in range(bins_ref.shape[0])]
    order = [bin_at(me, i) for i in range(n)]
    hole = find(n * (n - 1) // 2 - sum(bins), order)
    places = [find(b, order) for b in bins]
    return hole, [jnp.where(p > hole, p - 1, p) for p in places]


def step_kernel(
    n,
    count,
    q_ref,
    g_ref,
    enc_hbm,
    kw_ref,
    vw_ref,
    lengths_ref,
    bins_ref,
    docs_ref,
    ctx_ref,
    qg_ref,
    eg_ref,
    kwg_ref,
    vwg_ref,
    enc,
    wts,
    wend,
    acc,
    arrived,
    tags,
    arrived_tags,
    grads,
    ret,
    own,
    gend,
    pend,
    msend,
    mrecv,
    tsend,
    trecv,
    hops,
    passed,
    local_sem,
    gather_send,
    gather_recv,
    lift_send,
    lift_recv,
    core_send,
    core_recv,
    tag_send,
    tag_recv,
    out_send,
    out_recv,
    back_send,
    back_recv,
    g_send,
    g_recv,
    mid_send,
    mid_recv,
    end_send,
    end_recv,
    prod_send,
    prod_recv,
    pair_send,
    pair_recv,
    hop_send,
    hop_recv,
):
    bf16 = jnp.bfloat16
    me, z = lax.axis_index("dp"), lax.axis_index("mp")
    core = me % 2
    x = (me // 2) % 2
    y = me // 4

    def place(py, px, pc):
        return (py * 2 + px) * 2 + pc

    at_x, at_y = place(y, 1 - x, core), place(1 - y, x, core)
    at_c, at_d = place(y, x, 1 - core), place(1 - y, 1 - x, core)
    c_x, c_y = place(y, 1 - x, 1 - core), place(1 - y, x, 1 - core)
    c_d = place(1 - y, 1 - x, 1 - core)
    depth, width = kw_ref.shape
    rows = enc.shape[0]
    blocks = rows // BLK
    blk = BLK
    heads = width // HD
    tokens = q_ref.shape[0]
    last = count - 1
    end = (z // 2) * last
    far_end = last - end
    side = z // 2
    is_end = z == end
    is_inner = z != end
    mate = z + 1 - 2 * (z % 2)
    across = last - z

    def remote(src, dst, send, recv, **device):
        return pltpu.make_async_remote_copy(
            src_ref=src,
            dst_ref=dst,
            send_sem=send,
            recv_sem=recv,
            device_id=device,
            device_id_type=MESH,
        )

    load_enc = pltpu.make_async_copy(enc_hbm, enc, local_sem.at[0])
    load_enc.start()
    barrier = pltpu.get_barrier_semaphore()
    for d in range(1, n):
        pl.semaphore_signal(
            barrier, inc=1, device_id={"dp": (me + d) % n}, device_id_type=MESH
        )
    pl.semaphore_signal(barrier, inc=1, device_id={"mp": mate}, device_id_type=MESH)

    @pl.when(is_inner)
    def _():
        pl.semaphore_signal(barrier, inc=1, device_id={"mp": across}, device_id_type=MESH)


    for d in range(n):
        to = (me + d) % n
        doc = jnp.int32(-1)
        for b in range(blocks):
            doc = jnp.where(bins_ref[b] == to, docs_ref[b], doc)
        tags[to] = jnp.full(tags.shape[1:], doc.astype(jnp.float32), jnp.float32)
    pl.semaphore_wait(barrier, n + (z + 1) // 2 % 2)

    def part_cols(part):
        return pl.ds(part * width, width)

    def head_cols(part, h):
        return pl.ds(pl.multiple_of(part * width + h * HD, HD), HD)

    def land(src, part, h):
        return wts.at[src, :, head_cols(part, h)]

    started = []

    def ship(h, ident, ref, src, part, to):
        copy = remote(
            ref, land(src, part, h), gather_send.at[h, ident], gather_recv.at[h, ident], dp=to
        )
        copy.start()
        started.append(copy)

    def landed(h, ident, src, part):
        remote(
            land(src, part, h),
            land(src, part, h),
            gather_send.at[h, ident],
            gather_recv.at[h, ident],
            dp=at_c,
        ).wait_recv()

    def lifted(src, part, h):
        return wend.at[src % 4, :, head_cols(part, h)]

    ours, theirs = (me, at_x, at_y, at_d), (at_c, c_x, c_y, c_d)
    early = [(0, 0, 0), (0, 1, 0), (0, 0, 1), (0, 1, 1), (1, 0, 0), (2, 1, 0), (1, 1, 0), (2, 0, 0)]
    early += [(3, 0, 0), (3, 1, 0), (1, 0, 1), (2, 1, 1), (1, 1, 1), (2, 0, 1)]
    late = [(3, 0, 1), (3, 1, 1)]
    pieces = early + late

    def lift(i, part, h, ref=None):
        src = ours[i]
        ident = 4 * i + 2 * part + h

        @pl.when(jnp.logical_and(is_end, src // 4 != side))
        def _():
            remote(
                land(src, part, h) if ref is None else ref,
                lifted(src, part, h),
                lift_send.at[ident],
                lift_recv.at[ident],
                mp=mate,
            ).start()

    def each_piece(todo, listed, of_end):
        for i, part, h in listed:

            @pl.when(jnp.logical_and(is_end if of_end else is_inner, ours[i] // 4 != side))
            def _():
                todo(i, part, h, ours[i])

    def lift_copy(i, part, h, src):
        ident = 4 * i + 2 * part + h
        ref = lifted(src, part, h)
        return remote(ref, ref, lift_send.at[ident], lift_recv.at[ident], mp=mate)

    def core_copy(i, part, h, src):
        ident = 4 * i + 2 * part + h
        ref = lifted(src, part, h)
        return remote(ref, ref, core_send.at[ident], core_recv.at[ident], dp=at_c)

    def hand_over(i, part, h, src):
        lift_copy(i, part, h, src).wait_recv()
        core_copy(i, part, h, src).start()

    def ship_own(h):
        cols = pl.ds(h * HD, HD)
        kw, vw = kw_ref.at[:, cols], vw_ref.at[:, cols]
        ship(h, 0, kw, me, 0, at_x)
        ship(h, 3, vw, me, 1, at_y)
        ship(h, 1, vw, me, 1, at_x)
        ship(h, 2, kw, me, 0, at_y)
        ship(h, 6, kw, me, 0, at_c)
        ship(h, 7, vw, me, 1, at_c)
        lift(0, 0, h, kw)
        lift(0, 1, h, vw)

    ship_own(0)
    own_k = pltpu.make_async_copy(kw_ref, wts.at[me, :, part_cols(0)], local_sem.at[1])
    own_v = pltpu.make_async_copy(vw_ref, wts.at[me, :, part_cols(1)], local_sem.at[2])
    own_k.start()
    own_v.start()
    tag_copies = []
    for d in range(1, n):
        to = (me + d) % n
        copy = remote(
            tags.at[to], arrived_tags.at[me], tag_send.at[d], tag_recv.at[d], dp=to
        )
        copy.start()
        tag_copies.append(copy)
    arrived_tags[me] = tags[me]
    own_k.wait()
    own_v.wait()
    load_enc.wait()

    def multiply(h, first_src, second_src, swap=0, fresh=False):
        @pl.loop(0, 2)
        def _(t):
            src = first_src + t * (second_src - first_src)
            columns = pl.ds(pl.multiple_of(src * depth, depth), depth)
            cols = head_cols(t + swap - 2 * t * swap, h)
            product = jnp.dot(
                enc[:, columns], wts[src, :, cols], preferred_element_type=jnp.float32
            ).reshape(blocks, blk, HD)
            if fresh:
                acc[:, :, cols] = product
            else:
                acc[:, :, cols] += product

    def gather(h, when_passed):
        multiply(h, me, me, fresh=True)
        landed(h, 6, at_c, 0)
        landed(h, 7, at_c, 1)
        multiply(h, at_c, at_c)
        landed(h, 0, at_x, 0)
        ship(h, 4, land(at_x, 0, h), at_x, 0, at_y)
        ship(h, 8, land(at_x, 0, h), at_x, 0, at_c)
        lift(1, 0, h)
        landed(h, 3, at_y, 1)
        ship(h, 5, land(at_y, 1, h), at_y, 1, at_x)
        ship(h, 11, land(at_y, 1, h), at_y, 1, at_c)
        lift(2, 1, h)
        when_passed()
        multiply(h, at_x, at_y)
        landed(h, 8, c_x, 0)
        landed(h, 11, c_y, 1)
        multiply(h, c_x, c_y)
        landed(h, 1, at_x, 1)
        ship(h, 9, land(at_x, 1, h), at_x, 1, at_c)
        lift(1, 1, h)
        landed(h, 2, at_y, 0)
        ship(h, 10, land(at_y, 0, h), at_y, 0, at_c)
        lift(2, 0, h)
        multiply(h, at_y, at_x)
        landed(h, 9, c_x, 1)
        landed(h, 10, c_y, 0)
        multiply(h, c_y, c_x)
        landed(h, 4, at_d, 0)
        ship(h, 12, land(at_d, 0, h), at_d, 0, at_c)
        lift(3, 0, h)
        landed(h, 5, at_d, 1)
        ship(h, 13, land(at_d, 1, h), at_d, 1, at_c)
        lift(3, 1, h)
        multiply(h, at_d, at_d)
        landed(h, 12, c_d, 0)
        landed(h, 13, c_d, 1)
        multiply(h, c_d, c_d)

    def rows_of(slot):
        return pl.ds(pl.multiple_of(slot * blk, blk), blk)

    def slot_at(i):
        return bin_at(me, i)

    bins = [bins_ref[b] for b in range(blocks)]
    hole, turns = block_turns(me, n, bins_ref)

    def out_copy(h, i):
        to = slot_at(i)
        return remote(
            grads.at[h, :, rows_of(to), :],
            arrived.at[h, :, rows_of(me), :],
            out_send.at[h, i],
            out_recv.at[h, i],
            dp=to,
        )

    def send_slots(h):
        for i in [*range(1, n), 0]:
            to = slot_at(i)
            index = find(to, bins)
            for part in range(2):
                cols = pl.ds(part * width + h * HD, HD)
                picked = acc[index, :, cols].astype(bf16)
                if i == 0:
                    arrived[h, part, rows_of(me), :] = picked
                else:
                    grads[h, part, rows_of(to), :] = picked
            if i > 0:
                out_copy(h, i).start()

    gather(0, lambda: ship_own(1))
    gather(1, lambda: send_slots(0))
    send_slots(1)
    each_piece(hand_over, early, False)
    position = lax.broadcasted_iota(jnp.int32, (tokens, 1), 0)
    token_doc = jnp.zeros(position.shape, jnp.float32)
    doc_end = jnp.int32(0)
    for k in range(lengths_ref.shape[1]):
        doc_end = doc_end + lengths_ref[0, k]
        token_doc = token_doc + jnp.where(position >= doc_end, 1.0, 0.0)
    for copy in tag_copies:
        copy.wait()
    tag_row = jnp.concatenate([arrived_tags[s, 0:1, :] for s in range(n)], axis=1)
    live = tag_row == token_doc
    present = jnp.max(jnp.where(live, 1.0, 0.0), axis=1, keepdims=True) > 0.0
    scaling = HD ** (-0.5)
    for h in range(heads):
        for i in range(1, n):
            out_copy(h, i).wait()
        hk = pl.ds(h * HD, HD)
        q, g = q_ref[:, hk], g_ref[:, hk]
        scores = contract(q, arrived[h, 0], 1, 1) * scaling
        highest = jnp.max(jnp.where(live, scores, masked_value), axis=1, keepdims=True)
        highest = jnp.where(present, highest, 0.0)
        raised = jnp.exp(jnp.where(live, scores - highest, masked_value))
        totals = jnp.maximum(jnp.sum(raised, axis=1, keepdims=True), 1.0)
        attention = raised / totals
        rounded = attention.astype(bf16)
        grad_raw = contract(g, arrived[h, 1], 1, 1)
        deltas = jnp.sum(attention * grad_raw, axis=1, keepdims=True)
        score_grad = (attention * (grad_raw - deltas) * scaling).astype(bf16)
        grads[h, 0] = contract(score_grad, q, 0, 0).astype(bf16)
        grads[h, 1] = contract(rounded, g, 0, 0).astype(bf16)
        tsend[h, pl.ds(0, tokens), :] = rounded
        tsend[h, pl.ds(tokens, tokens), :] = score_grad
        if h == 0:
            each_piece(hand_over, late, False)

    def back_copy(i):
        to = slot_at(i)
        return remote(
            grads.at[:, :, rows_of(to), :],
            ret.at[:, :, rows_of(me), :],
            back_send.at[i],
            back_recv.at[i],
            dp=to,
        )

    for i in range(1, n):
        back_copy(i).start()
    ret[:, :, rows_of(me), :] = grads[:, :, rows_of(me), :]
    for h in range(heads):
        hk = pl.ds(h * HD, HD)
        ctx_ref[:, hk] = jnp.dot(
            tsend[h, pl.ds(0, tokens), :], arrived[h, 1], preferred_element_type=jnp.float32
        ).astype(bf16)
        qg_ref[:, hk] = jnp.dot(
            tsend[h, pl.ds(tokens, tokens), :], arrived[h, 0], preferred_element_type=jnp.float32
        ).astype(bf16)

    def g_copy(r):
        return remote(own.at[r], gend.at[r], g_send.at[r], g_recv.at[r], mp=mate)

    half = blk // 2

    def half_rows(k):
        return pl.ds(pl.multiple_of(k * half, half), half)

    def first_g_copy(k):
        sem = k * blocks
        return remote(
            own.at[0, half_rows(k)], gend.at[0, half_rows(k)], g_send.at[sem], g_recv.at[sem], mp=mate
        )


    def first_mid_copy(way, k):
        sem = k * blocks
        return remote(
            msend.at[way, 0, half_rows(k)],
            mrecv.at[way, 0, half_rows(k)],
            mid_send.at[way, sem],
            mid_recv.at[way, sem],
            mp=across,
        )

    def mid_copy(way, r):
        return remote(
            msend.at[way, r], mrecv.at[way, r], mid_send.at[way, r], mid_recv.at[way, r], mp=across
        )

    def end_copy(r):
        return remote(mrecv.at[0, r], mrecv.at[0, r], end_send.at[r], end_recv.at[r], mp=mate)

    def prod_copy(r):
        return remote(msend.at[0, r], pend.at[r], prod_send.at[r], prod_recv.at[r], mp=mate)

    def pair_copy(i):
        return remote(tsend.at[i], trecv.at[i], pair_send.at[i], pair_recv.at[i], dp=at_c)

    def hop_copy(way, i, src):
        to = at_x if (way == 0) == (i < 2) else at_y
        return remote(src, hops.at[way, i], hop_send.at[way, i], hop_recv.at[way, i], dp=to)

    for i, part, h in pieces:

        @pl.when(jnp.logical_and(is_inner, theirs[i] // 4 != side))
        def _():
            core_copy(i, part, h, theirs[i]).wait_recv()

    def collect(r):
        back_copy_at = slot_at(r + 1)
        remote(
            ret.at[:, :, rows_of(back_copy_at), :],
            ret.at[:, :, rows_of(back_copy_at), :],
            back_send.at[r + 1],
            back_recv.at[r + 1],
            dp=at_c,
        ).wait_recv()
        later = hole <= r
        for h in range(heads):
            for part in range(2):
                own[r, :, pl.ds(part * width + h * HD, HD)] = jnp.where(
                    later,
                    ret[h, part, rows_of(back_copy_at), :],
                    ret[h, part, rows_of(slot_at(r)), :],
                )

        @pl.when(jnp.logical_and(is_end, r > 0))
        def _():
            g_copy(r).start()

    def own_weights(d, j):
        return wts[2 * d + j]

    def end_weights(d, j):
        return wend[(d % 2) * 2 + j]

    def shard_of(i, parity):
        flip_x, flip_y = 1 - i // 2, 1 - i % 2
        px = x + flip_x - 2 * x * flip_x
        py = y + flip_y - 2 * y * flip_y
        return place(py, px, parity)

    def term(shard, part, h):
        columns = pl.ds(pl.multiple_of(shard * depth, depth), depth)
        return contract(enc[:, columns], ret[h, part, pl.ds(0, rows), :], 0, 0).astype(bf16)

    def each_slab(todo):
        for part in range(2):
            for h in range(heads):
                todo(part, h, pl.ds(part * width + h * HD, HD))

    def half_cols(j):
        return pl.ds(pl.multiple_of(j * width, width), width)

    collect(0)

    @pl.when(is_end)
    def _():
        first_g_copy(0).start()
        first_g_copy(1).start()

    @pl.when(is_inner)
    def _():
        @pl.loop(0, 2)
        def _(k):
            first_g_copy(k).wait_recv()
            for way, dest in ((0, far_end), (1, across)):

                @pl.loop(0, 2)
                def _(j):
                    summed = contract(own[0, half_rows(k)], own_weights(dest, j), 1, 1)
                    summed += contract(gend[0, half_rows(k)], end_weights(dest, j), 1, 1)
                    msend[way, 0, half_rows(k), half_cols(j)] = summed.astype(bf16)

                first_mid_copy(way, k).start()

    def send_across(way, r):
        dest = across if way else far_end

        @pl.loop(0, 2)
        def _(j):
            summed = contract(own[r], own_weights(dest, j), 1, 1)
            summed += contract(gend[r], end_weights(dest, j), 1, 1)
            msend[way, r, :, half_cols(j)] = summed.astype(bf16)

        mid_copy(way, r).start()

    @pl.loop(1, blocks)
    def _(r):
        @pl.when(r < 3)
        def _():
            collect(r)

        @pl.when(is_inner)
        def _():
            g_copy(r).wait_recv()
            send_across(0, r)

            @pl.when(r > 1)
            def _():
                send_across(1, r - 1)

        @pl.when(r == 2)
        def _():
            @pl.loop(3, blocks)
            def _(later):
                collect(later)

            for b in range(blocks):
                block = own[turns[b]]
                for h in range(heads):
                    for part in range(2):
                        first = part * width + h * HD
                        ret[h, part, pl.ds(b * blk, blk), :] = block[:, first : first + HD]

            @pl.loop(0, 4)
            def _(i):
                shard = shard_of(i, 1 - core)

                def fill(part, h, cols):
                    tsend[i, :, cols] = term(shard, part, h)

                each_slab(fill)
                pair_copy(i).start()

        @pl.when(r == 3)
        def _():
            @pl.loop(0, 4)
            def _(i):
                shard = shard_of(i, core)
                pair_copy(i).wait_recv()

                def fill(part, h, cols):
                    summed = term(shard, part, h).astype(jnp.float32)
                    summed += trecv[i, :, cols].astype(jnp.float32)
                    trecv[i, :, cols] = summed.astype(bf16)

                each_slab(fill)

                @pl.when(i == 1)
                def _():
                    hop_copy(0, 1, trecv.at[0, :, part_cols(0)]).start()
                    hop_copy(0, 0, trecv.at[1, :, part_cols(0)]).start()
                    hop_copy(1, 1, trecv.at[0, :, part_cols(1)]).start()

                @pl.when(i == 2)
                def _():
                    hop_copy(1, 0, trecv.at[2, :, part_cols(1)]).start()

    @pl.when(is_end)
    def _():
        @pl.loop(0, blocks)
        def _(r):
            @pl.loop(0, 2)
            def _(j):
                msend[0, r, :, half_cols(j)] = contract(own[r], own_weights(mate, j), 1, 1).astype(bf16)

            prod_copy(r).start()

    @pl.when(is_inner)
    def _():
        send_across(1, blocks - 1)

    for way in range(2):
        hop_copy(way, 1, hops.at[way, 1]).wait_recv()
        summed = trecv[2 - way, :, part_cols(way)].astype(jnp.float32)
        summed += hops[way, 1].astype(jnp.float32)
        passed[way] = summed.astype(bf16)
        hop_copy(way, 2, passed.at[way]).start()

    total = acc.at[0]

    def wait_mid(way, r):
        @pl.when(r == 0)
        def _():
            first_mid_copy(way, 0).wait_recv()
            first_mid_copy(way, 1).wait_recv()

        @pl.when(r > 0)
        def _():
            mid_copy(way, r).wait_recv()

    def own_product(r, dest):
        @pl.loop(0, 2)
        def _(j):
            total[:, half_cols(j)] = contract(own[r], own_weights(dest, j), 1, 1)

    @pl.loop(0, blocks)
    def _(r):
        @pl.when(is_inner)
        def _():
            own_product(r, end)
            wait_mid(0, r)
            mrecv[0, r] = (total[...] + mrecv[0, r].astype(jnp.float32)).astype(bf16)
            end_copy(r).start()
            own_product(r, z)
            prod_copy(r).wait_recv()
            total[...] += pend[r].astype(jnp.float32)
            wait_mid(1, r)
            eg_ref[r] = (total[...] + mrecv[1, r].astype(jnp.float32)).astype(bf16)

        @pl.when(is_end)
        def _():
            own_product(r, z)
            end_copy(r).wait_recv()
            eg_ref[r] = (total[...] + mrecv[0, r].astype(jnp.float32)).astype(bf16)

        @pl.when(r == blocks - 2)
        def _():
            for way, out in ((0, kwg_ref), (1, vwg_ref)):
                hop_copy(way, 0, hops.at[way, 0]).wait_recv()
                hop_copy(way, 2, hops.at[way, 2]).wait_recv()
                summed = trecv[3, :, part_cols(way)].astype(jnp.float32)
                summed += hops[way, 0].astype(jnp.float32) + hops[way, 2].astype(jnp.float32)
                out[...] = summed.astype(bf16)

    for copy in started:
        copy.wait_send()
    each_piece(lambda *piece: lift_copy(*piece).wait_send(), pieces, True)
    each_piece(lambda *piece: core_copy(*piece).wait_send(), pieces, False)

    @pl.loop(0, blocks)
    def _(r):
        @pl.when(is_end)
        def _():
            prod_copy(r).wait_send()

            @pl.when(r > 0)
            def _():
                g_copy(r).wait_send()

        @pl.when(is_inner)
        def _():
            end_copy(r).wait_send()

            @pl.when(r > 0)
            def _():
                mid_copy(0, r).wait_send()
                mid_copy(1, r).wait_send()

    @pl.loop(0, 2)
    def _(k):
        @pl.when(is_end)
        def _():
            first_g_copy(k).wait_send()

        @pl.when(is_inner)
        def _():
            first_mid_copy(0, k).wait_send()
            first_mid_copy(1, k).wait_send()

    for i in range(1, n):
        back_copy(i).wait_send()
    for i in range(4):
        pair_copy(i).wait_send()
    for way in range(2):
        for i in range(3):
            hop_copy(way, i, hops.at[way, i]).wait_send()


def deliver_kernel(n, bins_ref, *refs):
    turns = block_turns(lax.axis_index("dp"), n, bins_ref)[1]
    count = (len(refs) - 2) // 3
    ins, outs = refs[:count], refs[count : 2 * count]
    held, (load_sem, store_sem) = refs[2 * count : 3 * count], refs[3 * count :]
    loads, stores = [], []
    for k in range(count):
        pieces = [(ins[k], held[k], outs[k])]
        if len(ins[k].shape) == 3:
            blocks, size, _ = ins[k].shape
            pieces = [
                (ins[k].at[turns[b]], held[k].at[b], outs[k].at[pl.ds(b * size, size), :])
                for b in range(blocks)
            ]
        for source, room, target in pieces:
            ident = len(loads)
            load = pltpu.make_async_copy(source, room, load_sem.at[ident])
            load.start()
            loads.append(load)
            stores.append(pltpu.make_async_copy(room, target, store_sem.at[ident]))
    for load, store in zip(loads, stores):
        load.wait()
        store.start()
    for store in stores:
        store.wait()


def deliver(n, bins, arrays):
    hbm = pl.BlockSpec(memory_space=pl.ANY)
    copies = sum(a.shape[0] if a.ndim == 3 else 1 for a in arrays)
    dma = pltpu.SemaphoreType.DMA((copies,))
    return pl.pallas_call(
        functools.partial(deliver_kernel, n),
        out_shape=tuple(
            jax.ShapeDtypeStruct((a.size // a.shape[-1], a.shape[-1]), a.dtype) for a in arrays
        ),
        in_specs=[pl.BlockSpec(memory_space=pltpu.SMEM)] + [hbm] * len(arrays),
        out_specs=(hbm,) * len(arrays),
        scratch_shapes=[pltpu.VMEM(a.shape, a.dtype) for a in arrays] + [dma, dma],
    )(bins, *arrays)


def per_device_cube(
    queries,
    context_grad,
    encoder_rows,
    key_weight,
    value_weight,
    document_lengths,
    block_bin,
    block_document,
):
    n, count = lax.axis_size("dp"), lax.axis_size("mp")
    rows, model = encoder_rows.shape
    depth, width = key_weight.shape
    heads = width // HD
    tokens = queries.shape[0]
    blocks = rows // BLK
    chips = n // 2
    vmem = pl.BlockSpec(memory_space=pltpu.VMEM)
    smem = pl.BlockSpec(memory_space=pltpu.SMEM)
    hbm = pl.BlockSpec(memory_space=pl.ANY)
    bf16 = jnp.bfloat16
    dma = pltpu.SemaphoreType.DMA
    shape = jax.ShapeDtypeStruct
    pairs = []
    for extent in [(heads, 14), (16,), (16,), (n,), (heads, n), (n,), (n,), (2, n), (blocks,), (blocks,), (chips,), (2, 3)]:
        pairs += [dma(extent), dma(extent)]
    outs = pl.pallas_call(
        functools.partial(step_kernel, n, count),
        out_shape=(
            shape((tokens, width), bf16),
            shape((tokens, width), bf16),
            shape((blocks, BLK, model // count), bf16),
            shape((depth, width), bf16),
            shape((depth, width), bf16),
        ),
        in_specs=[vmem, vmem, hbm, vmem, vmem, smem, smem, smem],
        out_specs=(vmem,) * 5,
        scratch_shapes=[
            pltpu.VMEM((rows, model), bf16),
            pltpu.VMEM((n, depth, 2 * width), bf16),
            pltpu.VMEM((n // 2, depth, 2 * width), bf16),
            pltpu.VMEM((blocks, BLK, 2 * width), jnp.float32),
            pltpu.VMEM((heads, 2, n * BLK, HD), bf16),
            pltpu.VMEM((n, 8, BLK), jnp.float32),
            pltpu.VMEM((n, 8, BLK), jnp.float32),
            pltpu.VMEM((heads, 2, n * BLK, HD), bf16),
            pltpu.VMEM((heads, 2, n * BLK, HD), bf16),
            pltpu.VMEM((blocks, BLK, 2 * width), bf16),
            pltpu.VMEM((blocks, BLK, 2 * width), bf16),
            pltpu.VMEM((blocks, BLK, 2 * width), bf16),
            pltpu.VMEM((2, blocks, BLK, 2 * width), bf16),
            pltpu.VMEM((2, blocks, BLK, 2 * width), bf16),
            pltpu.VMEM((chips, depth, 2 * width), bf16),
            pltpu.VMEM((chips, depth, 2 * width), bf16),
            pltpu.VMEM((2, 3, depth, width), bf16),
            pltpu.VMEM((2, depth, width), bf16),
            dma((3,)),
            *pairs,
        ],
        compiler_params=pltpu.CompilerParams(
            collective_id=0, has_side_effects=True, vmem_limit_bytes=67043328
        ),
    )(
        queries,
        context_grad,
        encoder_rows,
        key_weight,
        value_weight,
        document_lengths,
        block_bin,
        block_document,
    )
    return deliver(n, block_bin, outs)


def solution(mesh):
    in_specs = (
        P("dp", "mp"),
        P("dp", "mp"),
        P("dp", None),
        P("dp", "mp"),
        P("dp", "mp"),
        P("dp", None),
        P("dp"),
        P("dp"),
    )
    out_specs = (P("dp", "mp"), P("dp", "mp"), P("dp", "mp"), P("dp", "mp"), P("dp", "mp"))
    cube = mesh.shape["dp"] == 2 * 2 * 2 and mesh.shape["mp"] == 2 * 2
    return jax.shard_map(
        per_device_cube if cube else per_device, mesh=mesh, in_specs=in_specs, out_specs=out_specs, check_vma=False
    )
```

```python
import functools

import jax
import jax.numpy as jnp
from jax import lax
from jax.experimental import pallas as pl
from jax.experimental.pallas import tpu as pltpu
from jax.sharding import PartitionSpec as P

HD = 256
BLK = 128


masked_value = -1e30


def attend_weights(scores, live_mask):
    present = jnp.any(live_mask, axis=1)[None, :, None]
    blocked = jnp.where(live_mask[None], scores, masked_value)
    highest = jnp.max(blocked, axis=2, keepdims=True)
    highest = jnp.where(present, highest, 0.0)
    raised = jnp.exp(jnp.where(live_mask[None], scores - highest, masked_value))
    totals = jnp.maximum(jnp.sum(raised, axis=2, keepdims=True), 1.0)
    return raised / totals


def token_documents(lengths, token_count):
    doc_ends = jnp.cumsum(lengths)
    positions = jnp.arange(token_count, dtype=jnp.int32)
    return jnp.sum((doc_ends[None, :] <= positions[:, None]).astype(jnp.int32), axis=1)


def per_device(
    queries,
    context_grad,
    encoder_rows,
    key_weight,
    value_weight,
    document_lengths,
    block_bin,
    block_document,
):
    bin_count = lax.axis_size("dp")
    full_key, full_value = (
        lax.all_gather(key_weight, "dp", axis=0, tiled=True),
        lax.all_gather(value_weight, "dp", axis=0, tiled=True),
    )
    head_width = full_key.shape[1]
    head_count = head_width // HD
    block_rows = BLK
    blocks_here = block_bin.shape[0]
    both_weights = jnp.concatenate([full_key, full_value], axis=1)
    projected = jnp.dot(encoder_rows, both_weights, preferred_element_type=jnp.float32).astype(
        jnp.bfloat16
    )
    route_table = (block_bin[:, None] == jnp.arange(bin_count, dtype=jnp.int32)[None, :]).astype(
        jnp.bfloat16
    )
    flat_blocks = projected.reshape(blocks_here, block_rows * 2 * head_width)
    outbound = lax.dot_general(
        route_table, flat_blocks, (((0,), (0,)), ((), ())), preferred_element_type=jnp.float32
    )
    outbound = outbound.astype(jnp.bfloat16).reshape(bin_count, block_rows, 2 * head_width)
    slot_docs = (
        lax.dot_general(
            route_table.astype(jnp.float32),
            (block_document + 1).astype(jnp.float32),
            (((0,), (0,)), ((), ())),
        )
        - 1.0
    )
    tag_rows = jnp.broadcast_to(slot_docs[:, None], (bin_count, block_rows)).astype(jnp.bfloat16)
    arrived, arrived_tags = (
        lax.all_to_all(outbound, "dp", split_axis=0, concat_axis=0, tiled=True),
        lax.all_to_all(tag_rows, "dp", split_axis=0, concat_axis=0, tiled=True),
    )
    key_slots = arrived[:, :, :head_width].reshape(bin_count * block_rows, head_count, HD)
    value_slots = arrived[:, :, head_width:].reshape(bin_count * block_rows, head_count, HD)
    token_count = queries.shape[0]
    token_docs = token_documents(document_lengths[0], token_count).astype(jnp.float32)
    live_mask = arrived_tags.reshape(-1).astype(jnp.float32)[None, :] == token_docs[:, None]
    query_heads = queries.reshape(token_count, head_count, HD)
    grad_heads = context_grad.reshape(token_count, head_count, HD)
    scaling = HD ** (-0.5)
    scores = (
        jnp.einsum("thd,shd->hts", query_heads, key_slots, preferred_element_type=jnp.float32)
        * scaling
    )
    attention = attend_weights(scores, live_mask)
    rounded = attention.astype(jnp.bfloat16)
    context = jnp.einsum(
        "hts,shd->thd", rounded, value_slots, preferred_element_type=jnp.float32
    ).astype(jnp.bfloat16)
    grad_raw = jnp.einsum(
        "thd,shd->hts", grad_heads, value_slots, preferred_element_type=jnp.float32
    )
    deltas = jnp.sum(attention * grad_raw, axis=2, keepdims=True)
    score_grad = (attention * (grad_raw - deltas) * scaling).astype(jnp.bfloat16)
    query_grad = jnp.einsum(
        "hts,shd->thd", score_grad, key_slots, preferred_element_type=jnp.float32
    ).astype(jnp.bfloat16)
    key_grad = jnp.einsum(
        "hts,thd->shd", score_grad, query_heads, preferred_element_type=jnp.float32
    ).astype(jnp.bfloat16)
    value_grad = jnp.einsum(
        "hts,thd->shd", rounded, grad_heads, preferred_element_type=jnp.float32
    ).astype(jnp.bfloat16)
    slot_grads = jnp.concatenate(
        [
            key_grad.reshape(bin_count, block_rows, head_width),
            value_grad.reshape(bin_count, block_rows, head_width),
        ],
        axis=2,
    )
    returned = lax.all_to_all(slot_grads, "dp", split_axis=0, concat_axis=0, tiled=True)
    own_grads = jnp.dot(
        route_table,
        returned.reshape(bin_count, block_rows * 2 * head_width),
        preferred_element_type=jnp.float32,
    )
    own_grads = own_grads.astype(jnp.bfloat16).reshape(encoder_rows.shape[0], 2 * head_width)
    weight_terms = lax.dot_general(
        encoder_rows, own_grads, (((0,), (0,)), ((), ())), preferred_element_type=jnp.float32
    )
    weight_sums = lax.psum_scatter(
        weight_terms.astype(jnp.bfloat16), "dp", scatter_dimension=0, tiled=True
    ).astype(jnp.float32)
    key_weight_grad = weight_sums[:, :head_width].astype(jnp.bfloat16)
    value_weight_grad = weight_sums[:, head_width:].astype(jnp.bfloat16)
    row_terms = lax.dot_general(
        own_grads, both_weights, (((1,), (1,)), ((), ())), preferred_element_type=jnp.float32
    )
    encoder_grad = lax.psum_scatter(
        row_terms.astype(jnp.bfloat16), "mp", scatter_dimension=1, tiled=True
    )
    return (
        context.reshape(token_count, head_width),
        query_grad.reshape(token_count, head_width),
        encoder_grad,
        key_weight_grad,
        value_weight_grad,
    )


MESH = pl.DeviceIdType.MESH


def contract(a, b, dim_a, dim_b):
    return lax.dot_general(
        a, b, (((dim_a,), (dim_b,)), ((), ())), preferred_element_type=jnp.float32
    )


def bin_at(me, i):
    def flip(bit, turned):
        return bit + turned - 2 * bit * turned

    core, x, y = me % 2, (me // 2) % 2, me // 4
    return (flip(y, i // 4) * 2 + flip(x, (i // 2) % 2)) * 2 + flip(core, i % 2)


def find(value, options):
    index = jnp.int32(0)
    for k, option in enumerate(options):
        index = jnp.where(option == value, k, index)
    return index


def block_turns(me, n, bins_ref):
    bins = [bins_ref[b] for b in range(bins_ref.shape[0])]
    order = [bin_at(me, i) for i in range(n)]
    hole = find(n * (n - 1) // 2 - sum(bins), order)
    places = [find(b, order) for b in bins]
    return hole, [jnp.where(p > hole, p - 1, p) for p in places]


def step_kernel(
    n,
    count,
    q_ref,
    g_ref,
    enc_hbm,
    kw_ref,
    vw_ref,
    lengths_ref,
    bins_ref,
    docs_ref,
    ctx_ref,
    qg_ref,
    eg_ref,
    kwg_ref,
    vwg_ref,
    enc,
    wts,
    wend,
    acc,
    arrived,
    tags,
    arrived_tags,
    grads,
    ret,
    own,
    gend,
    pend,
    msend,
    mrecv,
    tsend,
    trecv,
    hops,
    passed,
    local_sem,
    gather_send,
    gather_recv,
    lift_send,
    lift_recv,
    core_send,
    core_recv,
    tag_send,
    tag_recv,
    out_send,
    out_recv,
    back_send,
    back_recv,
    g_send,
    g_recv,
    mid_send,
    mid_recv,
    end_send,
    end_recv,
    prod_send,
    prod_recv,
    pair_send,
    pair_recv,
    hop_send,
    hop_recv,
):
    bf16 = jnp.bfloat16
    me, z = lax.axis_index("dp"), lax.axis_index("mp")
    core = me % 2
    x = (me // 2) % 2
    y = me // 4

    def place(py, px, pc):
        return (py * 2 + px) * 2 + pc

    at_x, at_y = place(y, 1 - x, core), place(1 - y, x, core)
    at_c, at_d = place(y, x, 1 - core), place(1 - y, 1 - x, core)
    c_x, c_y = place(y, 1 - x, 1 - core), place(1 - y, x, 1 - core)
    c_d = place(1 - y, 1 - x, 1 - core)
    depth, width = kw_ref.shape
    rows = enc.shape[0]
    blocks = rows // BLK
    blk = BLK
    heads = width // HD
    tokens = q_ref.shape[0]
    last = count - 1
    end = (z // 2) * last
    far_end = last - end
    side = z // 2
    is_end = z == end
    is_inner = z != end
    mate = z + 1 - 2 * (z % 2)
    across = last - z

    def remote(src, dst, send, recv, **device):
        return pltpu.make_async_remote_copy(
            src_ref=src,
            dst_ref=dst,
            send_sem=send,
            recv_sem=recv,
            device_id=device,
            device_id_type=MESH,
        )

    load_enc = pltpu.make_async_copy(enc_hbm, enc, local_sem.at[0])
    load_enc.start()
    barrier = pltpu.get_barrier_semaphore()
    for d in range(1, n):
        pl.semaphore_signal(
            barrier, inc=1, device_id={"dp": (me + d) % n}, device_id_type=MESH
        )
    pl.semaphore_signal(barrier, inc=1, device_id={"mp": mate}, device_id_type=MESH)

    @pl.when(is_inner)
    def _():
        pl.semaphore_signal(barrier, inc=1, device_id={"mp": across}, device_id_type=MESH)


    for d in range(n):
        to = (me + d) % n
        doc = jnp.int32(-1)
        for b in range(blocks):
            doc = jnp.where(bins_ref[b] == to, docs_ref[b], doc)
        tags[to] = jnp.full(tags.shape[1:], doc.astype(jnp.float32), jnp.float32)
    pl.semaphore_wait(barrier, n + (z + 1) // 2 % 2)

    def part_cols(part):
        return pl.ds(part * width, width)

    def head_cols(part, h):
        return pl.ds(pl.multiple_of(part * width + h * HD, HD), HD)

    def land(src, part, h):
        return wts.at[src, :, head_cols(part, h)]

    started = []

    def ship(h, ident, ref, src, part, to):
        copy = remote(
            ref, land(src, part, h), gather_send.at[h, ident], gather_recv.at[h, ident], dp=to
        )
        copy.start()
        started.append(copy)

    def landed(h, ident, src, part):
        remote(
            land(src, part, h),
            land(src, part, h),
            gather_send.at[h, ident],
            gather_recv.at[h, ident],
            dp=at_c,
        ).wait_recv()

    def lifted(src, part, h):
        return wend.at[src % 4, :, head_cols(part, h)]

    ours, theirs = (me, at_x, at_y, at_d), (at_c, c_x, c_y, c_d)
    early = [(0, 0, 0), (0, 1, 0), (0, 0, 1), (0, 1, 1), (1, 0, 0), (2, 1, 0), (1, 1, 0), (2, 0, 0)]
    early += [(3, 0, 0), (3, 1, 0), (1, 0, 1), (2, 1, 1), (1, 1, 1), (2, 0, 1)]
    late = [(3, 0, 1), (3, 1, 1)]
    pieces = early + late

    def lift(i, part, h, ref=None):
        src = ours[i]
        ident = 4 * i + 2 * part + h

        @pl.when(jnp.logical_and(is_end, src // 4 != side))
        def _():
            remote(
                land(src, part, h) if ref is None else ref,
                lifted(src, part, h),
                lift_send.at[ident],
                lift_recv.at[ident],
                mp=mate,
            ).start()

    def each_piece(todo, listed, of_end):
        for i, part, h in listed:

            @pl.when(jnp.logical_and(is_end if of_end else is_inner, ours[i] // 4 != side))
            def _():
                todo(i, part, h, ours[i])

    def lift_copy(i, part, h, src):
        ident = 4 * i + 2 * part + h
        ref = lifted(src, part, h)
        return remote(ref, ref, lift_send.at[ident], lift_recv.at[ident], mp=mate)

    def core_copy(i, part, h, src):
        ident = 4 * i + 2 * part + h
        ref = lifted(src, part, h)
        return remote(ref, ref, core_send.at[ident], core_recv.at[ident], dp=at_c)

    def hand_over(i, part, h, src):
        lift_copy(i, part, h, src).wait_recv()
        core_copy(i, part, h, src).start()

    def ship_own(h):
        cols = pl.ds(h * HD, HD)
        kw, vw = kw_ref.at[:, cols], vw_ref.at[:, cols]
        ship(h, 0, kw, me, 0, at_x)
        ship(h, 3, vw, me, 1, at_y)
        ship(h, 1, vw, me, 1, at_x)
        ship(h, 2, kw, me, 0, at_y)
        ship(h, 6, kw, me, 0, at_c)
        ship(h, 7, vw, me, 1, at_c)
        lift(0, 0, h, kw)
        lift(0, 1, h, vw)

    ship_own(0)
    own_k = pltpu.make_async_copy(kw_ref, wts.at[me, :, part_cols(0)], local_sem.at[1])
    own_v = pltpu.make_async_copy(vw_ref, wts.at[me, :, part_cols(1)], local_sem.at[2])
    own_k.start()
    own_v.start()
    tag_copies = []
    for d in range(1, n):
        to = (me + d) % n
        copy = remote(
            tags.at[to], arrived_tags.at[me], tag_send.at[d], tag_recv.at[d], dp=to
        )
        copy.start()
        tag_copies.append(copy)
    arrived_tags[me] = tags[me]
    own_k.wait()
    own_v.wait()
    load_enc.wait()

    def multiply(h, first_src, second_src, swap=0, fresh=False):
        @pl.loop(0, 2)
        def _(t):
            src = first_src + t * (second_src - first_src)
            columns = pl.ds(pl.multiple_of(src * depth, depth), depth)
            cols = head_cols(t + swap - 2 * t * swap, h)
            product = jnp.dot(
                enc[:, columns], wts[src, :, cols], preferred_element_type=jnp.float32
            ).reshape(blocks, blk, HD)
            if fresh:
                acc[:, :, cols] = product
            else:
                acc[:, :, cols] += product

    def gather(h, when_passed):
        multiply(h, me, me, fresh=True)
        landed(h, 6, at_c, 0)
        landed(h, 7, at_c, 1)
        multiply(h, at_c, at_c)
        landed(h, 0, at_x, 0)
        ship(h, 4, land(at_x, 0, h), at_x, 0, at_y)
        ship(h, 8, land(at_x, 0, h), at_x, 0, at_c)
        lift(1, 0, h)
        landed(h, 3, at_y, 1)
        ship(h, 5, land(at_y, 1, h), at_y, 1, at_x)
        ship(h, 11, land(at_y, 1, h), at_y, 1, at_c)
        lift(2, 1, h)
        when_passed()
        multiply(h, at_x, at_y)
        landed(h, 8, c_x, 0)
        landed(h, 11, c_y, 1)
        multiply(h, c_x, c_y)
        landed(h, 1, at_x, 1)
        ship(h, 9, land(at_x, 1, h), at_x, 1, at_c)
        lift(1, 1, h)
        landed(h, 2, at_y, 0)
        ship(h, 10, land(at_y, 0, h), at_y, 0, at_c)
        lift(2, 0, h)
        multiply(h, at_y, at_x)
        landed(h, 9, c_x, 1)
        landed(h, 10, c_y, 0)
        multiply(h, c_y, c_x)
        landed(h, 4, at_d, 0)
        ship(h, 12, land(at_d, 0, h), at_d, 0, at_c)
        lift(3, 0, h)
        landed(h, 5, at_d, 1)
        ship(h, 13, land(at_d, 1, h), at_d, 1, at_c)
        lift(3, 1, h)
        multiply(h, at_d, at_d)
        landed(h, 12, c_d, 0)
        landed(h, 13, c_d, 1)
        multiply(h, c_d, c_d)

    def rows_of(slot):
        return pl.ds(pl.multiple_of(slot * blk, blk), blk)

    def slot_at(i):
        return bin_at(me, i)

    bins = [bins_ref[b] for b in range(blocks)]
    hole, turns = block_turns(me, n, bins_ref)

    def out_copy(h, i):
        to = slot_at(i)
        return remote(
            grads.at[h, :, rows_of(to), :],
            arrived.at[h, :, rows_of(me), :],
            out_send.at[h, i],
            out_recv.at[h, i],
            dp=to,
        )

    def send_slots(h):
        for i in [*range(1, n), 0]:
            to = slot_at(i)
            index = find(to, bins)
            for part in range(2):
                cols = pl.ds(part * width + h * HD, HD)
                picked = acc[index, :, cols].astype(bf16)
                if i == 0:
                    arrived[h, part, rows_of(me), :] = picked
                else:
                    grads[h, part, rows_of(to), :] = picked
            if i > 0:
                out_copy(h, i).start()

    gather(0, lambda: ship_own(1))
    gather(1, lambda: send_slots(0))
    send_slots(1)
    each_piece(hand_over, early, False)
    position = lax.broadcasted_iota(jnp.int32, (tokens, 1), 0)
    token_doc = jnp.zeros(position.shape, jnp.float32)
    doc_end = jnp.int32(0)
    for k in range(lengths_ref.shape[1]):
        doc_end = doc_end + lengths_ref[0, k]
        token_doc = token_doc + jnp.where(position >= doc_end, 1.0, 0.0)
    for copy in tag_copies:
        copy.wait()
    tag_row = jnp.concatenate([arrived_tags[s, 0:1, :] for s in range(n)], axis=1)
    live = tag_row == token_doc
    present = jnp.max(jnp.where(live, 1.0, 0.0), axis=1, keepdims=True) > 0.0
    scaling = HD ** (-0.5)
    for h in range(heads):
        for i in range(1, n):
            out_copy(h, i).wait()
        hk = pl.ds(h * HD, HD)
        q, g = q_ref[:, hk], g_ref[:, hk]
        scores = contract(q, arrived[h, 0], 1, 1) * scaling
        highest = jnp.max(jnp.where(live, scores, masked_value), axis=1, keepdims=True)
        highest = jnp.where(present, highest, 0.0)
        raised = jnp.exp(jnp.where(live, scores - highest, masked_value))
        totals = jnp.maximum(jnp.sum(raised, axis=1, keepdims=True), 1.0)
        attention = raised / totals
        rounded = attention.astype(bf16)
        grad_raw = contract(g, arrived[h, 1], 1, 1)
        deltas = jnp.sum(attention * grad_raw, axis=1, keepdims=True)
        score_grad = (attention * (grad_raw - deltas) * scaling).astype(bf16)
        grads[h, 0] = contract(score_grad, q, 0, 0).astype(bf16)
        grads[h, 1] = contract(rounded, g, 0, 0).astype(bf16)
        tsend[h, pl.ds(0, tokens), :] = rounded
        tsend[h, pl.ds(tokens, tokens), :] = score_grad
        if h == 0:
            each_piece(hand_over, late, False)

    def back_copy(i):
        to = slot_at(i)
        return remote(
            grads.at[:, :, rows_of(to), :],
            ret.at[:, :, rows_of(me), :],
            back_send.at[i],
            back_recv.at[i],
            dp=to,
        )

    for i in range(1, n):
        back_copy(i).start()
    ret[:, :, rows_of(me), :] = grads[:, :, rows_of(me), :]
    for h in range(heads):
        hk = pl.ds(h * HD, HD)
        ctx_ref[:, hk] = jnp.dot(
            tsend[h, pl.ds(0, tokens), :], arrived[h, 1], preferred_element_type=jnp.float32
        ).astype(bf16)
        qg_ref[:, hk] = jnp.dot(
            tsend[h, pl.ds(tokens, tokens), :], arrived[h, 0], preferred_element_type=jnp.float32
        ).astype(bf16)

    def g_copy(r):
        return remote(own.at[r], gend.at[r], g_send.at[r], g_recv.at[r], mp=mate)

    half = blk // 2

    def half_rows(k):
        return pl.ds(pl.multiple_of(k * half, half), half)

    def first_g_copy(k):
        sem = k * blocks
        return remote(
            own.at[0, half_rows(k)], gend.at[0, half_rows(k)], g_send.at[sem], g_recv.at[sem], mp=mate
        )


    def first_mid_copy(way, k):
        sem = k * blocks
        return remote(
            msend.at[way, 0, half_rows(k)],
            mrecv.at[way, 0, half_rows(k)],
            mid_send.at[way, sem],
            mid_recv.at[way, sem],
            mp=across,
        )

    def mid_copy(way, r):
        return remote(
            msend.at[way, r], mrecv.at[way, r], mid_send.at[way, r], mid_recv.at[way, r], mp=across
        )

    def end_copy(r):
        return remote(mrecv.at[0, r], mrecv.at[0, r], end_send.at[r], end_recv.at[r], mp=mate)

    def prod_copy(r):
        return remote(msend.at[0, r], pend.at[r], prod_send.at[r], prod_recv.at[r], mp=mate)

    def pair_copy(i):
        return remote(tsend.at[i], trecv.at[i], pair_send.at[i], pair_recv.at[i], dp=at_c)

    def hop_copy(way, i, src):
        to = at_x if (way == 0) == (i < 2) else at_y
        return remote(src, hops.at[way, i], hop_send.at[way, i], hop_recv.at[way, i], dp=to)

    for i, part, h in pieces:

        @pl.when(jnp.logical_and(is_inner, theirs[i] // 4 != side))
        def _():
            core_copy(i, part, h, theirs[i]).wait_recv()

    def collect(r):
        back_copy_at = slot_at(r + 1)
        remote(
            ret.at[:, :, rows_of(back_copy_at), :],
            ret.at[:, :, rows_of(back_copy_at), :],
            back_send.at[r + 1],
            back_recv.at[r + 1],
            dp=at_c,
        ).wait_recv()
        later = hole <= r
        for h in range(heads):
            for part in range(2):
                own[r, :, pl.ds(part * width + h * HD, HD)] = jnp.where(
                    later,
                    ret[h, part, rows_of(back_copy_at), :],
                    ret[h, part, rows_of(slot_at(r)), :],
                )

        @pl.when(jnp.logical_and(is_end, r > 0))
        def _():
            g_copy(r).start()

    def own_weights(d, j):
        return wts[2 * d + j]

    def end_weights(d, j):
        return wend[(d % 2) * 2 + j]

    def shard_of(i, parity):
        flip_x, flip_y = 1 - i // 2, 1 - i % 2
        px = x + flip_x - 2 * x * flip_x
        py = y + flip_y - 2 * y * flip_y
        return place(py, px, parity)

    def term(shard, part, h):
        columns = pl.ds(pl.multiple_of(shard * depth, depth), depth)
        return contract(enc[:, columns], ret[h, part, pl.ds(0, rows), :], 0, 0).astype(bf16)

    def each_slab(todo):
        for part in range(2):
            for h in range(heads):
                todo(part, h, pl.ds(part * width + h * HD, HD))

    def half_cols(j):
        return pl.ds(pl.multiple_of(j * width, width), width)

    collect(0)

    @pl.when(is_end)
    def _():
        first_g_copy(0).start()
        first_g_copy(1).start()

    @pl.when(is_inner)
    def _():
        @pl.loop(0, 2)
        def _(k):
            first_g_copy(k).wait_recv()
            for way, dest in ((0, far_end), (1, across)):

                @pl.loop(0, 2)
                def _(j):
                    summed = contract(own[0, half_rows(k)], own_weights(dest, j), 1, 1)
                    summed += contract(gend[0, half_rows(k)], end_weights(dest, j), 1, 1)
                    msend[way, 0, half_rows(k), half_cols(j)] = summed.astype(bf16)

                first_mid_copy(way, k).start()

    def send_across(way, r):
        dest = across if way else far_end

        @pl.loop(0, 2)
        def _(j):
            summed = contract(own[r], own_weights(dest, j), 1, 1)
            summed += contract(gend[r], end_weights(dest, j), 1, 1)
            msend[way, r, :, half_cols(j)] = summed.astype(bf16)

        mid_copy(way, r).start()

    @pl.loop(1, blocks)
    def _(r):
        @pl.when(r < 3)
        def _():
            collect(r)

        @pl.when(is_inner)
        def _():
            g_copy(r).wait_recv()
            send_across(0, r)

            @pl.when(r > 1)
            def _():
                send_across(1, r - 1)

        @pl.when(r == 2)
        def _():
            @pl.loop(3, blocks)
            def _(later):
                collect(later)

            for b in range(blocks):
                block = own[turns[b]]
                for h in range(heads):
                    for part in range(2):
                        first = part * width + h * HD
                        ret[h, part, pl.ds(b * blk, blk), :] = block[:, first : first + HD]

            @pl.loop(0, 4)
            def _(i):
                shard = shard_of(i, 1 - core)

                def fill(part, h, cols):
                    tsend[i, :, cols] = term(shard, part, h)

                each_slab(fill)
                pair_copy(i).start()

        @pl.when(r == 3)
        def _():
            @pl.loop(0, 4)
            def _(i):
                shard = shard_of(i, core)
                pair_copy(i).wait_recv()

                def fill(part, h, cols):
                    summed = term(shard, part, h).astype(jnp.float32)
                    summed += trecv[i, :, cols].astype(jnp.float32)
                    trecv[i, :, cols] = summed.astype(bf16)

                each_slab(fill)

                @pl.when(i == 1)
                def _():
                    hop_copy(0, 1, trecv.at[0, :, part_cols(0)]).start()
                    hop_copy(0, 0, trecv.at[1, :, part_cols(0)]).start()
                    hop_copy(1, 1, trecv.at[0, :, part_cols(1)]).start()

                @pl.when(i == 2)
                def _():
                    hop_copy(1, 0, trecv.at[2, :, part_cols(1)]).start()

    @pl.when(is_end)
    def _():
        @pl.loop(0, blocks)
        def _(r):
            @pl.loop(0, 2)
            def _(j):
                msend[0, r, :, half_cols(j)] = contract(own[r], own_weights(mate, j), 1, 1).astype(bf16)

            prod_copy(r).start()

    @pl.when(is_inner)
    def _():
        send_across(1, blocks - 1)

    for way in range(2):
        hop_copy(way, 1, hops.at[way, 1]).wait_recv()
        summed = trecv[2 - way, :, part_cols(way)].astype(jnp.float32)
        summed += hops[way, 1].astype(jnp.float32)
        passed[way] = summed.astype(bf16)
        hop_copy(way, 2, passed.at[way]).start()

    total = acc.at[0]

    def wait_mid(way, r):
        @pl.when(r == 0)
        def _():
            first_mid_copy(way, 0).wait_recv()
            first_mid_copy(way, 1).wait_recv()

        @pl.when(r > 0)
        def _():
            mid_copy(way, r).wait_recv()

    def own_product(r, dest):
        @pl.loop(0, 2)
        def _(j):
            total[:, half_cols(j)] = contract(own[r], own_weights(dest, j), 1, 1)

    def finish(r):
        own_product(r, z)
        prod_copy(r).wait_recv()
        total[...] += pend[r].astype(jnp.float32)
        wait_mid(1, r)
        eg_ref[r] = (total[...] + mrecv[1, r].astype(jnp.float32)).astype(bf16)

    @pl.loop(0, blocks)
    def _(r):
        @pl.when(is_inner)
        def _():
            own_product(r, end)
            wait_mid(0, r)
            mrecv[0, r] = (total[...] + mrecv[0, r].astype(jnp.float32)).astype(bf16)
            end_copy(r).start()

            @pl.when(r > 0)
            def _():
                finish(r - 1)

            @pl.when(r == blocks - 1)
            def _():
                finish(r)

        @pl.when(is_end)
        def _():
            own_product(r, z)
            end_copy(r).wait_recv()
            eg_ref[r] = (total[...] + mrecv[0, r].astype(jnp.float32)).astype(bf16)

        @pl.when(r == blocks - 2)
        def _():
            for way, out in ((0, kwg_ref), (1, vwg_ref)):
                hop_copy(way, 0, hops.at[way, 0]).wait_recv()
                hop_copy(way, 2, hops.at[way, 2]).wait_recv()
                summed = trecv[3, :, part_cols(way)].astype(jnp.float32)
                summed += hops[way, 0].astype(jnp.float32) + hops[way, 2].astype(jnp.float32)
                out[...] = summed.astype(bf16)

    for copy in started:
        copy.wait_send()
    each_piece(lambda *piece: lift_copy(*piece).wait_send(), pieces, True)
    each_piece(lambda *piece: core_copy(*piece).wait_send(), pieces, False)

    @pl.loop(0, blocks)
    def _(r):
        @pl.when(is_end)
        def _():
            prod_copy(r).wait_send()

            @pl.when(r > 0)
            def _():
                g_copy(r).wait_send()

        @pl.when(is_inner)
        def _():
            end_copy(r).wait_send()

            @pl.when(r > 0)
            def _():
                mid_copy(0, r).wait_send()
                mid_copy(1, r).wait_send()

    @pl.loop(0, 2)
    def _(k):
        @pl.when(is_end)
        def _():
            first_g_copy(k).wait_send()

        @pl.when(is_inner)
        def _():
            first_mid_copy(0, k).wait_send()
            first_mid_copy(1, k).wait_send()

    for i in range(1, n):
        back_copy(i).wait_send()
    for i in range(4):
        pair_copy(i).wait_send()
    for way in range(2):
        for i in range(3):
            hop_copy(way, i, hops.at[way, i]).wait_send()


def deliver_kernel(n, bins_ref, *refs):
    turns = block_turns(lax.axis_index("dp"), n, bins_ref)[1]
    count = (len(refs) - 1) // 2
    ins, outs, store_sem = refs[:count], refs[count : 2 * count], refs[2 * count]
    stores = []
    for k in range(count):
        pieces = [(ins[k], outs[k])]
        if len(ins[k].shape) == 3:
            blocks, size, _ = ins[k].shape
            pieces = [
                (ins[k].at[turns[b]], outs[k].at[pl.ds(b * size, size), :]) for b in range(blocks)
            ]
        for source, target in pieces:
            stores.append(pltpu.make_async_copy(source, target, store_sem.at[len(stores)]))
            stores[-1].start()
    for store in stores:
        store.wait()


def deliver(n, bins, arrays):
    hbm = pl.BlockSpec(memory_space=pl.ANY)
    vmem = pl.BlockSpec(memory_space=pltpu.VMEM)
    copies = sum(a.shape[0] if a.ndim == 3 else 1 for a in arrays)
    return pl.pallas_call(
        functools.partial(deliver_kernel, n),
        out_shape=tuple(
            jax.ShapeDtypeStruct((a.size // a.shape[-1], a.shape[-1]), a.dtype) for a in arrays
        ),
        in_specs=[pl.BlockSpec(memory_space=pltpu.SMEM)] + [vmem] * len(arrays),
        out_specs=(hbm,) * len(arrays),
        scratch_shapes=[pltpu.SemaphoreType.DMA((copies,))],
        compiler_params=pltpu.CompilerParams(vmem_limit_bytes=8 * 1024 * 1024),
    )(bins, *arrays)


def per_device_cube(
    queries,
    context_grad,
    encoder_rows,
    key_weight,
    value_weight,
    document_lengths,
    block_bin,
    block_document,
):
    n, count = lax.axis_size("dp"), lax.axis_size("mp")
    rows, model = encoder_rows.shape
    depth, width = key_weight.shape
    heads = width // HD
    tokens = queries.shape[0]
    blocks = rows // BLK
    chips = n // 2
    vmem = pl.BlockSpec(memory_space=pltpu.VMEM)
    smem = pl.BlockSpec(memory_space=pltpu.SMEM)
    hbm = pl.BlockSpec(memory_space=pl.ANY)
    bf16 = jnp.bfloat16
    dma = pltpu.SemaphoreType.DMA
    shape = pltpu.VMEM
    pairs = []
    for extent in [(heads, 14), (16,), (16,), (n,), (heads, n), (n,), (n,), (2, n), (blocks,), (blocks,), (chips,), (2, 3)]:
        pairs += [dma(extent), dma(extent)]
    outs = pl.pallas_call(
        functools.partial(step_kernel, n, count),
        out_shape=(
            shape((tokens, width), bf16),
            shape((tokens, width), bf16),
            shape((blocks, BLK, model // count), bf16),
            shape((depth, width), bf16),
            shape((depth, width), bf16),
        ),
        in_specs=[vmem, vmem, hbm, vmem, vmem, smem, smem, smem],
        out_specs=(vmem,) * 5,
        scratch_shapes=[
            pltpu.VMEM((rows, model), bf16),
            pltpu.VMEM((n, depth, 2 * width), bf16),
            pltpu.VMEM((n // 2, depth, 2 * width), bf16),
            pltpu.VMEM((blocks, BLK, 2 * width), jnp.float32),
            pltpu.VMEM((heads, 2, n * BLK, HD), bf16),
            pltpu.VMEM((n, 8, BLK), jnp.float32),
            pltpu.VMEM((n, 8, BLK), jnp.float32),
            pltpu.VMEM((heads, 2, n * BLK, HD), bf16),
            pltpu.VMEM((heads, 2, n * BLK, HD), bf16),
            pltpu.VMEM((blocks, BLK, 2 * width), bf16),
            pltpu.VMEM((blocks, BLK, 2 * width), bf16),
            pltpu.VMEM((blocks, BLK, 2 * width), bf16),
            pltpu.VMEM((2, blocks, BLK, 2 * width), bf16),
            pltpu.VMEM((2, blocks, BLK, 2 * width), bf16),
            pltpu.VMEM((chips, depth, 2 * width), bf16),
            pltpu.VMEM((chips, depth, 2 * width), bf16),
            pltpu.VMEM((2, 3, depth, width), bf16),
            pltpu.VMEM((2, depth, width), bf16),
            dma((3,)),
            *pairs,
        ],
        compiler_params=pltpu.CompilerParams(
            collective_id=0, has_side_effects=True, vmem_limit_bytes=60 * 1024 * 1024
        ),
    )(
        queries,
        context_grad,
        encoder_rows,
        key_weight,
        value_weight,
        document_lengths,
        block_bin,
        block_document,
    )
    return deliver(n, block_bin, outs)


def solution(mesh):
    in_specs = (
        P("dp", "mp"),
        P("dp", "mp"),
        P("dp", None),
        P("dp", "mp"),
        P("dp", "mp"),
        P("dp", None),
        P("dp"),
        P("dp"),
    )
    out_specs = (P("dp", "mp"), P("dp", "mp"), P("dp", "mp"), P("dp", "mp"), P("dp", "mp"))
    cube = mesh.shape["dp"] == 2 * 2 * 2 and mesh.shape["mp"] == 2 * 2
    return jax.shard_map(
        per_device_cube if cube else per_device, mesh=mesh, in_specs=in_specs, out_specs=out_specs, check_vma=False
    )
```

```python
import functools

import jax
import jax.numpy as jnp
from jax import lax
from jax.experimental import pallas as pl
from jax.experimental.pallas import tpu as pltpu
from jax.sharding import PartitionSpec as P

HD = 256
BLK = 128


masked_value = -1e30


def attend_weights(scores, live_mask):
    present = jnp.any(live_mask, axis=1)[None, :, None]
    blocked = jnp.where(live_mask[None], scores, masked_value)
    highest = jnp.max(blocked, axis=2, keepdims=True)
    highest = jnp.where(present, highest, 0.0)
    raised = jnp.exp(jnp.where(live_mask[None], scores - highest, masked_value))
    totals = jnp.maximum(jnp.sum(raised, axis=2, keepdims=True), 1.0)
    return raised / totals


def token_documents(lengths, token_count):
    doc_ends = jnp.cumsum(lengths)
    positions = jnp.arange(token_count, dtype=jnp.int32)
    return jnp.sum((doc_ends[None, :] <= positions[:, None]).astype(jnp.int32), axis=1)


def per_device(
    queries,
    context_grad,
    encoder_rows,
    key_weight,
    value_weight,
    document_lengths,
    block_bin,
    block_document,
):
    bin_count = lax.axis_size("dp")
    full_key, full_value = (
        lax.all_gather(key_weight, "dp", axis=0, tiled=True),
        lax.all_gather(value_weight, "dp", axis=0, tiled=True),
    )
    head_width = full_key.shape[1]
    head_count = head_width // HD
    block_rows = BLK
    blocks_here = block_bin.shape[0]
    both_weights = jnp.concatenate([full_key, full_value], axis=1)
    projected = jnp.dot(encoder_rows, both_weights, preferred_element_type=jnp.float32).astype(
        jnp.bfloat16
    )
    route_table = (block_bin[:, None] == jnp.arange(bin_count, dtype=jnp.int32)[None, :]).astype(
        jnp.bfloat16
    )
    flat_blocks = projected.reshape(blocks_here, block_rows * 2 * head_width)
    outbound = lax.dot_general(
        route_table, flat_blocks, (((0,), (0,)), ((), ())), preferred_element_type=jnp.float32
    )
    outbound = outbound.astype(jnp.bfloat16).reshape(bin_count, block_rows, 2 * head_width)
    slot_docs = (
        lax.dot_general(
            route_table.astype(jnp.float32),
            (block_document + 1).astype(jnp.float32),
            (((0,), (0,)), ((), ())),
        )
        - 1.0
    )
    tag_rows = jnp.broadcast_to(slot_docs[:, None], (bin_count, block_rows)).astype(jnp.bfloat16)
    arrived, arrived_tags = (
        lax.all_to_all(outbound, "dp", split_axis=0, concat_axis=0, tiled=True),
        lax.all_to_all(tag_rows, "dp", split_axis=0, concat_axis=0, tiled=True),
    )
    key_slots = arrived[:, :, :head_width].reshape(bin_count * block_rows, head_count, HD)
    value_slots = arrived[:, :, head_width:].reshape(bin_count * block_rows, head_count, HD)
    token_count = queries.shape[0]
    token_docs = token_documents(document_lengths[0], token_count).astype(jnp.float32)
    live_mask = arrived_tags.reshape(-1).astype(jnp.float32)[None, :] == token_docs[:, None]
    query_heads = queries.reshape(token_count, head_count, HD)
    grad_heads = context_grad.reshape(token_count, head_count, HD)
    scaling = HD ** (-0.5)
    scores = (
        jnp.einsum("thd,shd->hts", query_heads, key_slots, preferred_element_type=jnp.float32)
        * scaling
    )
    attention = attend_weights(scores, live_mask)
    rounded = attention.astype(jnp.bfloat16)
    context = jnp.einsum(
        "hts,shd->thd", rounded, value_slots, preferred_element_type=jnp.float32
    ).astype(jnp.bfloat16)
    grad_raw = jnp.einsum(
        "thd,shd->hts", grad_heads, value_slots, preferred_element_type=jnp.float32
    )
    deltas = jnp.sum(attention * grad_raw, axis=2, keepdims=True)
    score_grad = (attention * (grad_raw - deltas) * scaling).astype(jnp.bfloat16)
    query_grad = jnp.einsum(
        "hts,shd->thd", score_grad, key_slots, preferred_element_type=jnp.float32
    ).astype(jnp.bfloat16)
    key_grad = jnp.einsum(
        "hts,thd->shd", score_grad, query_heads, preferred_element_type=jnp.float32
    ).astype(jnp.bfloat16)
    value_grad = jnp.einsum(
        "hts,thd->shd", rounded, grad_heads, preferred_element_type=jnp.float32
    ).astype(jnp.bfloat16)
    slot_grads = jnp.concatenate(
        [
            key_grad.reshape(bin_count, block_rows, head_width),
            value_grad.reshape(bin_count, block_rows, head_width),
        ],
        axis=2,
    )
    returned = lax.all_to_all(slot_grads, "dp", split_axis=0, concat_axis=0, tiled=True)
    own_grads = jnp.dot(
        route_table,
        returned.reshape(bin_count, block_rows * 2 * head_width),
        preferred_element_type=jnp.float32,
    )
    own_grads = own_grads.astype(jnp.bfloat16).reshape(encoder_rows.shape[0], 2 * head_width)
    weight_terms = lax.dot_general(
        encoder_rows, own_grads, (((0,), (0,)), ((), ())), preferred_element_type=jnp.float32
    )
    weight_sums = lax.psum_scatter(
        weight_terms.astype(jnp.bfloat16), "dp", scatter_dimension=0, tiled=True
    ).astype(jnp.float32)
    key_weight_grad = weight_sums[:, :head_width].astype(jnp.bfloat16)
    value_weight_grad = weight_sums[:, head_width:].astype(jnp.bfloat16)
    row_terms = lax.dot_general(
        own_grads, both_weights, (((1,), (1,)), ((), ())), preferred_element_type=jnp.float32
    )
    encoder_grad = lax.psum_scatter(
        row_terms.astype(jnp.bfloat16), "mp", scatter_dimension=1, tiled=True
    )
    return (
        context.reshape(token_count, head_width),
        query_grad.reshape(token_count, head_width),
        encoder_grad,
        key_weight_grad,
        value_weight_grad,
    )


MESH = pl.DeviceIdType.MESH


def contract(a, b, dim_a, dim_b):
    return lax.dot_general(
        a, b, (((dim_a,), (dim_b,)), ((), ())), preferred_element_type=jnp.float32
    )


def bin_at(me, i):
    def flip(bit, turned):
        return bit + turned - 2 * bit * turned

    core, x, y = me % 2, (me // 2) % 2, me // 4
    return (flip(y, i // 4) * 2 + flip(x, (i // 2) % 2)) * 2 + flip(core, i % 2)


def find(value, options):
    index = jnp.int32(0)
    for k, option in enumerate(options):
        index = jnp.where(option == value, k, index)
    return index


def block_turns(me, n, bins_ref):
    bins = [bins_ref[b] for b in range(bins_ref.shape[0])]
    order = [bin_at(me, i) for i in range(n)]
    hole = find(n * (n - 1) // 2 - sum(bins), order)
    places = [find(b, order) for b in bins]
    return hole, [jnp.where(p > hole, p - 1, p) for p in places]


def step_kernel(
    n,
    count,
    q_ref,
    g_ref,
    enc_hbm,
    kw_ref,
    vw_ref,
    lengths_ref,
    bins_ref,
    docs_ref,
    ctx_ref,
    qg_ref,
    eg_ref,
    kwg_ref,
    vwg_ref,
    enc,
    wts,
    wend,
    acc,
    arrived,
    tags,
    arrived_tags,
    grads,
    ret,
    own,
    gend,
    pend,
    msend,
    mrecv,
    tsend,
    trecv,
    hops,
    passed,
    local_sem,
    gather_send,
    gather_recv,
    lift_send,
    lift_recv,
    core_send,
    core_recv,
    tag_send,
    tag_recv,
    out_send,
    out_recv,
    back_send,
    back_recv,
    g_send,
    g_recv,
    mid_send,
    mid_recv,
    end_send,
    end_recv,
    prod_send,
    prod_recv,
    pair_send,
    pair_recv,
    hop_send,
    hop_recv,
):
    bf16 = jnp.bfloat16
    me, z = lax.axis_index("dp"), lax.axis_index("mp")
    core = me % 2
    x = (me // 2) % 2
    y = me // 4

    def place(py, px, pc):
        return (py * 2 + px) * 2 + pc

    at_x, at_y = place(y, 1 - x, core), place(1 - y, x, core)
    at_c, at_d = place(y, x, 1 - core), place(1 - y, 1 - x, core)
    c_x, c_y = place(y, 1 - x, 1 - core), place(1 - y, x, 1 - core)
    c_d = place(1 - y, 1 - x, 1 - core)
    depth, width = kw_ref.shape
    rows = enc.shape[0]
    blocks = rows // BLK
    blk = BLK
    heads = width // HD
    tokens = q_ref.shape[0]
    last = count - 1
    end = (z // 2) * last
    far_end = last - end
    side = z // 2
    is_end = z == end
    is_inner = z != end
    mate = z + 1 - 2 * (z % 2)
    across = last - z

    def remote(src, dst, send, recv, **device):
        return pltpu.make_async_remote_copy(
            src_ref=src,
            dst_ref=dst,
            send_sem=send,
            recv_sem=recv,
            device_id=device,
            device_id_type=MESH,
        )

    load_enc = pltpu.make_async_copy(enc_hbm, enc, local_sem.at[0])
    load_enc.start()
    barrier = pltpu.get_barrier_semaphore()
    for d in range(1, n):
        pl.semaphore_signal(
            barrier, inc=1, device_id={"dp": (me + d) % n}, device_id_type=MESH
        )
    pl.semaphore_signal(barrier, inc=1, device_id={"mp": mate}, device_id_type=MESH)

    @pl.when(is_inner)
    def _():
        pl.semaphore_signal(barrier, inc=1, device_id={"mp": across}, device_id_type=MESH)


    for d in range(n):
        to = (me + d) % n
        doc = jnp.int32(-1)
        for b in range(blocks):
            doc = jnp.where(bins_ref[b] == to, docs_ref[b], doc)
        tags[to] = jnp.full(tags.shape[1:], doc.astype(jnp.float32), jnp.float32)
    pl.semaphore_wait(barrier, n + (z + 1) // 2 % 2)

    def part_cols(part):
        return pl.ds(part * width, width)

    def head_cols(part, h):
        return pl.ds(pl.multiple_of(part * width + h * HD, HD), HD)

    def land(src, part, h):
        return wts.at[src, :, head_cols(part, h)]

    started = []

    def ship(h, ident, ref, src, part, to):
        copy = remote(
            ref, land(src, part, h), gather_send.at[h, ident], gather_recv.at[h, ident], dp=to
        )
        copy.start()
        started.append(copy)

    def landed(h, ident, src, part):
        remote(
            land(src, part, h),
            land(src, part, h),
            gather_send.at[h, ident],
            gather_recv.at[h, ident],
            dp=at_c,
        ).wait_recv()

    def lifted(src, part, h):
        return wend.at[src % 4, :, head_cols(part, h)]

    ours, theirs = (me, at_x, at_y, at_d), (at_c, c_x, c_y, c_d)
    early = [(0, 0, 0), (0, 1, 0), (0, 0, 1), (0, 1, 1), (1, 0, 0), (2, 1, 0), (1, 1, 0), (2, 0, 0)]
    early += [(3, 0, 0), (3, 1, 0), (1, 0, 1), (2, 1, 1), (1, 1, 1), (2, 0, 1)]
    late = [(3, 0, 1), (3, 1, 1)]
    pieces = early + late

    def lift(i, part, h, ref=None):
        src = ours[i]
        ident = 4 * i + 2 * part + h

        @pl.when(jnp.logical_and(is_end, src // 4 != side))
        def _():
            remote(
                land(src, part, h) if ref is None else ref,
                lifted(src, part, h),
                lift_send.at[ident],
                lift_recv.at[ident],
                mp=mate,
            ).start()

    def each_piece(todo, listed, of_end):
        for i, part, h in listed:

            @pl.when(jnp.logical_and(is_end if of_end else is_inner, ours[i] // 4 != side))
            def _():
                todo(i, part, h, ours[i])

    def lift_copy(i, part, h, src):
        ident = 4 * i + 2 * part + h
        ref = lifted(src, part, h)
        return remote(ref, ref, lift_send.at[ident], lift_recv.at[ident], mp=mate)

    def core_copy(i, part, h, src):
        ident = 4 * i + 2 * part + h
        ref = lifted(src, part, h)
        return remote(ref, ref, core_send.at[ident], core_recv.at[ident], dp=at_c)

    def hand_over(i, part, h, src):
        lift_copy(i, part, h, src).wait_recv()
        core_copy(i, part, h, src).start()

    def ship_own(h):
        cols = pl.ds(h * HD, HD)
        kw, vw = kw_ref.at[:, cols], vw_ref.at[:, cols]
        ship(h, 0, kw, me, 0, at_x)
        ship(h, 3, vw, me, 1, at_y)
        ship(h, 1, vw, me, 1, at_x)
        ship(h, 2, kw, me, 0, at_y)
        ship(h, 6, kw, me, 0, at_c)
        ship(h, 7, vw, me, 1, at_c)
        lift(0, 0, h, kw)
        lift(0, 1, h, vw)

    ship_own(0)
    own_k = pltpu.make_async_copy(kw_ref, wts.at[me, :, part_cols(0)], local_sem.at[1])
    own_v = pltpu.make_async_copy(vw_ref, wts.at[me, :, part_cols(1)], local_sem.at[2])
    own_k.start()
    own_v.start()
    tag_copies = []
    for d in range(1, n):
        to = (me + d) % n
        copy = remote(
            tags.at[to], arrived_tags.at[me], tag_send.at[d], tag_recv.at[d], dp=to
        )
        copy.start()
        tag_copies.append(copy)
    arrived_tags[me] = tags[me]
    own_k.wait()
    own_v.wait()
    load_enc.wait()

    def multiply(h, first_src, second_src, swap=0, fresh=False):
        @pl.loop(0, 2)
        def _(t):
            src = first_src + t * (second_src - first_src)
            columns = pl.ds(pl.multiple_of(src * depth, depth), depth)
            cols = head_cols(t + swap - 2 * t * swap, h)
            product = jnp.dot(
                enc[:, columns], wts[src, :, cols], preferred_element_type=jnp.float32
            ).reshape(blocks, blk, HD)
            if fresh:
                acc[:, :, cols] = product
            else:
                acc[:, :, cols] += product

    def gather(h, when_passed):
        multiply(h, me, me, fresh=True)
        landed(h, 6, at_c, 0)
        landed(h, 7, at_c, 1)
        multiply(h, at_c, at_c)
        landed(h, 0, at_x, 0)
        ship(h, 4, land(at_x, 0, h), at_x, 0, at_y)
        ship(h, 8, land(at_x, 0, h), at_x, 0, at_c)
        lift(1, 0, h)
        landed(h, 3, at_y, 1)
        ship(h, 5, land(at_y, 1, h), at_y, 1, at_x)
        ship(h, 11, land(at_y, 1, h), at_y, 1, at_c)
        lift(2, 1, h)
        when_passed()
        multiply(h, at_x, at_y)
        landed(h, 8, c_x, 0)
        landed(h, 11, c_y, 1)
        multiply(h, c_x, c_y)
        landed(h, 1, at_x, 1)
        ship(h, 9, land(at_x, 1, h), at_x, 1, at_c)
        lift(1, 1, h)
        landed(h, 2, at_y, 0)
        ship(h, 10, land(at_y, 0, h), at_y, 0, at_c)
        lift(2, 0, h)
        multiply(h, at_y, at_x)
        landed(h, 9, c_x, 1)
        landed(h, 10, c_y, 0)
        multiply(h, c_y, c_x)
        landed(h, 4, at_d, 0)
        ship(h, 12, land(at_d, 0, h), at_d, 0, at_c)
        lift(3, 0, h)
        landed(h, 5, at_d, 1)
        ship(h, 13, land(at_d, 1, h), at_d, 1, at_c)
        lift(3, 1, h)
        multiply(h, at_d, at_d)
        landed(h, 12, c_d, 0)
        landed(h, 13, c_d, 1)
        multiply(h, c_d, c_d)

    def rows_of(slot):
        return pl.ds(pl.multiple_of(slot * blk, blk), blk)

    def slot_at(i):
        return bin_at(me, i)

    bins = [bins_ref[b] for b in range(blocks)]
    hole, turns = block_turns(me, n, bins_ref)

    def out_copy(h, i):
        to = slot_at(i)
        return remote(
            grads.at[h, :, rows_of(to), :],
            arrived.at[h, :, rows_of(me), :],
            out_send.at[h, i],
            out_recv.at[h, i],
            dp=to,
        )

    def send_slots(h):
        for i in [*range(1, n), 0]:
            to = slot_at(i)
            index = find(to, bins)
            for part in range(2):
                cols = pl.ds(part * width + h * HD, HD)
                picked = acc[index, :, cols].astype(bf16)
                if i == 0:
                    arrived[h, part, rows_of(me), :] = picked
                else:
                    grads[h, part, rows_of(to), :] = picked
            if i > 0:
                out_copy(h, i).start()

    gather(0, lambda: ship_own(1))
    gather(1, lambda: send_slots(0))
    send_slots(1)
    each_piece(hand_over, early, False)
    position = lax.broadcasted_iota(jnp.int32, (tokens, 1), 0)
    token_doc = jnp.zeros(position.shape, jnp.float32)
    doc_end = jnp.int32(0)
    for k in range(lengths_ref.shape[1]):
        doc_end = doc_end + lengths_ref[0, k]
        token_doc = token_doc + jnp.where(position >= doc_end, 1.0, 0.0)
    for copy in tag_copies:
        copy.wait()
    tag_row = jnp.concatenate([arrived_tags[s, 0:1, :] for s in range(n)], axis=1)
    live = tag_row == token_doc
    present = jnp.max(jnp.where(live, 1.0, 0.0), axis=1, keepdims=True) > 0.0
    scaling = HD ** (-0.5)
    for h in range(heads):
        for i in range(1, n):
            out_copy(h, i).wait()
        hk = pl.ds(h * HD, HD)
        q, g = q_ref[:, hk], g_ref[:, hk]
        scores = contract(q, arrived[h, 0], 1, 1) * scaling
        highest = jnp.max(jnp.where(live, scores, masked_value), axis=1, keepdims=True)
        highest = jnp.where(present, highest, 0.0)
        raised = jnp.exp(jnp.where(live, scores - highest, masked_value))
        totals = jnp.maximum(jnp.sum(raised, axis=1, keepdims=True), 1.0)
        attention = raised / totals
        rounded = attention.astype(bf16)
        grad_raw = contract(g, arrived[h, 1], 1, 1)
        deltas = jnp.sum(attention * grad_raw, axis=1, keepdims=True)
        score_grad = (attention * (grad_raw - deltas) * scaling).astype(bf16)
        grads[h, 0] = contract(score_grad, q, 0, 0).astype(bf16)
        grads[h, 1] = contract(rounded, g, 0, 0).astype(bf16)
        tsend[h, pl.ds(0, tokens), :] = rounded
        tsend[h, pl.ds(tokens, tokens), :] = score_grad
        if h == 0:
            each_piece(hand_over, late, False)

    def back_copy(i):
        to = slot_at(i)
        return remote(
            grads.at[:, :, rows_of(to), :],
            ret.at[:, :, rows_of(me), :],
            back_send.at[i],
            back_recv.at[i],
            dp=to,
        )

    for i in range(1, n):
        back_copy(i).start()
    ret[:, :, rows_of(me), :] = grads[:, :, rows_of(me), :]
    for h in range(heads):
        hk = pl.ds(h * HD, HD)
        ctx_ref[:, hk] = jnp.dot(
            tsend[h, pl.ds(0, tokens), :], arrived[h, 1], preferred_element_type=jnp.float32
        ).astype(bf16)
        qg_ref[:, hk] = jnp.dot(
            tsend[h, pl.ds(tokens, tokens), :], arrived[h, 0], preferred_element_type=jnp.float32
        ).astype(bf16)

    def g_copy(r):
        return remote(own.at[r], gend.at[r], g_send.at[r], g_recv.at[r], mp=mate)

    half = blk // 2

    def half_rows(k):
        return pl.ds(pl.multiple_of(k * half, half), half)

    def first_g_copy(k):
        sem = k * blocks
        return remote(
            own.at[0, half_rows(k)], gend.at[0, half_rows(k)], g_send.at[sem], g_recv.at[sem], mp=mate
        )


    def first_mid_copy(way, k):
        sem = k * blocks
        return remote(
            msend.at[way, 0, half_rows(k)],
            mrecv.at[way, 0, half_rows(k)],
            mid_send.at[way, sem],
            mid_recv.at[way, sem],
            mp=across,
        )

    def mid_copy(way, r):
        return remote(
            msend.at[way, r], mrecv.at[way, r], mid_send.at[way, r], mid_recv.at[way, r], mp=across
        )

    def end_copy(r):
        return remote(mrecv.at[0, r], mrecv.at[0, r], end_send.at[r], end_recv.at[r], mp=mate)

    def prod_copy(r):
        return remote(msend.at[0, r], pend.at[r], prod_send.at[r], prod_recv.at[r], mp=mate)

    def pair_copy(i):
        return remote(tsend.at[i], trecv.at[i], pair_send.at[i], pair_recv.at[i], dp=at_c)

    def hop_copy(way, i, src):
        to = at_x if (way == 0) == (i < 2) else at_y
        return remote(src, hops.at[way, i], hop_send.at[way, i], hop_recv.at[way, i], dp=to)

    for i, part, h in pieces:

        @pl.when(jnp.logical_and(is_inner, theirs[i] // 4 != side))
        def _():
            core_copy(i, part, h, theirs[i]).wait_recv()

    def collect(r):
        back_copy_at = slot_at(r + 1)
        remote(
            ret.at[:, :, rows_of(back_copy_at), :],
            ret.at[:, :, rows_of(back_copy_at), :],
            back_send.at[r + 1],
            back_recv.at[r + 1],
            dp=at_c,
        ).wait_recv()
        later = hole <= r
        for h in range(heads):
            for part in range(2):
                own[r, :, pl.ds(part * width + h * HD, HD)] = jnp.where(
                    later,
                    ret[h, part, rows_of(back_copy_at), :],
                    ret[h, part, rows_of(slot_at(r)), :],
                )

        @pl.when(jnp.logical_and(is_end, r > 0))
        def _():
            g_copy(r).start()

    def own_weights(d, j):
        return wts[2 * d + j]

    def end_weights(d, j):
        return wend[(d % 2) * 2 + j]

    def shard_of(i, parity):
        flip_x, flip_y = 1 - i // 2, 1 - i % 2
        px = x + flip_x - 2 * x * flip_x
        py = y + flip_y - 2 * y * flip_y
        return place(py, px, parity)

    def term(shard, part, h):
        columns = pl.ds(pl.multiple_of(shard * depth, depth), depth)
        return contract(enc[:, columns], ret[h, part, pl.ds(0, rows), :], 0, 0).astype(bf16)

    def each_slab(todo):
        for part in range(2):
            for h in range(heads):
                todo(part, h, pl.ds(part * width + h * HD, HD))

    def half_cols(j):
        return pl.ds(pl.multiple_of(j * width, width), width)

    total = acc.at[0]

    def wait_mid(way, r):
        @pl.when(r == 0)
        def _():
            first_mid_copy(way, 0).wait_recv()
            first_mid_copy(way, 1).wait_recv()

        @pl.when(r > 0)
        def _():
            mid_copy(way, r).wait_recv()

    def own_product(r, dest):
        @pl.loop(0, 2)
        def _(j):
            total[:, half_cols(j)] = contract(own[r], own_weights(dest, j), 1, 1)

    def forward(r):
        own_product(r, end)
        wait_mid(0, r)
        mrecv[0, r] = (total[...] + mrecv[0, r].astype(jnp.float32)).astype(bf16)
        end_copy(r).start()

    collect(0)

    @pl.when(is_end)
    def _():
        first_g_copy(0).start()
        first_g_copy(1).start()

    @pl.when(is_inner)
    def _():
        crossing = ((0, far_end), (1, across))
        for way, dest in crossing:

            @pl.loop(0, 2)
            def _(j):
                acc[1 + way, :, half_cols(j)] = contract(own[0], own_weights(dest, j), 1, 1)

        @pl.loop(0, 2)
        def _(k):
            first_g_copy(k).wait_recv()
            for way, dest in crossing:

                @pl.loop(0, 2)
                def _(j):
                    summed = acc[1 + way, half_rows(k), half_cols(j)]
                    summed += contract(gend[0, half_rows(k)], end_weights(dest, j), 1, 1)
                    msend[way, 0, half_rows(k), half_cols(j)] = summed.astype(bf16)

                first_mid_copy(way, k).start()

    def send_across(way, r):
        dest = across if way else far_end

        @pl.loop(0, 2)
        def _(j):
            summed = contract(own[r], own_weights(dest, j), 1, 1)
            summed += contract(gend[r], end_weights(dest, j), 1, 1)
            msend[way, r, :, half_cols(j)] = summed.astype(bf16)

        mid_copy(way, r).start()

    @pl.loop(1, blocks)
    def _(r):
        @pl.when(r < 3)
        def _():
            collect(r)

        @pl.when(is_inner)
        def _():
            g_copy(r).wait_recv()
            send_across(0, r)

            @pl.when(r > 1)
            def _():
                send_across(1, r - 1)
                forward(r - 2)

        @pl.when(r == 2)
        def _():
            @pl.loop(3, blocks)
            def _(later):
                collect(later)

            for b in range(blocks):
                block = own[turns[b]]
                for h in range(heads):
                    for part in range(2):
                        first = part * width + h * HD
                        ret[h, part, pl.ds(b * blk, blk), :] = block[:, first : first + HD]

            @pl.loop(0, 4)
            def _(i):
                shard = shard_of(i, 1 - core)

                def fill(part, h, cols):
                    tsend[i, :, cols] = term(shard, part, h)

                each_slab(fill)
                pair_copy(i).start()

        @pl.when(r == 3)
        def _():
            @pl.loop(0, 4)
            def _(i):
                shard = shard_of(i, core)
                pair_copy(i).wait_recv()

                def fill(part, h, cols):
                    summed = term(shard, part, h).astype(jnp.float32)
                    summed += trecv[i, :, cols].astype(jnp.float32)
                    trecv[i, :, cols] = summed.astype(bf16)

                each_slab(fill)

                @pl.when(i == 1)
                def _():
                    hop_copy(0, 1, trecv.at[0, :, part_cols(0)]).start()
                    hop_copy(0, 0, trecv.at[1, :, part_cols(0)]).start()
                    hop_copy(1, 1, trecv.at[0, :, part_cols(1)]).start()

                @pl.when(i == 2)
                def _():
                    hop_copy(1, 0, trecv.at[2, :, part_cols(1)]).start()

    @pl.when(is_end)
    def _():
        @pl.loop(0, blocks)
        def _(r):
            @pl.loop(0, 2)
            def _(j):
                msend[0, r, :, half_cols(j)] = contract(own[r], own_weights(mate, j), 1, 1).astype(bf16)

            prod_copy(r).start()

    @pl.when(is_inner)
    def _():
        send_across(1, blocks - 1)

    for way in range(2):
        hop_copy(way, 1, hops.at[way, 1]).wait_recv()
        summed = trecv[2 - way, :, part_cols(way)].astype(jnp.float32)
        summed += hops[way, 1].astype(jnp.float32)
        passed[way] = summed.astype(bf16)
        hop_copy(way, 2, passed.at[way]).start()

    def finish(r):
        own_product(r, z)
        prod_copy(r).wait_recv()
        total[...] += pend[r].astype(jnp.float32)
        wait_mid(1, r)
        eg_ref[r] = (total[...] + mrecv[1, r].astype(jnp.float32)).astype(bf16)

    @pl.loop(0, blocks)
    def _(r):
        @pl.when(is_inner)
        def _():
            @pl.when(jnp.logical_and(r + 3 >= blocks, r + 1 < blocks))
            def _():
                forward(r + 1)

            finish(r)

        @pl.when(is_end)
        def _():
            own_product(r, z)
            end_copy(r).wait_recv()
            eg_ref[r] = (total[...] + mrecv[0, r].astype(jnp.float32)).astype(bf16)

        @pl.when(r == blocks - 2)
        def _():
            for way, out in ((0, kwg_ref), (1, vwg_ref)):
                hop_copy(way, 0, hops.at[way, 0]).wait_recv()
                hop_copy(way, 2, hops.at[way, 2]).wait_recv()
                summed = trecv[3, :, part_cols(way)].astype(jnp.float32)
                summed += hops[way, 0].astype(jnp.float32) + hops[way, 2].astype(jnp.float32)
                out[...] = summed.astype(bf16)

    for copy in started:
        copy.wait_send()
    each_piece(lambda *piece: lift_copy(*piece).wait_send(), pieces, True)
    each_piece(lambda *piece: core_copy(*piece).wait_send(), pieces, False)

    @pl.loop(0, blocks)
    def _(r):
        @pl.when(is_end)
        def _():
            prod_copy(r).wait_send()

            @pl.when(r > 0)
            def _():
                g_copy(r).wait_send()

        @pl.when(is_inner)
        def _():
            end_copy(r).wait_send()

            @pl.when(r > 0)
            def _():
                mid_copy(0, r).wait_send()
                mid_copy(1, r).wait_send()

    @pl.loop(0, 2)
    def _(k):
        @pl.when(is_end)
        def _():
            first_g_copy(k).wait_send()

        @pl.when(is_inner)
        def _():
            first_mid_copy(0, k).wait_send()
            first_mid_copy(1, k).wait_send()

    for i in range(1, n):
        back_copy(i).wait_send()
    for i in range(4):
        pair_copy(i).wait_send()
    for way in range(2):
        for i in range(3):
            hop_copy(way, i, hops.at[way, i]).wait_send()


def deliver_kernel(n, bins_ref, *refs):
    turns = block_turns(lax.axis_index("dp"), n, bins_ref)[1]
    count = (len(refs) - 1) // 2
    ins, outs, store_sem = refs[:count], refs[count : 2 * count], refs[2 * count]
    stores = []
    for k in range(count):
        pieces = [(ins[k], outs[k])]
        if len(ins[k].shape) == 3:
            blocks, size, _ = ins[k].shape
            pieces = [
                (ins[k].at[turns[b]], outs[k].at[pl.ds(b * size, size), :]) for b in range(blocks)
            ]
        for source, target in pieces:
            stores.append(pltpu.make_async_copy(source, target, store_sem.at[len(stores)]))
            stores[-1].start()
    for store in stores:
        store.wait()


def deliver(n, bins, arrays):
    hbm = pl.BlockSpec(memory_space=pl.ANY)
    vmem = pl.BlockSpec(memory_space=pltpu.VMEM)
    copies = sum(a.shape[0] if a.ndim == 3 else 1 for a in arrays)
    return pl.pallas_call(
        functools.partial(deliver_kernel, n),
        out_shape=tuple(
            jax.ShapeDtypeStruct((a.size // a.shape[-1], a.shape[-1]), a.dtype) for a in arrays
        ),
        in_specs=[pl.BlockSpec(memory_space=pltpu.SMEM)] + [vmem] * len(arrays),
        out_specs=(hbm,) * len(arrays),
        scratch_shapes=[pltpu.SemaphoreType.DMA((copies,))],
        compiler_params=pltpu.CompilerParams(vmem_limit_bytes=8 * 1024 * 1024),
    )(bins, *arrays)


def per_device_cube(
    queries,
    context_grad,
    encoder_rows,
    key_weight,
    value_weight,
    document_lengths,
    block_bin,
    block_document,
):
    n, count = lax.axis_size("dp"), lax.axis_size("mp")
    rows, model = encoder_rows.shape
    depth, width = key_weight.shape
    heads = width // HD
    tokens = queries.shape[0]
    blocks = rows // BLK
    chips = n // 2
    vmem = pl.BlockSpec(memory_space=pltpu.VMEM)
    smem = pl.BlockSpec(memory_space=pltpu.SMEM)
    hbm = pl.BlockSpec(memory_space=pl.ANY)
    bf16 = jnp.bfloat16
    dma = pltpu.SemaphoreType.DMA
    shape = pltpu.VMEM
    pairs = []
    for extent in [(heads, 14), (16,), (16,), (n,), (heads, n), (n,), (n,), (2, n), (blocks,), (blocks,), (chips,), (2, 3)]:
        pairs += [dma(extent), dma(extent)]
    outs = pl.pallas_call(
        functools.partial(step_kernel, n, count),
        out_shape=(
            shape((tokens, width), bf16),
            shape((tokens, width), bf16),
            shape((blocks, BLK, model // count), bf16),
            shape((depth, width), bf16),
            shape((depth, width), bf16),
        ),
        in_specs=[vmem, vmem, hbm, vmem, vmem, smem, smem, smem],
        out_specs=(vmem,) * 5,
        scratch_shapes=[
            pltpu.VMEM((rows, model), bf16),
            pltpu.VMEM((n, depth, 2 * width), bf16),
            pltpu.VMEM((n // 2, depth, 2 * width), bf16),
            pltpu.VMEM((blocks, BLK, 2 * width), jnp.float32),
            pltpu.VMEM((heads, 2, n * BLK, HD), bf16),
            pltpu.VMEM((n, 8, BLK), jnp.float32),
            pltpu.VMEM((n, 8, BLK), jnp.float32),
            pltpu.VMEM((heads, 2, n * BLK, HD), bf16),
            pltpu.VMEM((heads, 2, n * BLK, HD), bf16),
            pltpu.VMEM((blocks, BLK, 2 * width), bf16),
            pltpu.VMEM((blocks, BLK, 2 * width), bf16),
            pltpu.VMEM((blocks, BLK, 2 * width), bf16),
            pltpu.VMEM((2, blocks, BLK, 2 * width), bf16),
            pltpu.VMEM((2, blocks, BLK, 2 * width), bf16),
            pltpu.VMEM((chips, depth, 2 * width), bf16),
            pltpu.VMEM((chips, depth, 2 * width), bf16),
            pltpu.VMEM((2, 3, depth, width), bf16),
            pltpu.VMEM((2, depth, width), bf16),
            dma((3,)),
            *pairs,
        ],
        compiler_params=pltpu.CompilerParams(
            collective_id=0, has_side_effects=True, vmem_limit_bytes=60 * 1024 * 1024
        ),
    )(
        queries,
        context_grad,
        encoder_rows,
        key_weight,
        value_weight,
        document_lengths,
        block_bin,
        block_document,
    )
    return deliver(n, block_bin, outs)


def solution(mesh):
    in_specs = (
        P("dp", "mp"),
        P("dp", "mp"),
        P("dp", None),
        P("dp", "mp"),
        P("dp", "mp"),
        P("dp", None),
        P("dp"),
        P("dp"),
    )
    out_specs = (P("dp", "mp"), P("dp", "mp"), P("dp", "mp"), P("dp", "mp"), P("dp", "mp"))
    cube = mesh.shape["dp"] == 2 * 2 * 2 and mesh.shape["mp"] == 2 * 2
    return jax.shard_map(
        per_device_cube if cube else per_device, mesh=mesh, in_specs=in_specs, out_specs=out_specs, check_vma=False
    )
```

```python
import functools

import jax
import jax.numpy as jnp
from jax import lax
from jax.experimental import pallas as pl
from jax.experimental.pallas import tpu as pltpu
from jax.sharding import PartitionSpec as P

HD = 256
BLK = 128


masked_value = -1e30


def attend_weights(scores, live_mask):
    present = jnp.any(live_mask, axis=1)[None, :, None]
    blocked = jnp.where(live_mask[None], scores, masked_value)
    highest = jnp.max(blocked, axis=2, keepdims=True)
    highest = jnp.where(present, highest, 0.0)
    raised = jnp.exp(jnp.where(live_mask[None], scores - highest, masked_value))
    totals = jnp.maximum(jnp.sum(raised, axis=2, keepdims=True), 1.0)
    return raised / totals


def token_documents(lengths, token_count):
    doc_ends = jnp.cumsum(lengths)
    positions = jnp.arange(token_count, dtype=jnp.int32)
    return jnp.sum((doc_ends[None, :] <= positions[:, None]).astype(jnp.int32), axis=1)


def per_device(
    queries,
    context_grad,
    encoder_rows,
    key_weight,
    value_weight,
    document_lengths,
    block_bin,
    block_document,
):
    bin_count = lax.axis_size("dp")
    full_key, full_value = (
        lax.all_gather(key_weight, "dp", axis=0, tiled=True),
        lax.all_gather(value_weight, "dp", axis=0, tiled=True),
    )
    head_width = full_key.shape[1]
    head_count = head_width // HD
    block_rows = BLK
    blocks_here = block_bin.shape[0]
    both_weights = jnp.concatenate([full_key, full_value], axis=1)
    projected = jnp.dot(encoder_rows, both_weights, preferred_element_type=jnp.float32).astype(
        jnp.bfloat16
    )
    route_table = (block_bin[:, None] == jnp.arange(bin_count, dtype=jnp.int32)[None, :]).astype(
        jnp.bfloat16
    )
    flat_blocks = projected.reshape(blocks_here, block_rows * 2 * head_width)
    outbound = lax.dot_general(
        route_table, flat_blocks, (((0,), (0,)), ((), ())), preferred_element_type=jnp.float32
    )
    outbound = outbound.astype(jnp.bfloat16).reshape(bin_count, block_rows, 2 * head_width)
    slot_docs = (
        lax.dot_general(
            route_table.astype(jnp.float32),
            (block_document + 1).astype(jnp.float32),
            (((0,), (0,)), ((), ())),
        )
        - 1.0
    )
    tag_rows = jnp.broadcast_to(slot_docs[:, None], (bin_count, block_rows)).astype(jnp.bfloat16)
    arrived, arrived_tags = (
        lax.all_to_all(outbound, "dp", split_axis=0, concat_axis=0, tiled=True),
        lax.all_to_all(tag_rows, "dp", split_axis=0, concat_axis=0, tiled=True),
    )
    key_slots = arrived[:, :, :head_width].reshape(bin_count * block_rows, head_count, HD)
    value_slots = arrived[:, :, head_width:].reshape(bin_count * block_rows, head_count, HD)
    token_count = queries.shape[0]
    token_docs = token_documents(document_lengths[0], token_count).astype(jnp.float32)
    live_mask = arrived_tags.reshape(-1).astype(jnp.float32)[None, :] == token_docs[:, None]
    query_heads = queries.reshape(token_count, head_count, HD)
    grad_heads = context_grad.reshape(token_count, head_count, HD)
    scaling = HD ** (-0.5)
    scores = (
        jnp.einsum("thd,shd->hts", query_heads, key_slots, preferred_element_type=jnp.float32)
        * scaling
    )
    attention = attend_weights(scores, live_mask)
    rounded = attention.astype(jnp.bfloat16)
    context = jnp.einsum(
        "hts,shd->thd", rounded, value_slots, preferred_element_type=jnp.float32
    ).astype(jnp.bfloat16)
    grad_raw = jnp.einsum(
        "thd,shd->hts", grad_heads, value_slots, preferred_element_type=jnp.float32
    )
    deltas = jnp.sum(attention * grad_raw, axis=2, keepdims=True)
    score_grad = (attention * (grad_raw - deltas) * scaling).astype(jnp.bfloat16)
    query_grad = jnp.einsum(
        "hts,shd->thd", score_grad, key_slots, preferred_element_type=jnp.float32
    ).astype(jnp.bfloat16)
    key_grad = jnp.einsum(
        "hts,thd->shd", score_grad, query_heads, preferred_element_type=jnp.float32
    ).astype(jnp.bfloat16)
    value_grad = jnp.einsum(
        "hts,thd->shd", rounded, grad_heads, preferred_element_type=jnp.float32
    ).astype(jnp.bfloat16)
    slot_grads = jnp.concatenate(
        [
            key_grad.reshape(bin_count, block_rows, head_width),
            value_grad.reshape(bin_count, block_rows, head_width),
        ],
        axis=2,
    )
    returned = lax.all_to_all(slot_grads, "dp", split_axis=0, concat_axis=0, tiled=True)
    own_grads = jnp.dot(
        route_table,
        returned.reshape(bin_count, block_rows * 2 * head_width),
        preferred_element_type=jnp.float32,
    )
    own_grads = own_grads.astype(jnp.bfloat16).reshape(encoder_rows.shape[0], 2 * head_width)
    weight_terms = lax.dot_general(
        encoder_rows, own_grads, (((0,), (0,)), ((), ())), preferred_element_type=jnp.float32
    )
    weight_sums = lax.psum_scatter(
        weight_terms.astype(jnp.bfloat16), "dp", scatter_dimension=0, tiled=True
    ).astype(jnp.float32)
    key_weight_grad = weight_sums[:, :head_width].astype(jnp.bfloat16)
    value_weight_grad = weight_sums[:, head_width:].astype(jnp.bfloat16)
    row_terms = lax.dot_general(
        own_grads, both_weights, (((1,), (1,)), ((), ())), preferred_element_type=jnp.float32
    )
    encoder_grad = lax.psum_scatter(
        row_terms.astype(jnp.bfloat16), "mp", scatter_dimension=1, tiled=True
    )
    return (
        context.reshape(token_count, head_width),
        query_grad.reshape(token_count, head_width),
        encoder_grad,
        key_weight_grad,
        value_weight_grad,
    )


MESH = pl.DeviceIdType.MESH


def contract(a, b, dim_a, dim_b):
    return lax.dot_general(
        a, b, (((dim_a,), (dim_b,)), ((), ())), preferred_element_type=jnp.float32
    )


def bin_at(me, i):
    def flip(bit, turned):
        return bit + turned - 2 * bit * turned

    core, x, y = me % 2, (me // 2) % 2, me // 4
    return (flip(y, i // 4) * 2 + flip(x, (i // 2) % 2)) * 2 + flip(core, i % 2)


def find(value, options):
    index = jnp.int32(0)
    for k, option in enumerate(options):
        index = jnp.where(option == value, k, index)
    return index


def block_turns(me, n, bins_ref):
    bins = [bins_ref[b] for b in range(bins_ref.shape[0])]
    order = [bin_at(me, i) for i in range(n)]
    hole = find(n * (n - 1) // 2 - sum(bins), order)
    places = [find(b, order) for b in bins]
    return hole, [jnp.where(p > hole, p - 1, p) for p in places]


def step_kernel(
    n,
    count,
    q_hbm,
    g_hbm,
    enc_hbm,
    kw_hbm,
    vw_hbm,
    lengths_ref,
    bins_ref,
    docs_ref,
    ctx_ref,
    qg_ref,
    eg_ref,
    kwg_ref,
    vwg_ref,
    q_ref,
    g_ref,
    enc,
    wts,
    wend,
    acc,
    arrived,
    tags,
    arrived_tags,
    grads,
    ret,
    own,
    gend,
    pend,
    msend,
    mrecv,
    tsend,
    trecv,
    hops,
    passed,
    local_sem,
    gather_send,
    gather_recv,
    lift_send,
    lift_recv,
    core_send,
    core_recv,
    tag_send,
    tag_recv,
    out_send,
    out_recv,
    back_send,
    back_recv,
    g_send,
    g_recv,
    mid_send,
    mid_recv,
    end_send,
    end_recv,
    prod_send,
    prod_recv,
    pair_send,
    pair_recv,
    hop_send,
    hop_recv,
):
    bf16 = jnp.bfloat16
    me, z = lax.axis_index("dp"), lax.axis_index("mp")
    core = me % 2
    x = (me // 2) % 2
    y = me // 4

    def place(py, px, pc):
        return (py * 2 + px) * 2 + pc

    at_x, at_y = place(y, 1 - x, core), place(1 - y, x, core)
    at_c, at_d = place(y, x, 1 - core), place(1 - y, 1 - x, core)
    c_x, c_y = place(y, 1 - x, 1 - core), place(1 - y, x, 1 - core)
    c_d = place(1 - y, 1 - x, 1 - core)
    depth, width = kw_hbm.shape
    rows = enc.shape[0]
    blocks = rows // BLK
    blk = BLK
    heads = width // HD
    tokens = q_ref.shape[0]
    last = count - 1
    end = (z // 2) * last
    far_end = last - end
    side = z // 2
    is_end = z == end
    is_inner = z != end
    mate = z + 1 - 2 * (z % 2)
    across = last - z

    def remote(src, dst, send, recv, **device):
        return pltpu.make_async_remote_copy(
            src_ref=src,
            dst_ref=dst,
            send_sem=send,
            recv_sem=recv,
            device_id=device,
            device_id_type=MESH,
        )

    def load(k, source, target):
        return pltpu.make_async_copy(source, target, local_sem.at[k])

    own_k = load(1, kw_hbm, wts.at[me, :, pl.ds(0, width)])
    own_v = load(2, vw_hbm, wts.at[me, :, pl.ds(width, width)])
    load_enc = load(0, enc_hbm, enc)
    load_q, load_g = load(3, q_hbm, q_ref), load(4, g_hbm, g_ref)
    for copy in (own_k, own_v, load_enc, load_q, load_g):
        copy.start()
    barrier = pltpu.get_barrier_semaphore()
    for d in range(1, n):
        pl.semaphore_signal(
            barrier, inc=1, device_id={"dp": (me + d) % n}, device_id_type=MESH
        )
    pl.semaphore_signal(barrier, inc=1, device_id={"mp": mate}, device_id_type=MESH)

    @pl.when(is_inner)
    def _():
        pl.semaphore_signal(barrier, inc=1, device_id={"mp": across}, device_id_type=MESH)


    for d in range(n):
        to = (me + d) % n
        doc = jnp.int32(-1)
        for b in range(blocks):
            doc = jnp.where(bins_ref[b] == to, docs_ref[b], doc)
        tags[to] = jnp.full(tags.shape[1:], doc.astype(jnp.float32), jnp.float32)
    pl.semaphore_wait(barrier, n + (z + 1) // 2 % 2)

    def part_cols(part):
        return pl.ds(part * width, width)

    def head_cols(part, h):
        return pl.ds(pl.multiple_of(part * width + h * HD, HD), HD)

    def land(src, part, h):
        return wts.at[src, :, head_cols(part, h)]

    started = []

    def ship(h, ident, ref, src, part, to):
        copy = remote(
            ref, land(src, part, h), gather_send.at[h, ident], gather_recv.at[h, ident], dp=to
        )
        copy.start()
        started.append(copy)

    def landed(h, ident, src, part):
        remote(
            land(src, part, h),
            land(src, part, h),
            gather_send.at[h, ident],
            gather_recv.at[h, ident],
            dp=at_c,
        ).wait_recv()

    def lifted(src, part, h):
        return wend.at[src % 4, :, head_cols(part, h)]

    ours, theirs = (me, at_x, at_y, at_d), (at_c, c_x, c_y, c_d)
    early = [(0, 0, 0), (0, 1, 0), (0, 0, 1), (0, 1, 1), (1, 0, 0), (2, 1, 0), (1, 1, 0), (2, 0, 0)]
    early += [(3, 0, 0), (3, 1, 0), (1, 0, 1), (2, 1, 1), (1, 1, 1), (2, 0, 1)]
    late = [(3, 0, 1), (3, 1, 1)]
    pieces = early + late

    def lift(i, part, h):
        src = ours[i]
        ident = 4 * i + 2 * part + h

        @pl.when(jnp.logical_and(is_end, src // 4 != side))
        def _():
            remote(
                land(src, part, h),
                lifted(src, part, h),
                lift_send.at[ident],
                lift_recv.at[ident],
                mp=mate,
            ).start()

    def each_piece(todo, listed, of_end):
        for i, part, h in listed:

            @pl.when(jnp.logical_and(is_end if of_end else is_inner, ours[i] // 4 != side))
            def _():
                todo(i, part, h, ours[i])

    def lift_copy(i, part, h, src):
        ident = 4 * i + 2 * part + h
        ref = lifted(src, part, h)
        return remote(ref, ref, lift_send.at[ident], lift_recv.at[ident], mp=mate)

    def core_copy(i, part, h, src):
        ident = 4 * i + 2 * part + h
        ref = lifted(src, part, h)
        return remote(ref, ref, core_send.at[ident], core_recv.at[ident], dp=at_c)

    def hand_over(i, part, h, src):
        lift_copy(i, part, h, src).wait_recv()
        core_copy(i, part, h, src).start()

    def ship_own(h):
        kw, vw = land(me, 0, h), land(me, 1, h)
        ship(h, 0, kw, me, 0, at_x)
        ship(h, 3, vw, me, 1, at_y)
        ship(h, 1, vw, me, 1, at_x)
        ship(h, 2, kw, me, 0, at_y)
        ship(h, 6, kw, me, 0, at_c)
        ship(h, 7, vw, me, 1, at_c)
        lift(0, 0, h)
        lift(0, 1, h)

    own_k.wait()
    own_v.wait()
    ship_own(0)
    tag_copies = []
    for d in range(1, n):
        to = (me + d) % n
        copy = remote(
            tags.at[to], arrived_tags.at[me], tag_send.at[d], tag_recv.at[d], dp=to
        )
        copy.start()
        tag_copies.append(copy)
    arrived_tags[me] = tags[me]
    load_enc.wait()

    def multiply(h, first_src, second_src, swap=0, fresh=False):
        @pl.loop(0, 2)
        def _(t):
            src = first_src + t * (second_src - first_src)
            columns = pl.ds(pl.multiple_of(src * depth, depth), depth)
            cols = head_cols(t + swap - 2 * t * swap, h)
            product = jnp.dot(
                enc[:, columns], wts[src, :, cols], preferred_element_type=jnp.float32
            ).reshape(blocks, blk, HD)
            if fresh:
                acc[:, :, cols] = product
            else:
                acc[:, :, cols] += product

    def gather(h, when_passed):
        multiply(h, me, me, fresh=True)
        landed(h, 6, at_c, 0)
        landed(h, 7, at_c, 1)
        multiply(h, at_c, at_c)
        landed(h, 0, at_x, 0)
        ship(h, 4, land(at_x, 0, h), at_x, 0, at_y)
        ship(h, 8, land(at_x, 0, h), at_x, 0, at_c)
        lift(1, 0, h)
        landed(h, 3, at_y, 1)
        ship(h, 5, land(at_y, 1, h), at_y, 1, at_x)
        ship(h, 11, land(at_y, 1, h), at_y, 1, at_c)
        lift(2, 1, h)
        when_passed()
        multiply(h, at_x, at_y)
        landed(h, 8, c_x, 0)
        landed(h, 11, c_y, 1)
        multiply(h, c_x, c_y)
        landed(h, 1, at_x, 1)
        ship(h, 9, land(at_x, 1, h), at_x, 1, at_c)
        lift(1, 1, h)
        landed(h, 2, at_y, 0)
        ship(h, 10, land(at_y, 0, h), at_y, 0, at_c)
        lift(2, 0, h)
        multiply(h, at_y, at_x)
        landed(h, 9, c_x, 1)
        landed(h, 10, c_y, 0)
        multiply(h, c_y, c_x)
        landed(h, 4, at_d, 0)
        ship(h, 12, land(at_d, 0, h), at_d, 0, at_c)
        lift(3, 0, h)
        landed(h, 5, at_d, 1)
        ship(h, 13, land(at_d, 1, h), at_d, 1, at_c)
        lift(3, 1, h)
        multiply(h, at_d, at_d)
        landed(h, 12, c_d, 0)
        landed(h, 13, c_d, 1)
        multiply(h, c_d, c_d)

    def rows_of(slot):
        return pl.ds(pl.multiple_of(slot * blk, blk), blk)

    def slot_at(i):
        return bin_at(me, i)

    bins = [bins_ref[b] for b in range(blocks)]
    hole, turns = block_turns(me, n, bins_ref)

    def out_copy(h, i):
        to = slot_at(i)
        return remote(
            grads.at[h, :, rows_of(to), :],
            arrived.at[h, :, rows_of(me), :],
            out_send.at[h, i],
            out_recv.at[h, i],
            dp=to,
        )

    def send_slots(h):
        for i in [*range(1, n), 0]:
            to = slot_at(i)
            index = find(to, bins)
            for part in range(2):
                cols = pl.ds(part * width + h * HD, HD)
                picked = acc[index, :, cols].astype(bf16)
                if i == 0:
                    arrived[h, part, rows_of(me), :] = picked
                else:
                    grads[h, part, rows_of(to), :] = picked
            if i > 0:
                out_copy(h, i).start()

    gather(0, lambda: ship_own(1))
    gather(1, lambda: send_slots(0))
    send_slots(1)
    each_piece(hand_over, early, False)
    position = lax.broadcasted_iota(jnp.int32, (tokens, 1), 0)
    token_doc = jnp.zeros(position.shape, jnp.float32)
    doc_end = jnp.int32(0)
    for k in range(lengths_ref.shape[1]):
        doc_end = doc_end + lengths_ref[0, k]
        token_doc = token_doc + jnp.where(position >= doc_end, 1.0, 0.0)
    for copy in tag_copies:
        copy.wait()
    load_q.wait()
    load_g.wait()
    tag_row = jnp.concatenate([arrived_tags[s, 0:1, :] for s in range(n)], axis=1)
    live = tag_row == token_doc
    present = jnp.max(jnp.where(live, 1.0, 0.0), axis=1, keepdims=True) > 0.0
    scaling = HD ** (-0.5)
    for h in range(heads):
        for i in range(1, n):
            out_copy(h, i).wait()
        hk = pl.ds(h * HD, HD)
        q, g = q_ref[:, hk], g_ref[:, hk]
        scores = contract(q, arrived[h, 0], 1, 1) * scaling
        highest = jnp.max(jnp.where(live, scores, masked_value), axis=1, keepdims=True)
        highest = jnp.where(present, highest, 0.0)
        raised = jnp.exp(jnp.where(live, scores - highest, masked_value))
        totals = jnp.maximum(jnp.sum(raised, axis=1, keepdims=True), 1.0)
        attention = raised / totals
        rounded = attention.astype(bf16)
        grad_raw = contract(g, arrived[h, 1], 1, 1)
        deltas = jnp.sum(attention * grad_raw, axis=1, keepdims=True)
        score_grad = (attention * (grad_raw - deltas) * scaling).astype(bf16)
        grads[h, 0] = contract(score_grad, q, 0, 0).astype(bf16)
        grads[h, 1] = contract(rounded, g, 0, 0).astype(bf16)
        tsend[h, pl.ds(0, tokens), :] = rounded
        tsend[h, pl.ds(tokens, tokens), :] = score_grad
        if h == 0:
            each_piece(hand_over, late, False)

    def back_copy(i):
        to = slot_at(i)
        return remote(
            grads.at[:, :, rows_of(to), :],
            ret.at[:, :, rows_of(me), :],
            back_send.at[i],
            back_recv.at[i],
            dp=to,
        )

    for i in range(1, n):
        back_copy(i).start()
    ret[:, :, rows_of(me), :] = grads[:, :, rows_of(me), :]
    def g_copy(r):
        return remote(own.at[r], gend.at[r], g_send.at[r], g_recv.at[r], mp=mate)

    pieces_first = 4
    piece = blk // pieces_first

    def piece_rows(k):
        return pl.ds(pl.multiple_of(k * piece, piece), piece)

    def first_g_copy(k):
        sem = blocks + k
        return remote(
            own.at[0, piece_rows(k)], gend.at[0, piece_rows(k)], g_send.at[sem], g_recv.at[sem], mp=mate
        )


    def first_mid_copy(way, k):
        sem = blocks + k
        return remote(
            msend.at[way, 0, piece_rows(k)],
            mrecv.at[way, 0, piece_rows(k)],
            mid_send.at[way, sem],
            mid_recv.at[way, sem],
            mp=across,
        )

    def mid_copy(way, r):
        return remote(
            msend.at[way, r], mrecv.at[way, r], mid_send.at[way, r], mid_recv.at[way, r], mp=across
        )

    def end_copy(r):
        return remote(mrecv.at[0, r], mrecv.at[0, r], end_send.at[r], end_recv.at[r], mp=mate)

    def prod_copy(r):
        return remote(msend.at[0, r], pend.at[r], prod_send.at[r], prod_recv.at[r], mp=mate)

    def pair_copy(i):
        return remote(tsend.at[i], trecv.at[i], pair_send.at[i], pair_recv.at[i], dp=at_c)

    def hop_copy(way, i, src):
        to = at_x if (way == 0) == (i < 2) else at_y
        return remote(src, hops.at[way, i], hop_send.at[way, i], hop_recv.at[way, i], dp=to)

    for i, part, h in pieces:

        @pl.when(jnp.logical_and(is_inner, theirs[i] // 4 != side))
        def _():
            core_copy(i, part, h, theirs[i]).wait_recv()

    def collect(r):
        back_copy_at = slot_at(r + 1)
        remote(
            ret.at[:, :, rows_of(back_copy_at), :],
            ret.at[:, :, rows_of(back_copy_at), :],
            back_send.at[r + 1],
            back_recv.at[r + 1],
            dp=at_c,
        ).wait_recv()
        later = hole <= r
        for h in range(heads):
            for part in range(2):
                own[r, :, pl.ds(part * width + h * HD, HD)] = jnp.where(
                    later,
                    ret[h, part, rows_of(back_copy_at), :],
                    ret[h, part, rows_of(slot_at(r)), :],
                )

        @pl.when(jnp.logical_and(is_end, r > 0))
        def _():
            g_copy(r).start()

    def own_weights(d, j):
        return wts[2 * d + j]

    def end_weights(d, j):
        return wend[(d % 2) * 2 + j]

    def shard_of(i, parity):
        flip_x, flip_y = 1 - i // 2, 1 - i % 2
        px = x + flip_x - 2 * x * flip_x
        py = y + flip_y - 2 * y * flip_y
        return place(py, px, parity)

    def term(shard, part, h):
        columns = pl.ds(pl.multiple_of(shard * depth, depth), depth)
        return contract(enc[:, columns], ret[h, part, pl.ds(0, rows), :], 0, 0).astype(bf16)

    def each_slab(todo):
        for part in range(2):
            for h in range(heads):
                todo(part, h, pl.ds(part * width + h * HD, HD))

    def half_cols(j):
        return pl.ds(pl.multiple_of(j * width, width), width)

    total = acc.at[0]

    def wait_mid(way, r):
        @pl.when(r == 0)
        def _():
            @pl.loop(0, pieces_first)
            def _(k):
                first_mid_copy(way, k).wait_recv()

        @pl.when(r > 0)
        def _():
            mid_copy(way, r).wait_recv()

    def own_product(r, dest):
        @pl.loop(0, 2)
        def _(j):
            total[:, half_cols(j)] = contract(own[r], own_weights(dest, j), 1, 1)

    def forward(r):
        own_product(r, end)
        wait_mid(0, r)
        mrecv[0, r] = (total[...] + mrecv[0, r].astype(jnp.float32)).astype(bf16)
        end_copy(r).start()

    collect(0)

    @pl.when(is_end)
    def _():
        @pl.loop(0, pieces_first)
        def _(k):
            first_g_copy(k).start()

    for h in range(heads):
        hk = pl.ds(h * HD, HD)
        ctx_ref[:, hk] = jnp.dot(
            tsend[h, pl.ds(0, tokens), :], arrived[h, 1], preferred_element_type=jnp.float32
        ).astype(bf16)
        qg_ref[:, hk] = jnp.dot(
            tsend[h, pl.ds(tokens, tokens), :], arrived[h, 0], preferred_element_type=jnp.float32
        ).astype(bf16)

    @pl.when(is_inner)
    def _():
        crossing = ((0, far_end), (1, across))
        for way, dest in crossing:

            @pl.loop(0, 2)
            def _(j):
                acc[1 + way, :, half_cols(j)] = contract(own[0], own_weights(dest, j), 1, 1)

        @pl.loop(0, pieces_first)
        def _(k):
            first_g_copy(k).wait_recv()
            for way, dest in crossing:

                @pl.loop(0, 2)
                def _(j):
                    summed = acc[1 + way, piece_rows(k), half_cols(j)]
                    summed += contract(gend[0, piece_rows(k)], end_weights(dest, j), 1, 1)
                    msend[way, 0, piece_rows(k), half_cols(j)] = summed.astype(bf16)

                first_mid_copy(way, k).start()

    def send_across(way, r):
        dest = across if way else far_end

        @pl.loop(0, 2)
        def _(j):
            summed = contract(own[r], own_weights(dest, j), 1, 1)
            summed += contract(gend[r], end_weights(dest, j), 1, 1)
            msend[way, r, :, half_cols(j)] = summed.astype(bf16)

        mid_copy(way, r).start()

    @pl.loop(1, blocks)
    def _(r):
        @pl.when(r < 3)
        def _():
            collect(r)

        @pl.when(is_inner)
        def _():
            g_copy(r).wait_recv()
            send_across(0, r)

            @pl.when(r > 1)
            def _():
                send_across(1, r - 1)
                forward(r - 2)

        @pl.when(r == 2)
        def _():
            @pl.loop(3, blocks)
            def _(later):
                collect(later)

            for b in range(blocks):
                block = own[turns[b]]
                for h in range(heads):
                    for part in range(2):
                        first = part * width + h * HD
                        ret[h, part, pl.ds(b * blk, blk), :] = block[:, first : first + HD]

            @pl.loop(0, 4)
            def _(i):
                shard = shard_of(i, 1 - core)

                def fill(part, h, cols):
                    tsend[i, :, cols] = term(shard, part, h)

                each_slab(fill)
                pair_copy(i).start()

        @pl.when(r == 3)
        def _():
            @pl.loop(0, 4)
            def _(i):
                shard = shard_of(i, core)
                pair_copy(i).wait_recv()

                def fill(part, h, cols):
                    summed = term(shard, part, h).astype(jnp.float32)
                    summed += trecv[i, :, cols].astype(jnp.float32)
                    trecv[i, :, cols] = summed.astype(bf16)

                each_slab(fill)

                @pl.when(i == 1)
                def _():
                    hop_copy(0, 1, trecv.at[0, :, part_cols(0)]).start()
                    hop_copy(0, 0, trecv.at[1, :, part_cols(0)]).start()
                    hop_copy(1, 1, trecv.at[0, :, part_cols(1)]).start()

                @pl.when(i == 2)
                def _():
                    hop_copy(1, 0, trecv.at[2, :, part_cols(1)]).start()

    @pl.when(is_end)
    def _():
        @pl.loop(0, blocks)
        def _(r):
            @pl.loop(0, 2)
            def _(j):
                msend[0, r, :, half_cols(j)] = contract(own[r], own_weights(mate, j), 1, 1).astype(bf16)

            prod_copy(r).start()

    @pl.when(is_inner)
    def _():
        send_across(1, blocks - 1)

    for way in range(2):
        hop_copy(way, 1, hops.at[way, 1]).wait_recv()
        summed = trecv[2 - way, :, part_cols(way)].astype(jnp.float32)
        summed += hops[way, 1].astype(jnp.float32)
        passed[way] = summed.astype(bf16)
        hop_copy(way, 2, passed.at[way]).start()

    def finish(r):
        own_product(r, z)
        prod_copy(r).wait_recv()
        total[...] += pend[r].astype(jnp.float32)
        wait_mid(1, r)
        eg_ref[r] = (total[...] + mrecv[1, r].astype(jnp.float32)).astype(bf16)

    @pl.loop(0, blocks)
    def _(r):
        @pl.when(is_inner)
        def _():
            @pl.when(jnp.logical_and(r + 3 >= blocks, r + 1 < blocks))
            def _():
                forward(r + 1)

            finish(r)

        @pl.when(is_end)
        def _():
            own_product(r, z)
            end_copy(r).wait_recv()
            eg_ref[r] = (total[...] + mrecv[0, r].astype(jnp.float32)).astype(bf16)

        @pl.when(r == blocks - 2)
        def _():
            for way, out in ((0, kwg_ref), (1, vwg_ref)):
                hop_copy(way, 0, hops.at[way, 0]).wait_recv()
                hop_copy(way, 2, hops.at[way, 2]).wait_recv()
                summed = trecv[3, :, part_cols(way)].astype(jnp.float32)
                summed += hops[way, 0].astype(jnp.float32) + hops[way, 2].astype(jnp.float32)
                out[...] = summed.astype(bf16)

    for copy in started:
        copy.wait_send()
    each_piece(lambda *piece: lift_copy(*piece).wait_send(), pieces, True)
    each_piece(lambda *piece: core_copy(*piece).wait_send(), pieces, False)

    @pl.loop(0, blocks)
    def _(r):
        @pl.when(is_end)
        def _():
            prod_copy(r).wait_send()

            @pl.when(r > 0)
            def _():
                g_copy(r).wait_send()

        @pl.when(is_inner)
        def _():
            end_copy(r).wait_send()

            @pl.when(r > 0)
            def _():
                mid_copy(0, r).wait_send()
                mid_copy(1, r).wait_send()

    @pl.loop(0, pieces_first)
    def _(k):
        @pl.when(is_end)
        def _():
            first_g_copy(k).wait_send()

        @pl.when(is_inner)
        def _():
            first_mid_copy(0, k).wait_send()
            first_mid_copy(1, k).wait_send()

    for i in range(1, n):
        back_copy(i).wait_send()
    for i in range(4):
        pair_copy(i).wait_send()
    for way in range(2):
        for i in range(3):
            hop_copy(way, i, hops.at[way, i]).wait_send()


def deliver_kernel(n, bins_ref, *refs):
    turns = block_turns(lax.axis_index("dp"), n, bins_ref)[1]
    count = (len(refs) - 1) // 2
    ins, outs, store_sem = refs[:count], refs[count : 2 * count], refs[2 * count]
    stores = []
    for k in range(count):
        pieces = [(ins[k], outs[k])]
        if len(ins[k].shape) == 3:
            blocks, size, _ = ins[k].shape
            pieces = [
                (ins[k].at[turns[b]], outs[k].at[pl.ds(b * size, size), :]) for b in range(blocks)
            ]
        for source, target in pieces:
            stores.append(pltpu.make_async_copy(source, target, store_sem.at[len(stores)]))
            stores[-1].start()
    for store in stores:
        store.wait()


def deliver(n, bins, arrays):
    hbm = pl.BlockSpec(memory_space=pl.ANY)
    vmem = pl.BlockSpec(memory_space=pltpu.VMEM)
    copies = sum(a.shape[0] if a.ndim == 3 else 1 for a in arrays)
    return pl.pallas_call(
        functools.partial(deliver_kernel, n),
        out_shape=tuple(
            jax.ShapeDtypeStruct((a.size // a.shape[-1], a.shape[-1]), a.dtype) for a in arrays
        ),
        in_specs=[pl.BlockSpec(memory_space=pltpu.SMEM)] + [vmem] * len(arrays),
        out_specs=(hbm,) * len(arrays),
        scratch_shapes=[pltpu.SemaphoreType.DMA((copies,))],
        compiler_params=pltpu.CompilerParams(vmem_limit_bytes=8 * 1024 * 1024),
    )(bins, *arrays)


def per_device_cube(
    queries,
    context_grad,
    encoder_rows,
    key_weight,
    value_weight,
    document_lengths,
    block_bin,
    block_document,
):
    n, count = lax.axis_size("dp"), lax.axis_size("mp")
    rows, model = encoder_rows.shape
    depth, width = key_weight.shape
    heads = width // HD
    tokens = queries.shape[0]
    blocks = rows // BLK
    chips = n // 2
    vmem = pl.BlockSpec(memory_space=pltpu.VMEM)
    smem = pl.BlockSpec(memory_space=pltpu.SMEM)
    hbm = pl.BlockSpec(memory_space=pl.ANY)
    bf16 = jnp.bfloat16
    dma = pltpu.SemaphoreType.DMA
    shape = pltpu.VMEM
    pairs = []
    for extent in [(heads, 14), (16,), (16,), (n,), (heads, n), (n,), (blocks + 4,), (2, blocks + 4), (blocks,), (blocks,), (chips,), (2, 3)]:
        pairs += [dma(extent), dma(extent)]
    outs = pl.pallas_call(
        functools.partial(step_kernel, n, count),
        out_shape=(
            shape((tokens, width), bf16),
            shape((tokens, width), bf16),
            shape((blocks, BLK, model // count), bf16),
            shape((depth, width), bf16),
            shape((depth, width), bf16),
        ),
        in_specs=[hbm, hbm, hbm, hbm, hbm, smem, smem, smem],
        out_specs=(vmem,) * 5,
        scratch_shapes=[
            pltpu.VMEM((tokens, width), bf16),
            pltpu.VMEM((tokens, width), bf16),
            pltpu.VMEM((rows, model), bf16),
            pltpu.VMEM((n, depth, 2 * width), bf16),
            pltpu.VMEM((n // 2, depth, 2 * width), bf16),
            pltpu.VMEM((blocks, BLK, 2 * width), jnp.float32),
            pltpu.VMEM((heads, 2, n * BLK, HD), bf16),
            pltpu.VMEM((n, 8, BLK), jnp.float32),
            pltpu.VMEM((n, 8, BLK), jnp.float32),
            pltpu.VMEM((heads, 2, n * BLK, HD), bf16),
            pltpu.VMEM((heads, 2, n * BLK, HD), bf16),
            pltpu.VMEM((blocks, BLK, 2 * width), bf16),
            pltpu.VMEM((blocks, BLK, 2 * width), bf16),
            pltpu.VMEM((blocks, BLK, 2 * width), bf16),
            pltpu.VMEM((2, blocks, BLK, 2 * width), bf16),
            pltpu.VMEM((2, blocks, BLK, 2 * width), bf16),
            pltpu.VMEM((chips, depth, 2 * width), bf16),
            pltpu.VMEM((chips, depth, 2 * width), bf16),
            pltpu.VMEM((2, 3, depth, width), bf16),
            pltpu.VMEM((2, depth, width), bf16),
            dma((5,)),
            *pairs,
        ],
        compiler_params=pltpu.CompilerParams(
            collective_id=0, has_side_effects=True, vmem_limit_bytes=60 * 1024 * 1024
        ),
    )(
        queries,
        context_grad,
        encoder_rows,
        key_weight,
        value_weight,
        document_lengths,
        block_bin,
        block_document,
    )
    return deliver(n, block_bin, outs)


def solution(mesh):
    in_specs = (
        P("dp", "mp"),
        P("dp", "mp"),
        P("dp", None),
        P("dp", "mp"),
        P("dp", "mp"),
        P("dp", None),
        P("dp"),
        P("dp"),
    )
    out_specs = (P("dp", "mp"), P("dp", "mp"), P("dp", "mp"), P("dp", "mp"), P("dp", "mp"))
    cube = mesh.shape["dp"] == 2 * 2 * 2 and mesh.shape["mp"] == 2 * 2
    return jax.shard_map(
        per_device_cube if cube else per_device, mesh=mesh, in_specs=in_specs, out_specs=out_specs, check_vma=False
    )
```

```python
import functools

import jax
import jax.numpy as jnp
from jax import lax
from jax.experimental import pallas as pl
from jax.experimental.pallas import tpu as pltpu
from jax.sharding import PartitionSpec as P

HD = 256
BLK = 128


masked_value = -1e30


def attend_weights(scores, live_mask):
    present = jnp.any(live_mask, axis=1)[None, :, None]
    blocked = jnp.where(live_mask[None], scores, masked_value)
    highest = jnp.max(blocked, axis=2, keepdims=True)
    highest = jnp.where(present, highest, 0.0)
    raised = jnp.exp(jnp.where(live_mask[None], scores - highest, masked_value))
    totals = jnp.maximum(jnp.sum(raised, axis=2, keepdims=True), 1.0)
    return raised / totals


def token_documents(lengths, token_count):
    doc_ends = jnp.cumsum(lengths)
    positions = jnp.arange(token_count, dtype=jnp.int32)
    return jnp.sum((doc_ends[None, :] <= positions[:, None]).astype(jnp.int32), axis=1)


def per_device(
    queries,
    context_grad,
    encoder_rows,
    key_weight,
    value_weight,
    document_lengths,
    block_bin,
    block_document,
):
    bin_count = lax.axis_size("dp")
    full_key, full_value = (
        lax.all_gather(key_weight, "dp", axis=0, tiled=True),
        lax.all_gather(value_weight, "dp", axis=0, tiled=True),
    )
    head_width = full_key.shape[1]
    head_count = head_width // HD
    block_rows = BLK
    blocks_here = block_bin.shape[0]
    both_weights = jnp.concatenate([full_key, full_value], axis=1)
    projected = jnp.dot(encoder_rows, both_weights, preferred_element_type=jnp.float32).astype(
        jnp.bfloat16
    )
    route_table = (block_bin[:, None] == jnp.arange(bin_count, dtype=jnp.int32)[None, :]).astype(
        jnp.bfloat16
    )
    flat_blocks = projected.reshape(blocks_here, block_rows * 2 * head_width)
    outbound = lax.dot_general(
        route_table, flat_blocks, (((0,), (0,)), ((), ())), preferred_element_type=jnp.float32
    )
    outbound = outbound.astype(jnp.bfloat16).reshape(bin_count, block_rows, 2 * head_width)
    slot_docs = (
        lax.dot_general(
            route_table.astype(jnp.float32),
            (block_document + 1).astype(jnp.float32),
            (((0,), (0,)), ((), ())),
        )
        - 1.0
    )
    tag_rows = jnp.broadcast_to(slot_docs[:, None], (bin_count, block_rows)).astype(jnp.bfloat16)
    arrived, arrived_tags = (
        lax.all_to_all(outbound, "dp", split_axis=0, concat_axis=0, tiled=True),
        lax.all_to_all(tag_rows, "dp", split_axis=0, concat_axis=0, tiled=True),
    )
    key_slots = arrived[:, :, :head_width].reshape(bin_count * block_rows, head_count, HD)
    value_slots = arrived[:, :, head_width:].reshape(bin_count * block_rows, head_count, HD)
    token_count = queries.shape[0]
    token_docs = token_documents(document_lengths[0], token_count).astype(jnp.float32)
    live_mask = arrived_tags.reshape(-1).astype(jnp.float32)[None, :] == token_docs[:, None]
    query_heads = queries.reshape(token_count, head_count, HD)
    grad_heads = context_grad.reshape(token_count, head_count, HD)
    scaling = HD ** (-0.5)
    scores = (
        jnp.einsum("thd,shd->hts", query_heads, key_slots, preferred_element_type=jnp.float32)
        * scaling
    )
    attention = attend_weights(scores, live_mask)
    rounded = attention.astype(jnp.bfloat16)
    context = jnp.einsum(
        "hts,shd->thd", rounded, value_slots, preferred_element_type=jnp.float32
    ).astype(jnp.bfloat16)
    grad_raw = jnp.einsum(
        "thd,shd->hts", grad_heads, value_slots, preferred_element_type=jnp.float32
    )
    deltas = jnp.sum(attention * grad_raw, axis=2, keepdims=True)
    score_grad = (attention * (grad_raw - deltas) * scaling).astype(jnp.bfloat16)
    query_grad = jnp.einsum(
        "hts,shd->thd", score_grad, key_slots, preferred_element_type=jnp.float32
    ).astype(jnp.bfloat16)
    key_grad = jnp.einsum(
        "hts,thd->shd", score_grad, query_heads, preferred_element_type=jnp.float32
    ).astype(jnp.bfloat16)
    value_grad = jnp.einsum(
        "hts,thd->shd", rounded, grad_heads, preferred_element_type=jnp.float32
    ).astype(jnp.bfloat16)
    slot_grads = jnp.concatenate(
        [
            key_grad.reshape(bin_count, block_rows, head_width),
            value_grad.reshape(bin_count, block_rows, head_width),
        ],
        axis=2,
    )
    returned = lax.all_to_all(slot_grads, "dp", split_axis=0, concat_axis=0, tiled=True)
    own_grads = jnp.dot(
        route_table,
        returned.reshape(bin_count, block_rows * 2 * head_width),
        preferred_element_type=jnp.float32,
    )
    own_grads = own_grads.astype(jnp.bfloat16).reshape(encoder_rows.shape[0], 2 * head_width)
    weight_terms = lax.dot_general(
        encoder_rows, own_grads, (((0,), (0,)), ((), ())), preferred_element_type=jnp.float32
    )
    weight_sums = lax.psum_scatter(
        weight_terms.astype(jnp.bfloat16), "dp", scatter_dimension=0, tiled=True
    ).astype(jnp.float32)
    key_weight_grad = weight_sums[:, :head_width].astype(jnp.bfloat16)
    value_weight_grad = weight_sums[:, head_width:].astype(jnp.bfloat16)
    row_terms = lax.dot_general(
        own_grads, both_weights, (((1,), (1,)), ((), ())), preferred_element_type=jnp.float32
    )
    encoder_grad = lax.psum_scatter(
        row_terms.astype(jnp.bfloat16), "mp", scatter_dimension=1, tiled=True
    )
    return (
        context.reshape(token_count, head_width),
        query_grad.reshape(token_count, head_width),
        encoder_grad,
        key_weight_grad,
        value_weight_grad,
    )


MESH = pl.DeviceIdType.MESH


def contract(a, b, dim_a, dim_b):
    return lax.dot_general(
        a, b, (((dim_a,), (dim_b,)), ((), ())), preferred_element_type=jnp.float32
    )


def bin_at(me, i):
    def flip(bit, turned):
        return bit + turned - 2 * bit * turned

    core, x, y = me % 2, (me // 2) % 2, me // 4
    return (flip(y, i // 4) * 2 + flip(x, (i // 2) % 2)) * 2 + flip(core, i % 2)


def find(value, options):
    index = jnp.int32(0)
    for k, option in enumerate(options):
        index = jnp.where(option == value, k, index)
    return index


def block_turns(me, n, bins_ref):
    bins = [bins_ref[b] for b in range(bins_ref.shape[0])]
    order = [bin_at(me, i) for i in range(n)]
    hole = find(n * (n - 1) // 2 - sum(bins), order)
    places = [find(b, order) for b in bins]
    return hole, [jnp.where(p > hole, p - 1, p) for p in places]


def step_kernel(
    n,
    count,
    q_hbm,
    g_hbm,
    enc_hbm,
    kw_hbm,
    vw_hbm,
    lengths_ref,
    bins_ref,
    docs_ref,
    ctx_ref,
    qg_ref,
    eg_ref,
    kwg_ref,
    vwg_ref,
    q_ref,
    g_ref,
    enc,
    wts,
    wend,
    acc,
    arrived,
    tags,
    arrived_tags,
    grads,
    ret,
    own,
    gend,
    pend,
    msend,
    mrecv,
    tsend,
    trecv,
    hops,
    passed,
    local_sem,
    gather_send,
    gather_recv,
    lift_send,
    lift_recv,
    core_send,
    core_recv,
    tag_send,
    tag_recv,
    out_send,
    out_recv,
    back_send,
    back_recv,
    g_send,
    g_recv,
    mid_send,
    mid_recv,
    end_send,
    end_recv,
    prod_send,
    prod_recv,
    pair_send,
    pair_recv,
    hop_send,
    hop_recv,
):
    bf16 = jnp.bfloat16
    me, z = lax.axis_index("dp"), lax.axis_index("mp")
    core = me % 2
    x = (me // 2) % 2
    y = me // 4

    def place(py, px, pc):
        return (py * 2 + px) * 2 + pc

    at_x, at_y = place(y, 1 - x, core), place(1 - y, x, core)
    at_c, at_d = place(y, x, 1 - core), place(1 - y, 1 - x, core)
    c_x, c_y = place(y, 1 - x, 1 - core), place(1 - y, x, 1 - core)
    c_d = place(1 - y, 1 - x, 1 - core)
    depth, width = kw_hbm.shape
    rows = enc.shape[0]
    blocks = rows // BLK
    blk = BLK
    heads = width // HD
    tokens = q_ref.shape[0]
    last = count - 1
    end = (z // 2) * last
    far_end = last - end
    side = z // 2
    is_end = z == end
    is_inner = z != end
    mate = z + 1 - 2 * (z % 2)
    across = last - z

    def remote(src, dst, send, recv, **device):
        return pltpu.make_async_remote_copy(
            src_ref=src,
            dst_ref=dst,
            send_sem=send,
            recv_sem=recv,
            device_id=device,
            device_id_type=MESH,
        )

    def load(k, source, target):
        return pltpu.make_async_copy(source, target, local_sem.at[k])

    own_k = load(1, kw_hbm, wts.at[me, :, pl.ds(0, width)])
    own_v = load(2, vw_hbm, wts.at[me, :, pl.ds(width, width)])
    load_enc = load(0, enc_hbm, enc)
    load_q, load_g = load(3, q_hbm, q_ref), load(4, g_hbm, g_ref)
    for copy in (own_k, own_v, load_enc, load_q, load_g):
        copy.start()
    barrier = pltpu.get_barrier_semaphore()
    for d in range(1, n):
        pl.semaphore_signal(
            barrier, inc=1, device_id={"dp": (me + d) % n}, device_id_type=MESH
        )
    pl.semaphore_signal(barrier, inc=1, device_id={"mp": mate}, device_id_type=MESH)

    @pl.when(is_inner)
    def _():
        pl.semaphore_signal(barrier, inc=1, device_id={"mp": across}, device_id_type=MESH)


    for d in range(n):
        to = (me + d) % n
        doc = jnp.int32(-1)
        for b in range(blocks):
            doc = jnp.where(bins_ref[b] == to, docs_ref[b], doc)
        tags[to] = jnp.full(tags.shape[1:], doc.astype(jnp.float32), jnp.float32)
    pl.semaphore_wait(barrier, n + (z + 1) // 2 % 2)

    def part_cols(part):
        return pl.ds(part * width, width)

    def head_cols(part, h):
        return pl.ds(pl.multiple_of(part * width + h * HD, HD), HD)

    def land(src, part, h):
        return wts.at[src, :, head_cols(part, h)]

    started = []

    def ship(h, ident, ref, src, part, to):
        copy = remote(
            ref, land(src, part, h), gather_send.at[h, ident], gather_recv.at[h, ident], dp=to
        )
        copy.start()
        started.append(copy)

    def landed(h, ident, src, part):
        remote(
            land(src, part, h),
            land(src, part, h),
            gather_send.at[h, ident],
            gather_recv.at[h, ident],
            dp=at_c,
        ).wait_recv()

    def lifted(src, part, h):
        return wend.at[src % 4, :, head_cols(part, h)]

    ours, theirs = (me, at_x, at_y, at_d), (at_c, c_x, c_y, c_d)
    early = [(0, 0, 0), (0, 1, 0), (0, 0, 1), (0, 1, 1), (1, 0, 0), (2, 1, 0), (1, 1, 0), (2, 0, 0)]
    early += [(3, 0, 0), (3, 1, 0), (1, 0, 1), (2, 1, 1), (1, 1, 1), (2, 0, 1)]
    late = [(3, 0, 1), (3, 1, 1)]
    pieces = early + late

    def lift(i, part, h):
        src = ours[i]
        ident = 4 * i + 2 * part + h

        @pl.when(jnp.logical_and(is_end, src // 4 != side))
        def _():
            remote(
                land(src, part, h),
                lifted(src, part, h),
                lift_send.at[ident],
                lift_recv.at[ident],
                mp=mate,
            ).start()

    def each_piece(todo, listed, of_end):
        for i, part, h in listed:

            @pl.when(jnp.logical_and(is_end if of_end else is_inner, ours[i] // 4 != side))
            def _():
                todo(i, part, h, ours[i])

    def lift_copy(i, part, h, src):
        ident = 4 * i + 2 * part + h
        ref = lifted(src, part, h)
        return remote(ref, ref, lift_send.at[ident], lift_recv.at[ident], mp=mate)

    def core_copy(i, part, h, src):
        ident = 4 * i + 2 * part + h
        ref = lifted(src, part, h)
        return remote(ref, ref, core_send.at[ident], core_recv.at[ident], dp=at_c)

    def hand_over(i, part, h, src):
        lift_copy(i, part, h, src).wait_recv()
        core_copy(i, part, h, src).start()

    def ship_own(h):
        kw, vw = land(me, 0, h), land(me, 1, h)
        ship(h, 0, kw, me, 0, at_x)
        ship(h, 3, vw, me, 1, at_y)
        ship(h, 1, vw, me, 1, at_x)
        ship(h, 2, kw, me, 0, at_y)
        ship(h, 6, kw, me, 0, at_c)
        ship(h, 7, vw, me, 1, at_c)
        lift(0, 0, h)
        lift(0, 1, h)

    own_k.wait()
    own_v.wait()
    ship_own(0)
    tag_copies = []
    for d in range(1, n):
        to = (me + d) % n
        copy = remote(
            tags.at[to], arrived_tags.at[me], tag_send.at[d], tag_recv.at[d], dp=to
        )
        copy.start()
        tag_copies.append(copy)
    arrived_tags[me] = tags[me]
    load_enc.wait()

    def multiply(h, first_src, second_src, swap=0, fresh=False):
        @pl.loop(0, 2)
        def _(t):
            src = first_src + t * (second_src - first_src)
            columns = pl.ds(pl.multiple_of(src * depth, depth), depth)
            cols = head_cols(t + swap - 2 * t * swap, h)
            product = jnp.dot(
                enc[:, columns], wts[src, :, cols], preferred_element_type=jnp.float32
            ).reshape(blocks, blk, HD)
            if fresh:
                acc[:, :, cols] = product
            else:
                acc[:, :, cols] += product

    def gather(h, when_passed):
        multiply(h, me, me, fresh=True)
        landed(h, 6, at_c, 0)
        landed(h, 7, at_c, 1)
        multiply(h, at_c, at_c)
        landed(h, 0, at_x, 0)
        ship(h, 4, land(at_x, 0, h), at_x, 0, at_y)
        ship(h, 8, land(at_x, 0, h), at_x, 0, at_c)
        lift(1, 0, h)
        landed(h, 3, at_y, 1)
        ship(h, 5, land(at_y, 1, h), at_y, 1, at_x)
        ship(h, 11, land(at_y, 1, h), at_y, 1, at_c)
        lift(2, 1, h)
        when_passed()
        multiply(h, at_x, at_y)
        landed(h, 8, c_x, 0)
        landed(h, 11, c_y, 1)
        multiply(h, c_x, c_y)
        landed(h, 1, at_x, 1)
        ship(h, 9, land(at_x, 1, h), at_x, 1, at_c)
        lift(1, 1, h)
        landed(h, 2, at_y, 0)
        ship(h, 10, land(at_y, 0, h), at_y, 0, at_c)
        lift(2, 0, h)
        multiply(h, at_y, at_x)
        landed(h, 9, c_x, 1)
        landed(h, 10, c_y, 0)
        multiply(h, c_y, c_x)
        landed(h, 4, at_d, 0)
        ship(h, 12, land(at_d, 0, h), at_d, 0, at_c)
        lift(3, 0, h)
        landed(h, 5, at_d, 1)
        ship(h, 13, land(at_d, 1, h), at_d, 1, at_c)
        lift(3, 1, h)
        multiply(h, at_d, at_d)
        landed(h, 12, c_d, 0)
        landed(h, 13, c_d, 1)
        multiply(h, c_d, c_d)

    def rows_of(slot):
        return pl.ds(pl.multiple_of(slot * blk, blk), blk)

    def slot_at(i):
        return bin_at(me, i)

    bins = [bins_ref[b] for b in range(blocks)]
    hole, turns = block_turns(me, n, bins_ref)

    def out_copy(h, part, i):
        to = slot_at(i)
        return remote(
            grads.at[h, part, rows_of(to), :],
            arrived.at[h, part, rows_of(me), :],
            out_send.at[h, part, i],
            out_recv.at[h, part, i],
            dp=to,
        )

    def send_slots(h):
        for part in range(2):
            cols = pl.ds(part * width + h * HD, HD)
            for i in [*range(1, n), 0]:
                to = slot_at(i)
                picked = acc[find(to, bins), :, cols].astype(bf16)
                if i == 0:
                    arrived[h, part, rows_of(me), :] = picked
                else:
                    grads[h, part, rows_of(to), :] = picked
                    out_copy(h, part, i).start()

    gather(0, lambda: ship_own(1))
    gather(1, lambda: send_slots(0))
    send_slots(1)
    each_piece(hand_over, early, False)
    position = lax.broadcasted_iota(jnp.int32, (tokens, 1), 0)
    token_doc = jnp.zeros(position.shape, jnp.float32)
    doc_end = jnp.int32(0)
    for k in range(lengths_ref.shape[1]):
        doc_end = doc_end + lengths_ref[0, k]
        token_doc = token_doc + jnp.where(position >= doc_end, 1.0, 0.0)
    for copy in tag_copies:
        copy.wait()
    load_q.wait()
    load_g.wait()
    tag_row = jnp.concatenate([arrived_tags[s, 0:1, :] for s in range(n)], axis=1)
    live = tag_row == token_doc
    present = jnp.max(jnp.where(live, 1.0, 0.0), axis=1, keepdims=True) > 0.0
    scaling = HD ** (-0.5)
    for h in range(heads):
        for i in range(1, n):
            out_copy(h, 0, i).wait()
        hk = pl.ds(h * HD, HD)
        q, g = q_ref[:, hk], g_ref[:, hk]
        scores = contract(q, arrived[h, 0], 1, 1) * scaling
        highest = jnp.max(jnp.where(live, scores, masked_value), axis=1, keepdims=True)
        highest = jnp.where(present, highest, 0.0)
        raised = jnp.exp(jnp.where(live, scores - highest, masked_value))
        totals = jnp.maximum(jnp.sum(raised, axis=1, keepdims=True), 1.0)
        attention = raised / totals
        rounded = attention.astype(bf16)
        for i in range(1, n):
            out_copy(h, 1, i).wait()
        grad_raw = contract(g, arrived[h, 1], 1, 1)
        deltas = jnp.sum(attention * grad_raw, axis=1, keepdims=True)
        score_grad = (attention * (grad_raw - deltas) * scaling).astype(bf16)
        grads[h, 0] = contract(score_grad, q, 0, 0).astype(bf16)
        grads[h, 1] = contract(rounded, g, 0, 0).astype(bf16)
        tsend[h, pl.ds(0, tokens), :] = rounded
        tsend[h, pl.ds(tokens, tokens), :] = score_grad
        if h == 0:
            each_piece(hand_over, late, False)

    def back_copy(i):
        to = slot_at(i)
        return remote(
            grads.at[:, :, rows_of(to), :],
            ret.at[:, :, rows_of(me), :],
            back_send.at[i],
            back_recv.at[i],
            dp=to,
        )

    for i in range(1, n):
        back_copy(i).start()
    ret[:, :, rows_of(me), :] = grads[:, :, rows_of(me), :]
    def g_copy(r):
        return remote(own.at[r], gend.at[r], g_send.at[r], g_recv.at[r], mp=mate)

    pieces_first = 4
    piece = blk // pieces_first

    def piece_rows(k):
        return pl.ds(pl.multiple_of(k * piece, piece), piece)

    def first_g_copy(k):
        sem = blocks + k
        return remote(
            own.at[0, piece_rows(k)], gend.at[0, piece_rows(k)], g_send.at[sem], g_recv.at[sem], mp=mate
        )


    def first_mid_copy(way, k):
        sem = blocks + k
        return remote(
            msend.at[way, 0, piece_rows(k)],
            mrecv.at[way, 0, piece_rows(k)],
            mid_send.at[way, sem],
            mid_recv.at[way, sem],
            mp=across,
        )

    def mid_copy(way, r):
        return remote(
            msend.at[way, r], mrecv.at[way, r], mid_send.at[way, r], mid_recv.at[way, r], mp=across
        )

    def end_copy(r):
        return remote(mrecv.at[0, r], mrecv.at[0, r], end_send.at[r], end_recv.at[r], mp=mate)

    def prod_copy(r):
        return remote(msend.at[0, r], pend.at[r], prod_send.at[r], prod_recv.at[r], mp=mate)

    def pair_copy(i):
        return remote(tsend.at[i], trecv.at[i], pair_send.at[i], pair_recv.at[i], dp=at_c)

    def hop_copy(way, i, src):
        to = at_x if (way == 0) == (i < 2) else at_y
        return remote(src, hops.at[way, i], hop_send.at[way, i], hop_recv.at[way, i], dp=to)

    for i, part, h in pieces:

        @pl.when(jnp.logical_and(is_inner, theirs[i] // 4 != side))
        def _():
            core_copy(i, part, h, theirs[i]).wait_recv()

    def collect(r):
        back_copy_at = slot_at(r + 1)
        remote(
            ret.at[:, :, rows_of(back_copy_at), :],
            ret.at[:, :, rows_of(back_copy_at), :],
            back_send.at[r + 1],
            back_recv.at[r + 1],
            dp=at_c,
        ).wait_recv()
        later = hole <= r
        for h in range(heads):
            for part in range(2):
                own[r, :, pl.ds(part * width + h * HD, HD)] = jnp.where(
                    later,
                    ret[h, part, rows_of(back_copy_at), :],
                    ret[h, part, rows_of(slot_at(r)), :],
                )

        @pl.when(jnp.logical_and(is_end, r > 0))
        def _():
            g_copy(r).start()

    def own_weights(d, j):
        return wts[2 * d + j]

    def end_weights(d, j):
        return wend[(d % 2) * 2 + j]

    def shard_of(i, parity):
        flip_x, flip_y = 1 - i // 2, 1 - i % 2
        px = x + flip_x - 2 * x * flip_x
        py = y + flip_y - 2 * y * flip_y
        return place(py, px, parity)

    def term(shard, part, h):
        columns = pl.ds(pl.multiple_of(shard * depth, depth), depth)
        return contract(enc[:, columns], ret[h, part, pl.ds(0, rows), :], 0, 0).astype(bf16)

    def each_slab(todo):
        for part in range(2):
            for h in range(heads):
                todo(part, h, pl.ds(part * width + h * HD, HD))

    def half_cols(j):
        return pl.ds(pl.multiple_of(j * width, width), width)

    total = acc.at[0]

    def wait_mid(way, r):
        @pl.when(r == 0)
        def _():
            @pl.loop(0, pieces_first)
            def _(k):
                first_mid_copy(way, k).wait_recv()

        @pl.when(r > 0)
        def _():
            mid_copy(way, r).wait_recv()

    def own_product(r, dest):
        @pl.loop(0, 2)
        def _(j):
            total[:, half_cols(j)] = contract(own[r], own_weights(dest, j), 1, 1)

    def forward(r):
        own_product(r, end)
        wait_mid(0, r)
        mrecv[0, r] = (total[...] + mrecv[0, r].astype(jnp.float32)).astype(bf16)
        end_copy(r).start()

    collect(0)

    @pl.when(is_end)
    def _():
        @pl.loop(0, pieces_first)
        def _(k):
            first_g_copy(k).start()

    for h in range(heads):
        hk = pl.ds(h * HD, HD)
        ctx_ref[:, hk] = jnp.dot(
            tsend[h, pl.ds(0, tokens), :], arrived[h, 1], preferred_element_type=jnp.float32
        ).astype(bf16)
        qg_ref[:, hk] = jnp.dot(
            tsend[h, pl.ds(tokens, tokens), :], arrived[h, 0], preferred_element_type=jnp.float32
        ).astype(bf16)

    @pl.when(is_inner)
    def _():
        crossing = ((0, far_end), (1, across))
        for way, dest in crossing:

            @pl.loop(0, 2)
            def _(j):
                acc[1 + way, :, half_cols(j)] = contract(own[0], own_weights(dest, j), 1, 1)

        @pl.loop(0, pieces_first)
        def _(k):
            first_g_copy(k).wait_recv()
            for way, dest in crossing:

                @pl.loop(0, 2)
                def _(j):
                    summed = acc[1 + way, piece_rows(k), half_cols(j)]
                    summed += contract(gend[0, piece_rows(k)], end_weights(dest, j), 1, 1)
                    msend[way, 0, piece_rows(k), half_cols(j)] = summed.astype(bf16)

                first_mid_copy(way, k).start()

    def send_across(way, r):
        dest = across if way else far_end

        @pl.loop(0, 2)
        def _(j):
            summed = contract(own[r], own_weights(dest, j), 1, 1)
            summed += contract(gend[r], end_weights(dest, j), 1, 1)
            msend[way, r, :, half_cols(j)] = summed.astype(bf16)

        mid_copy(way, r).start()

    @pl.loop(1, blocks)
    def _(r):
        @pl.when(r < 3)
        def _():
            collect(r)

        @pl.when(is_inner)
        def _():
            g_copy(r).wait_recv()
            send_across(0, r)

            @pl.when(r > 1)
            def _():
                send_across(1, r - 1)
                forward(r - 2)

        @pl.when(r == 2)
        def _():
            @pl.loop(3, blocks)
            def _(later):
                collect(later)

            for b in range(blocks):
                block = own[turns[b]]
                for h in range(heads):
                    for part in range(2):
                        first = part * width + h * HD
                        ret[h, part, pl.ds(b * blk, blk), :] = block[:, first : first + HD]

            @pl.loop(0, 4)
            def _(i):
                shard = shard_of(i, 1 - core)

                def fill(part, h, cols):
                    tsend[i, :, cols] = term(shard, part, h)

                each_slab(fill)
                pair_copy(i).start()

        @pl.when(r == 3)
        def _():
            @pl.loop(0, 4)
            def _(i):
                shard = shard_of(i, core)
                pair_copy(i).wait_recv()

                def fill(part, h, cols):
                    summed = term(shard, part, h).astype(jnp.float32)
                    summed += trecv[i, :, cols].astype(jnp.float32)
                    trecv[i, :, cols] = summed.astype(bf16)

                each_slab(fill)

                @pl.when(i == 1)
                def _():
                    hop_copy(0, 1, trecv.at[0, :, part_cols(0)]).start()
                    hop_copy(0, 0, trecv.at[1, :, part_cols(0)]).start()
                    hop_copy(1, 1, trecv.at[0, :, part_cols(1)]).start()

                @pl.when(i == 2)
                def _():
                    hop_copy(1, 0, trecv.at[2, :, part_cols(1)]).start()

    @pl.when(is_end)
    def _():
        @pl.loop(0, blocks)
        def _(r):
            @pl.loop(0, 2)
            def _(j):
                msend[0, r, :, half_cols(j)] = contract(own[r], own_weights(mate, j), 1, 1).astype(bf16)

            prod_copy(r).start()

    @pl.when(is_inner)
    def _():
        send_across(1, blocks - 1)

    for way in range(2):
        hop_copy(way, 1, hops.at[way, 1]).wait_recv()
        summed = trecv[2 - way, :, part_cols(way)].astype(jnp.float32)
        summed += hops[way, 1].astype(jnp.float32)
        passed[way] = summed.astype(bf16)
        hop_copy(way, 2, passed.at[way]).start()

    def finish(r):
        own_product(r, z)
        prod_copy(r).wait_recv()
        total[...] += pend[r].astype(jnp.float32)
        wait_mid(1, r)
        eg_ref[r] = (total[...] + mrecv[1, r].astype(jnp.float32)).astype(bf16)

    @pl.loop(0, blocks)
    def _(r):
        @pl.when(is_inner)
        def _():
            @pl.when(jnp.logical_and(r + 3 >= blocks, r + 1 < blocks))
            def _():
                forward(r + 1)

            finish(r)

        @pl.when(is_end)
        def _():
            own_product(r, z)
            end_copy(r).wait_recv()
            eg_ref[r] = (total[...] + mrecv[0, r].astype(jnp.float32)).astype(bf16)

        @pl.when(r == blocks - 2)
        def _():
            for way, out in ((0, kwg_ref), (1, vwg_ref)):
                hop_copy(way, 0, hops.at[way, 0]).wait_recv()
                hop_copy(way, 2, hops.at[way, 2]).wait_recv()
                summed = trecv[3, :, part_cols(way)].astype(jnp.float32)
                summed += hops[way, 0].astype(jnp.float32) + hops[way, 2].astype(jnp.float32)
                out[...] = summed.astype(bf16)

    for copy in started:
        copy.wait_send()
    each_piece(lambda *piece: lift_copy(*piece).wait_send(), pieces, True)
    each_piece(lambda *piece: core_copy(*piece).wait_send(), pieces, False)

    @pl.loop(0, blocks)
    def _(r):
        @pl.when(is_end)
        def _():
            prod_copy(r).wait_send()

            @pl.when(r > 0)
            def _():
                g_copy(r).wait_send()

        @pl.when(is_inner)
        def _():
            end_copy(r).wait_send()

            @pl.when(r > 0)
            def _():
                mid_copy(0, r).wait_send()
                mid_copy(1, r).wait_send()

    @pl.loop(0, pieces_first)
    def _(k):
        @pl.when(is_end)
        def _():
            first_g_copy(k).wait_send()

        @pl.when(is_inner)
        def _():
            first_mid_copy(0, k).wait_send()
            first_mid_copy(1, k).wait_send()

    for i in range(1, n):
        back_copy(i).wait_send()
    for i in range(4):
        pair_copy(i).wait_send()
    for way in range(2):
        for i in range(3):
            hop_copy(way, i, hops.at[way, i]).wait_send()


def deliver_kernel(n, bins_ref, *refs):
    turns = block_turns(lax.axis_index("dp"), n, bins_ref)[1]
    count = (len(refs) - 1) // 2
    ins, outs, store_sem = refs[:count], refs[count : 2 * count], refs[2 * count]
    stores = []
    for k in range(count):
        pieces = [(ins[k], outs[k])]
        if len(ins[k].shape) == 3:
            blocks, size, _ = ins[k].shape
            pieces = [
                (ins[k].at[turns[b]], outs[k].at[pl.ds(b * size, size), :]) for b in range(blocks)
            ]
        for source, target in pieces:
            stores.append(pltpu.make_async_copy(source, target, store_sem.at[len(stores)]))
            stores[-1].start()
    for store in stores:
        store.wait()


def deliver(n, bins, arrays):
    hbm = pl.BlockSpec(memory_space=pl.ANY)
    vmem = pl.BlockSpec(memory_space=pltpu.VMEM)
    copies = sum(a.shape[0] if a.ndim == 3 else 1 for a in arrays)
    return pl.pallas_call(
        functools.partial(deliver_kernel, n),
        out_shape=tuple(
            jax.ShapeDtypeStruct((a.size // a.shape[-1], a.shape[-1]), a.dtype) for a in arrays
        ),
        in_specs=[pl.BlockSpec(memory_space=pltpu.SMEM)] + [vmem] * len(arrays),
        out_specs=(hbm,) * len(arrays),
        scratch_shapes=[pltpu.SemaphoreType.DMA((copies,))],
        compiler_params=pltpu.CompilerParams(vmem_limit_bytes=8 * 1024 * 1024),
    )(bins, *arrays)


def per_device_cube(
    queries,
    context_grad,
    encoder_rows,
    key_weight,
    value_weight,
    document_lengths,
    block_bin,
    block_document,
):
    n, count = lax.axis_size("dp"), lax.axis_size("mp")
    rows, model = encoder_rows.shape
    depth, width = key_weight.shape
    heads = width // HD
    tokens = queries.shape[0]
    blocks = rows // BLK
    chips = n // 2
    vmem = pl.BlockSpec(memory_space=pltpu.VMEM)
    smem = pl.BlockSpec(memory_space=pltpu.SMEM)
    hbm = pl.BlockSpec(memory_space=pl.ANY)
    bf16 = jnp.bfloat16
    dma = pltpu.SemaphoreType.DMA
    shape = pltpu.VMEM
    pairs = []
    for extent in [(heads, 14), (16,), (16,), (n,), (heads, 2, n), (n,), (blocks + 4,), (2, blocks + 4), (blocks,), (blocks,), (chips,), (2, 3)]:
        pairs += [dma(extent), dma(extent)]
    outs = pl.pallas_call(
        functools.partial(step_kernel, n, count),
        out_shape=(
            shape((tokens, width), bf16),
            shape((tokens, width), bf16),
            shape((blocks, BLK, model // count), bf16),
            shape((depth, width), bf16),
            shape((depth, width), bf16),
        ),
        in_specs=[hbm, hbm, hbm, hbm, hbm, smem, smem, smem],
        out_specs=(vmem,) * 5,
        scratch_shapes=[
            pltpu.VMEM((tokens, width), bf16),
            pltpu.VMEM((tokens, width), bf16),
            pltpu.VMEM((rows, model), bf16),
            pltpu.VMEM((n, depth, 2 * width), bf16),
            pltpu.VMEM((n // 2, depth, 2 * width), bf16),
            pltpu.VMEM((blocks, BLK, 2 * width), jnp.float32),
            pltpu.VMEM((heads, 2, n * BLK, HD), bf16),
            pltpu.VMEM((n, 8, BLK), jnp.float32),
            pltpu.VMEM((n, 8, BLK), jnp.float32),
            pltpu.VMEM((heads, 2, n * BLK, HD), bf16),
            pltpu.VMEM((heads, 2, n * BLK, HD), bf16),
            pltpu.VMEM((blocks, BLK, 2 * width), bf16),
            pltpu.VMEM((blocks, BLK, 2 * width), bf16),
            pltpu.VMEM((blocks, BLK, 2 * width), bf16),
            pltpu.VMEM((2, blocks, BLK, 2 * width), bf16),
            pltpu.VMEM((2, blocks, BLK, 2 * width), bf16),
            pltpu.VMEM((chips, depth, 2 * width), bf16),
            pltpu.VMEM((chips, depth, 2 * width), bf16),
            pltpu.VMEM((2, 3, depth, width), bf16),
            pltpu.VMEM((2, depth, width), bf16),
            dma((5,)),
            *pairs,
        ],
        compiler_params=pltpu.CompilerParams(
            collective_id=0, has_side_effects=True, vmem_limit_bytes=60 * 1024 * 1024
        ),
    )(
        queries,
        context_grad,
        encoder_rows,
        key_weight,
        value_weight,
        document_lengths,
        block_bin,
        block_document,
    )
    return deliver(n, block_bin, outs)


def solution(mesh):
    in_specs = (
        P("dp", "mp"),
        P("dp", "mp"),
        P("dp", None),
        P("dp", "mp"),
        P("dp", "mp"),
        P("dp", None),
        P("dp"),
        P("dp"),
    )
    out_specs = (P("dp", "mp"), P("dp", "mp"), P("dp", "mp"), P("dp", "mp"), P("dp", "mp"))
    cube = mesh.shape["dp"] == 2 * 2 * 2 and mesh.shape["mp"] == 2 * 2
    return jax.shard_map(
        per_device_cube if cube else per_device, mesh=mesh, in_specs=in_specs, out_specs=out_specs, check_vma=False
    )
```
